128 devices in a mesh: cut: 8 (over x_lo, z), cross: 16 (over y, x_hi, core).
Axes of the slice: x: 4 (x_hi: 2, x_lo: 2; x = x_hi * 2 + x_lo), y: 4, z: 4, core: 2. Of those that a mesh axis runs over, the one named last changes fastest.
Arguments:
- warming_above_ambient: float32 [1024, 256, 128], P('cut', 'cross'), may hold values from 0 to 2
- fourier_stability_factor: float32 [1024, 256, 128], P('cut', 'cross'), may hold values from 0.02 to 0.1
- patch_locator: int32 [524288], P(('cut', 'cross')), may hold values from 0 to 524287
- photon_gain_wattage: float32 [524288], P(('cut', 'cross')), may hold values from 0.5 to 4
- on_skin_marker: int32 [524288], P(('cut', 'cross')), may hold values 0 or 1
- grain_placements: float32 [3, 524288], P(None, ('cut', 'cross')), may hold values from -1 to 1
- grain_motion_parts: float32 [3, 524288], P(None, ('cut', 'cross')), may hold values from -3 to 3
- tether_acted_grain: int32 [1048576], P(('cut', 'cross')), may hold values from 0 to 4095
- tether_other_grain: int32 [1048576], P(('cut', 'cross')), may hold values from 0 to 4607
- tether_relaxed_gap: float32 [1048576], P(('cut', 'cross')), may hold values from 0.5 to 1.5
- snapped_marker: int32 [1048576], P(('cut', 'cross')), may hold values 0 or 1
- exported_copies: int32 [32768], P(('cut', 'cross')), may hold values from 0 to 4095
Outputs:
- temperature_new: float32 [1024, 256, 128], P('cut', 'cross')
- positions_new: float32 [3, 524288], P(None, ('cut', 'cross'))
- velocities_new: float32 [3, 524288], P(None, ('cut', 'cross'))
The draws below stay inside these ranges and needn't reach their ends.
Inputs may be any that keep to these rules, and one draw needn't show every extreme that they name: `patch_locator`: values below 262144 name cells of the particle's own grid block along the cutting direction, the others cells of the next block.
All inputs are finite; a program needn't handle non-finite values. No bound on the sum of `on_skin_marker` or of `snapped_marker` on one device may be relied on, other than what follows from the above.
Results may differ from the reference program's by a relative error of at most 0.000071.
Values sent between devices are 32-bit elements; how exact they have to be, the bound alone decides.
A program may use at most 64 MiB of HBM per device.

```python
import math
import jax
import jax.numpy as jnp
from jax import lax

CX = 128
CY = 16
INWARD_EXTENT = 128
CAP = 256
GHOSTS = 256
BONDS = 8192
STEPS = 3
TANGENT_EXTENT = 1024
LATHE_AXIS_COUNT = 256
P_DEV = 4096
DOTS_OVERALL = 524288
GTOT = 32768
BTOT = 1048576
N_CUT = 8
N_CROSS = 16


def touch_ends(array, stream_key, least, largest):
    index_at = [jax.random.randint(jax.random.fold_in(stream_key, axis), (), 0, length) for axis, length in enumerate(array.shape)]
    widest = array.shape.index(max(array.shape))
    neighbour = index_at[:widest] + [(index_at[widest] + 1) % array.shape[widest]] + index_at[widest + 1:]
    return array.at[tuple(index_at)].set(least).at[tuple(neighbour)].set(largest)


def levels(rng, extent, shards, least, top_value):
    loudness = 1.0
    for dim, shards_of in shards:
        steps = jax.random.uniform(jax.random.fold_in(jax.random.fold_in(rng, 6), dim), (shards_of,), jnp.float32, least / len(shards), top_value / len(shards))
        loudness = loudness * jnp.repeat(jnp.exp(steps), extent[dim] // shards_of).reshape((-1,) + (1,) * (len(extent) - 1 - dim))
    return loudness


def normal_values(own_key, dims, spread, bound, pieces=(), held_as=jnp.bfloat16):
    gain = levels(own_key, dims, pieces, -0.22, 0.18) if pieces else 1.0
    drawn = jax.random.normal(own_key, dims, jnp.float32) * spread * gain
    return jnp.minimum(jnp.maximum(drawn, -bound), bound).astype(held_as)


def setup_inputs(seed: int = 0) -> dict:
    seeds = jax.random.split(jax.random.key(seed), 13)
    warming_above_ambient = jnp.clip(2.0 * jax.random.uniform(seeds[0], (TANGENT_EXTENT, LATHE_AXIS_COUNT, INWARD_EXTENT), jnp.float32) ** levels(seeds[0], (TANGENT_EXTENT, LATHE_AXIS_COUNT, INWARD_EXTENT), ((0, 8), (1, 16)), -0.2, 0.2), 0.0, 2.0)
    fourier_stability_factor = jnp.clip(jnp.exp(math.log(0.1) - 1.609438 * jax.random.uniform(seeds[1], (TANGENT_EXTENT, LATHE_AXIS_COUNT, INWARD_EXTENT), jnp.float32) ** levels(seeds[1], (TANGENT_EXTENT, LATHE_AXIS_COUNT, INWARD_EXTENT), ((0, 8), (1, 16)), -0.2, 0.2)), 0.02, 0.1)
    patch_locator = touch_ends(jax.random.randint(seeds[2], (DOTS_OVERALL,), 0, 2 * CX * CY * INWARD_EXTENT), jax.random.fold_in(seeds[2], 1), 0, (2 * CX * CY * INWARD_EXTENT) - 1).astype(jnp.int32)
    photon_gain_wattage = jnp.clip(jnp.exp(math.log(4.0) - 2.0794415 * jax.random.uniform(seeds[3], (DOTS_OVERALL,), jnp.float32) ** levels(seeds[3], (DOTS_OVERALL,), ((0, 128),), -0.2, 0.2)), 0.5, 4.0)
    on_skin_marker = touch_ends((jax.random.randint(seeds[4], (DOTS_OVERALL,), 0, 2) < 1).astype(jnp.int32), jax.random.fold_in(seeds[4], 1), 0, 1)
    grain_placements = jnp.clip(jax.random.uniform(seeds[5], (3, DOTS_OVERALL), jnp.float32, -1.0, 1.0) * levels(seeds[5], (3, DOTS_OVERALL), ((1, 128),), -0.4, 0.0), -1.0, 1.0)
    grain_motion_parts = normal_values(seeds[6], (3, DOTS_OVERALL), 0.5, 3.0, ((1, 128),), jnp.float32)
    tether_acted_grain = touch_ends(jax.random.randint(seeds[7], (BTOT,), 0, CAP * N_CROSS), jax.random.fold_in(seeds[7], 1), 0, (CAP * N_CROSS) - 1).astype(jnp.int32)
    tether_other_grain = touch_ends(jax.random.randint(seeds[8], (BTOT,), 0, CAP * N_CROSS + 2 * GHOSTS), jax.random.fold_in(seeds[8], 1), 0, (CAP * N_CROSS + 2 * GHOSTS) - 1).astype(jnp.int32)
    tether_relaxed_gap = jnp.clip(jnp.exp(math.log(1.5) - 1.0986123 * jax.random.uniform(seeds[9], (BTOT,), jnp.float32) ** levels(seeds[9], (BTOT,), ((0, 128),), -0.2, 0.2)), 0.5, 1.5)
    snapped_marker = touch_ends((jax.random.randint(seeds[10], (BTOT,), 0, 8) < 1).astype(jnp.int32), jax.random.fold_in(seeds[10], 1), 0, 1)
    exported_copies = touch_ends(jax.random.randint(seeds[11], (GTOT,), 0, CAP * N_CROSS), jax.random.fold_in(seeds[11], 1), 0, (CAP * N_CROSS) - 1).astype(jnp.int32)
    return {"warming_above_ambient": warming_above_ambient, "fourier_stability_factor": fourier_stability_factor, "patch_locator": patch_locator, "photon_gain_wattage": photon_gain_wattage, "on_skin_marker": on_skin_marker, "grain_placements": grain_placements, "grain_motion_parts": grain_motion_parts, "tether_acted_grain": tether_acted_grain, "tether_other_grain": tether_other_grain, "tether_relaxed_gap": tether_relaxed_gap, "snapped_marker": snapped_marker, "exported_copies": exported_copies}


def conduct(grain_warmth_reading):
    return 0.5 + 1.0 / (1.0 + grain_warmth_reading * grain_warmth_reading)

def advance(temp_pad, kappa_pad, thermal_input):
    temp_full = jnp.pad(temp_pad, ((0, 0), (0, 0), (1, 1)))
    kappa_full = jnp.pad(kappa_pad, ((0, 0), (0, 0), (1, 1)))
    conduct_full = kappa_full * conduct(temp_full)
    size_a = temp_full.shape[0] - 2
    size_b = temp_full.shape[1] - 2
    size_c = temp_full.shape[2] - 2
    center = temp_full[1:1 + size_a, 1:1 + size_b, 1:1 + size_c]
    middle = conduct_full[1:1 + size_a, 1:1 + size_b, 1:1 + size_c]
    change = jnp.zeros_like(center)
    for first, second, third in ((2, 1, 1), (0, 1, 1), (1, 2, 1), (1, 0, 1), (1, 1, 2), (1, 1, 0)):
        beside = temp_full[first:first + size_a, second:second + size_b, third:third + size_c]
        beside_c = conduct_full[first:first + size_a, second:second + size_b, third:third + size_c]
        change = change + 0.5 * (middle + beside_c) * (beside - center)
    return center + (change + thermal_input)

def pad_grid(field):
    field = jnp.pad(field, ((1, 1), (0, 0), (0, 0)), mode='wrap')
    return jnp.pad(field, ((0, 0), (1, 1), (0, 0)))

def reference(warming_above_ambient, fourier_stability_factor, patch_locator, photon_gain_wattage, on_skin_marker, grain_placements, grain_motion_parts, tether_acted_grain, tether_other_grain, tether_relaxed_gap, snapped_marker, exported_copies):
    structured_patch = CX * CY * INWARD_EXTENT
    rows = jnp.arange(DOTS_OVERALL, dtype=jnp.int32)
    device = rows // P_DEV
    cut_index = device // N_CROSS
    dest = rows % P_DEV // CAP
    offset = patch_locator // structured_patch
    remain = patch_locator % structured_patch
    grid_x = (cut_index + offset) % N_CUT * CX + remain // (CY * INWARD_EXTENT)
    grid_y = dest * CY + remain // INWARD_EXTENT % CY
    grid_z = remain % INWARD_EXTENT
    flat_cell = ((grid_x * LATHE_AXIS_COUNT + grid_y) * INWARD_EXTENT + grid_z).astype(jnp.int32)
    energy_current = on_skin_marker.astype(jnp.float32) * photon_gain_wattage * 0.5
    thermal_input = jnp.zeros((TANGENT_EXTENT * LATHE_AXIS_COUNT * INWARD_EXTENT,), jnp.float32).at[flat_cell].add(energy_current).reshape(TANGENT_EXTENT, LATHE_AXIS_COUNT, INWARD_EXTENT)
    kappa_pad = pad_grid(fourier_stability_factor)
    grain_warmth_reading = warming_above_ambient
    for substep in range(STEPS):
        grain_warmth_reading = advance(pad_grid(grain_warmth_reading), kappa_pad, thermal_input)
    particle_temp = grain_warmth_reading.reshape(-1)[flat_cell]
    brow = jnp.arange(BTOT, dtype=jnp.int32)
    bdev = brow // BONDS
    bcut = bdev // N_CROSS
    bside = bdev % N_CROSS
    low_dev = (bcut - 1) % N_CUT * N_CROSS + bside
    high_dev = (bcut + 1) % N_CUT * N_CROSS + bside
    low_k = jnp.clip(tether_other_grain - P_DEV, 0, GHOSTS - 1)
    high_k = jnp.clip(tether_other_grain - P_DEV - GHOSTS, 0, GHOSTS - 1)
    low_part = low_dev * P_DEV + exported_copies[(low_dev * GHOSTS + low_k).astype(jnp.int32)]
    high_part = high_dev * P_DEV + exported_copies[(high_dev * GHOSTS + high_k).astype(jnp.int32)]
    partner = jnp.where(tether_other_grain < P_DEV, bdev * P_DEV + tether_other_grain, jnp.where(tether_other_grain < P_DEV + GHOSTS, low_part, high_part)).astype(jnp.int32)
    first = (bdev * P_DEV + tether_acted_grain).astype(jnp.int32)
    delta = grain_placements[:, partner] - grain_placements[:, first]
    dist = jnp.sqrt(lax.optimization_barrier(jnp.sum(delta * delta, axis=0)))
    hot = tether_relaxed_gap * (1.0 + 0.2 * (0.5 * (particle_temp[first] + particle_temp[partner])))
    scale = (1.0 - snapped_marker.astype(jnp.float32)) * (dist - hot) / jnp.maximum(dist, 0.3)
    force = jnp.zeros((3, DOTS_OVERALL), jnp.float32).at[:, first].add(scale * delta)
    velocities_new = grain_motion_parts + 0.5 * force
    positions_new = grain_placements + 0.5 * velocities_new
    return (grain_warmth_reading, positions_new, velocities_new)
```

```python
import functools

import jax
import jax.numpy as jnp
from jax import lax
from jax.experimental import pallas as pl
from jax.experimental.pallas import tpu as pltpu
from jax.sharding import PartitionSpec as P

f32 = jnp.float32
bf16 = jnp.bfloat16
i32 = jnp.int32
MESH = pl.DeviceIdType.MESH
NT = (((1,), (1,)), ((), ()))
LANES = 128
VMEM = pl.BlockSpec(memory_space=pltpu.VMEM)


def stack(tile, count):
    return jnp.concatenate([tile] * count, axis=0)


def rows16(row):
    return jnp.broadcast_to(row, (16, row.shape[1])).astype(bf16)


def hot(row, iota):
    r = stack(rows16(row), iota.shape[0] // 16)
    return jnp.where(iota == r, jnp.ones_like(iota), jnp.zeros_like(iota))


def spread(row, val, iota):
    r = stack(rows16(row), iota.shape[0] // 16)
    v = stack(rows16(val), iota.shape[0] // 16)
    return jnp.where(iota == r, v, jnp.zeros_like(iota))


def iota_rows(count):
    return lax.broadcasted_iota(i32, (count, LANES), 0).astype(f32).astype(bf16)


def high(v):
    return v.astype(bf16).astype(f32)


def conduct(t):
    return 0.5 + 1.0 / (1.0 + t * t)


def peers(cuts, crosses):
    c, s = lax.axis_index("cut"), lax.axis_index("cross")
    below, above = lax.rem(c + cuts - 1, cuts), lax.rem(c + 1, cuts)
    return c, s, below, above


def greet(cuts, crosses):
    c, s, below, above = peers(cuts, crosses)
    barrier = pltpu.get_barrier_semaphore()

    def one(k, carry):
        pl.semaphore_signal(barrier, inc=1, device_id=(below, k), device_id_type=MESH)
        pl.semaphore_signal(barrier, inc=1, device_id=(above, k), device_id_type=MESH)
        return carry

    lax.fori_loop(0, crosses, one, 0)

    def other(k, carry):
        j = lax.rem(s + k, crosses)
        pl.semaphore_signal(barrier, inc=1, device_id=(c, j), device_id_type=MESH)
        return carry

    lax.fori_loop(1, crosses, other, 0)


def await_all(crosses):
    pl.semaphore_wait(pltpu.get_barrier_semaphore(), 3 * crosses - 1)


def remote(src, dst, send, recv, device):
    return pltpu.make_async_remote_copy(
        src_ref=src, dst_ref=dst, send_sem=send, recv_sem=recv, device_id=device, device_id_type=MESH
    )


def load_table(tab_ref, row_ref, channels, rows, pitch, dest):
    for ch in range(channels):
        for r in range(rows):
            dest[ch * pitch + r : ch * pitch + r + 1, :] = row_ref[ch : ch + 1, r * LANES : (r + 1) * LANES]
    v = dest[...]
    hi = v.astype(bf16)
    n = channels * pitch
    tab_ref[0:n, :] = hi
    tab_ref[n : 2 * n, :] = (v - hi.astype(f32)).astype(bf16)


def pick_small(tab, channels, pitch, high_row, low_row, iota128):
    got = jnp.dot(tab, hot(low_row, iota128), preferred_element_type=f32)
    n = channels * pitch
    s = lax.broadcasted_iota(i32, (pitch, LANES), 0).astype(f32)
    mask = s == high_row
    out = []
    for ch in range(channels):
        v = got[ch * pitch : (ch + 1) * pitch] + got[n + ch * pitch : n + (ch + 1) * pitch]
        out.append(jnp.sum(jnp.where(mask, v, 0.0), axis=0, keepdims=True))
    return out


def exchange_kernel(
    cuts, crosses, loc, gain, mark, temp, kappa, pos, acted, other, exported,
    lists, hx, hy, ghosts, d_own,
    send_lists, ysend, tab, flat, gsend, send_sem, recv_sem, hsend, hrecv,
):
    c, s, below, above = peers(cuts, crosses)
    greet(cuts, crosses)
    w = loc[...].astype(f32)
    flux = mark[...].astype(f32) * gain[...] * 0.5
    per = w.shape[0] // crosses
    for j in range(crosses):
        send_lists[j, 0:per, :] = w[j * per : (j + 1) * per]
        send_lists[j, per : 2 * per, :] = flux[j * per : (j + 1) * per]
    nx = ysend.shape[2]
    ny = temp.shape[0] // nx
    for a, ref in enumerate((temp, kappa)):
        ysend[a, 0] = ref[pl.ds(0, nx, stride=ny), :]
        ysend[a, 1] = ref[pl.ds(ny - 1, nx, stride=ny), :]
    hi_rows = pos.shape[1] // LANES
    load_table(tab, pos, 3, hi_rows, hi_rows, flat)
    iota = iota_rows(LANES)
    table = tab[...]
    gcount = exported.shape[0]
    for r in range(gcount):
        q = exported[r : r + 1, :]
        v = pick_small(table, 3, hi_rows, (q // LANES).astype(f32), (q % LANES).astype(f32), iota)
        for ch in range(3):
            gsend[ch * gcount + r : ch * gcount + r + 1, :] = v[ch]
    await_all(crosses)

    def send_one(k, carry):
        j = lax.rem(s + k, crosses)
        remote(
            send_lists.at[j], lists.at[crosses + s], send_sem.at[crosses + j], recv_sem.at[crosses + s], (above, j)
        ).start()
        return carry

    def send_same(k, carry):
        j = lax.rem(s + k, crosses)
        remote(send_lists.at[j], lists.at[s], send_sem.at[j], recv_sem.at[s], (c, j)).start()
        return carry

    lax.fori_loop(1, crosses, send_same, 0)
    lax.fori_loop(0, crosses, send_one, 0)
    lists[pl.ds(s, 1)] = send_lists[pl.ds(s, 1)]
    left, right = lax.rem(s + crosses - 1, crosses), lax.rem(s + 1, crosses)
    copies = []
    rows = temp.shape[0]
    for a, ref in enumerate((temp, kappa)):
        copies.append(remote(ref.at[pl.ds(rows - ny, ny)], hx.at[a, 0], hsend.at[4 * a], hrecv.at[4 * a], (above, s)))
        copies.append(remote(ref.at[pl.ds(0, ny)], hx.at[a, 1], hsend.at[4 * a + 1], hrecv.at[4 * a + 1], (below, s)))
        copies.append(remote(ysend.at[a, 1], hy.at[a, 0], hsend.at[4 * a + 2], hrecv.at[4 * a + 2], (c, right)))
        copies.append(remote(ysend.at[a, 0], hy.at[a, 1], hsend.at[4 * a + 3], hrecv.at[4 * a + 3], (c, left)))
    copies.append(remote(gsend, ghosts.at[0], hsend.at[8], hrecv.at[8], (above, s)))
    copies.append(remote(gsend, ghosts.at[1], hsend.at[9], hrecv.at[9], (below, s)))
    for copy in copies:
        copy.start()

    def gather(r, carry):
        q = acted[pl.ds(r, 1), :]
        first = pick_small(table, 3, hi_rows, (q // LANES).astype(f32), (q % LANES).astype(f32), iota)
        q = other[pl.ds(r, 1), :]
        second = pick_small(table, 3, hi_rows, (q // LANES).astype(f32), (q % LANES).astype(f32), iota)
        for ch in range(3):
            d_own[ch, pl.ds(r, 1), :] = second[ch] - first[ch]
        return carry

    lax.fori_loop(0, acted.shape[0], gather, 0, unroll=2)

    def take_same(k, carry):
        j = lax.rem(s + k, crosses)
        remote(send_lists.at[j], lists.at[j], send_sem.at[j], recv_sem.at[j], (c, j)).wait()
        return carry

    def take_one(j, carry):
        n = crosses + j
        remote(send_lists.at[j], lists.at[n], send_sem.at[n], recv_sem.at[n], (above, j)).wait()
        return carry

    lax.fori_loop(1, crosses, take_same, 0)
    lax.fori_loop(0, crosses, take_one, 0)
    for copy in copies:
        copy.wait()


def deposit_kernel(crosses, cells, lists, src, row, zed, val, sp, big):
    per = lists.shape[1] // 2
    for b in range(2 * crosses):
        w = lists[b, 0:per, :].astype(i32)
        here = (w >= cells) == (b >= crosses)
        w = w & (cells - 1)
        row[b * per : (b + 1) * per, :] = jnp.where(here, w // LANES, -1).astype(f32)
        zed[b * per : (b + 1) * per, :] = (w % LANES).astype(f32)
        val[b * per : (b + 1) * per, :] = jnp.where(here, lists[b, per : 2 * per, :], 0.0)
    big[...] = iota_rows(256)
    iota = big[...]
    small = iota[:LANES]
    count = row.shape[0]

    def build(r, carry):
        z = zed[pl.ds(r, 1), :]
        v = val[pl.ds(r, 1), :]
        hi = high(v)
        where = pl.ds(pl.multiple_of(r * LANES, LANES), LANES)
        sp[0:LANES, where] = spread(z, hi, small)
        sp[LANES : 2 * LANES, where] = spread(z, v - hi, small)
        return carry

    lax.fori_loop(0, count, build, 0, unroll=2)
    block, depth = 512, 16

    def outer(m, carry):
        first = m.astype(f32) * float(block)

        def inner(k, acc):
            pieces = []
            for h in range(depth):
                r = row[pl.ds(k * depth + h, 1), :] - first
                parts = []
                for g in range(block // 256):
                    q = r - 256.0 * g
                    parts.append(hot(jnp.where((q >= 0) & (q < 256), q, -1.0), iota))
                pieces.append(jnp.concatenate(parts, axis=0))
            where = pl.ds(pl.multiple_of(k * (depth * LANES), depth * LANES), depth * LANES)
            return acc + lax.dot_general(
                jnp.concatenate(pieces, axis=1), sp[:, where], NT, preferred_element_type=f32
            )

        acc = lax.fori_loop(0, count // depth, inner, jnp.zeros((block, 2 * LANES), f32))
        src[pl.ds(pl.multiple_of(m * block, block), block), :] = acc[:, :LANES] + acc[:, LANES:]
        return carry

    lax.fori_loop(0, src.shape[0] // block, outer, 0)


def main_kernel(
    cuts, crosses, temp, kappa, src, row, zed, hx, hy, ghosts, d_own, acted, other, gap, snapped, exported, loc, pos, vel,
    temp_out, pos_out, vel_out,
    ta, tb, ca, cb, ysend, hyt, hcy, tt, big, picked, back, stage, gtemp_send, gtemp, pq, own, tab,
    xs, xr, ys, yr, bs, br, gs, gr,
):
    c, s, below, above = peers(cuts, crosses)
    left, right = lax.rem(s + crosses - 1, crosses), lax.rem(s + 1, crosses)
    greet(cuts, crosses)
    rows = temp.shape[0]
    nx = hy.shape[2]
    ny = rows // nx
    final = crosses - 1
    low_edge, high_edge = s == 0, s == final
    sub = lax.broadcasted_iota(i32, (ny, LANES), 0)
    lane = lax.broadcasted_iota(i32, (ny, LANES), 1)

    def begin(x, carry):
        where = pl.ds(pl.multiple_of(x * ny, ny), ny)
        there = pl.ds(pl.multiple_of(x * ny + ny, ny), ny)
        t = temp[where, :]
        ta[there, :] = t
        ca[there, :] = kappa[where, :] * conduct(t)
        return carry

    lax.fori_loop(0, nx, begin, 0, unroll=4)
    ta[0:ny, :] = hx[0, 0]
    ta[rows + ny : rows + 2 * ny, :] = hx[0, 1]

    def edge(ref, tref):
        ref[0:ny, :] = hx[1, 0] * conduct(tref[0:ny, :])
        ref[rows + ny : rows + 2 * ny, :] = hx[1, 1] * conduct(tref[rows + ny : rows + 2 * ny, :])

    def rim(plane):
        lo = jnp.where(low_edge, 0.0, plane[0])
        hi = jnp.where(high_edge, 0.0, plane[1])
        klo = jnp.where(low_edge, 0.0, hy[1, 0])
        khi = jnp.where(high_edge, 0.0, hy[1, 1])
        hyt[0] = lo
        hyt[1] = hi
        hcy[0] = klo * conduct(lo)
        hcy[1] = khi * conduct(hi)

    def step(tin, cin, tout, cout):
        def body(x, carry):
            t0, c0, before = carry
            where = pl.ds(pl.multiple_of(x * ny, ny), ny)
            here = pl.ds(pl.multiple_of(x * ny + ny, ny), ny)
            ahead = pl.ds(pl.multiple_of(x * ny + 2 * ny, ny), ny)
            t1 = tin[ahead, :]
            c1 = cin[ahead, :]
            fx = (c0 + c1) * (t1 - t0)
            at = pl.ds(x, 1)
            thi = jnp.where(sub == ny - 1, hyt[1, at, :], pltpu.roll(t0, ny - 1, 0))
            chi = jnp.where(sub == ny - 1, hcy[1, at, :], pltpu.roll(c0, ny - 1, 0))
            fy = (c0 + chi) * (thi - t0)
            flo = (hcy[0, at, :] + c0[0:1]) * (t0[0:1] - hyt[0, at, :])
            fy0 = jnp.where(sub == 0, flo, pltpu.roll(fy, 1, 0))
            tz = jnp.where(lane == LANES - 1, 0.0, pltpu.roll(t0, LANES - 1, 1))
            cz = jnp.where(lane == LANES - 1, 0.0, pltpu.roll(c0, LANES - 1, 1))
            fz = (c0 + cz) * (tz - t0)
            fz0 = jnp.where(lane == 0, c0 * t0, pltpu.roll(fz, 1, 1))
            change = 0.5 * (((fx - before) + (fy - fy0)) + (fz - fz0))
            tn = t0 + (change + src[where, :])
            if cout is None:
                tout[where, :] = tn
            else:
                tout[here, :] = tn
                cout[here, :] = kappa[where, :] * conduct(tn)
            return t1, c1, fx

        t0 = tin[ny : 2 * ny, :]
        c0 = cin[ny : 2 * ny, :]
        tm = tin[0:ny, :]
        cm = cin[0:ny, :]
        lax.fori_loop(0, nx, body, (t0, c0, (cm + c0) * (t0 - tm)), unroll=4)

    def send_halo(k, tref):
        ysend[k, 0] = tref[pl.ds(ny, nx, stride=ny), :]
        ysend[k, 1] = tref[pl.ds(2 * ny - 1, nx, stride=ny), :]
        copies = [
            remote(ysend.at[k, 1], stage.at[k, 0], ys.at[2 * k], yr.at[2 * k], (c, right)),
            remote(ysend.at[k, 0], stage.at[k, 1], ys.at[2 * k + 1], yr.at[2 * k + 1], (c, left)),
            remote(
                tref.at[pl.ds(rows, ny)], tref.at[pl.ds(0, ny)], xs.at[2 * k], xr.at[2 * k], (above, s)
            ),
            remote(
                tref.at[pl.ds(ny, ny)], tref.at[pl.ds(rows + ny, ny)], xs.at[2 * k + 1], xr.at[2 * k + 1], (below, s)
            ),
        ]
        for copy in copies:
            copy.start()
        return copies

    edge(ca, ta)
    rim(hy[0])
    step(ta, ca, tb, cb)
    await_all(crosses)
    first = send_halo(0, tb)

    iota = iota_rows(LANES)
    hi_rows = pos.shape[1] // LANES
    gcount = exported.shape[0]
    bond_rows = acted.shape[0]
    gl = jnp.concatenate([ghosts[0], ghosts[1]], axis=0)
    pad = jnp.zeros((LANES - 4 * 3 * gcount, LANES), f32)
    glo = jnp.concatenate([high(gl), gl - high(gl), pad], axis=0).astype(bf16)

    def ghost_pick(r, carry):
        q = other[pl.ds(r, 1), :] - hi_rows * LANES
        got = jnp.dot(glo, hot((q & (LANES - 1)).astype(f32), iota), preferred_element_type=f32)
        got = got[0 : 6 * gcount] + got[6 * gcount : 12 * gcount]
        h = q // LANES
        for ch in range(3):
            v = jnp.zeros((1, LANES), f32)
            for side in range(2):
                for g in range(gcount):
                    n = (side * 3 + ch) * gcount + g
                    v = v + jnp.where((q >= 0) & (h == side * gcount + g), got[n : n + 1], 0.0)
            pq[ch, pl.ds(r, 1), :] = d_own[ch, pl.ds(r, 1), :] + v
        return carry

    lax.fori_loop(0, bond_rows, ghost_pick, 0, unroll=2)
    d = [pq[ch] for ch in range(3)]
    dist = jnp.sqrt(d[0] * d[0] + d[1] * d[1] + d[2] * d[2])
    g = gap[...]
    base = (1.0 - snapped[...].astype(f32)) / jnp.maximum(dist, 0.3)
    p = base * (dist - g)
    q = base * (-0.1 * g)
    for ch in range(3):
        pq[ch] = p * d[ch]
        pq[3 + ch] = q * d[ch]
    iota32 = iota[:hi_rows]

    def scatter(lo, hi):
        n = hi - lo
        depth = 4

        def body(k, acc):
            lhs, rhs = [], []
            for u in range(depth):
                r = k * depth + u
                a = acted[pl.ds(r, 1), :]
                rhs.append(hot((a % LANES).astype(f32), iota))
                h = (a // LANES).astype(f32)
                tops, lows = [], []
                for ch in range(lo, hi):
                    v = pq[ch, pl.ds(r, 1), :]
                    top = high(v)
                    tops.append(spread(h, top, iota32))
                    lows.append(spread(h, v - top, iota32))
                lhs.append(jnp.concatenate(tops + lows, axis=0))
            return acc + lax.dot_general(
                jnp.concatenate(lhs, axis=1), jnp.concatenate(rhs, axis=1), NT, preferred_element_type=f32
            )

        acc = lax.fori_loop(0, bond_rows // depth, body, jnp.zeros((2 * n * hi_rows, LANES), f32))
        return acc[: n * hi_rows] + acc[n * hi_rows :]

    own[...] = scatter(0, 6)

    for copy in first:
        copy.wait()
    edge(cb, tb)
    rim(stage[0])
    step(tb, cb, ta, ca)
    second = send_halo(1, ta)
    big[...] = iota_rows(256)
    for copy in second:
        copy.wait()
    edge(ca, ta)
    rim(stage[1])
    step(ta, ca, temp_out, None)

    for k in range(rows // LANES):
        b = temp_out[k * LANES : (k + 1) * LANES, :].T
        hi = b.astype(bf16)
        tt[0:LANES, k * LANES : (k + 1) * LANES] = hi
        tt[LANES : 2 * LANES, k * LANES : (k + 1) * LANES] = (b - hi.astype(f32)).astype(bf16)
    wide = big[...]
    per = picked.shape[1]
    both = 2
    zs = lax.broadcasted_iota(i32, (LANES, LANES), 0).astype(f32)

    def look(j, slots):
        cols = []
        for n in slots:
            for h in range(per):
                r = row[pl.ds(n * per + h, 1), :]
                parts = []
                for k in range(rows // 256):
                    q = r - 256.0 * k
                    parts.append(hot(jnp.where((q >= 0) & (q < 256), q, -1.0), wide))
                cols.append(jnp.concatenate(parts, axis=0))
        got = jnp.dot(tt[...], jnp.concatenate(cols, axis=1), preferred_element_type=f32)
        got = got[:LANES] + got[LANES:]
        for i, n in enumerate(slots):
            for h in range(per):
                u = i * per + h
                z = zed[pl.ds(n * per + h, 1), :]
                v = jnp.where(zs == z, got[:, u * LANES : (u + 1) * LANES], 0.0)
                picked[n, h : h + 1, :] = jnp.sum(v, axis=0, keepdims=True)

    def look_far(k, carry):
        j = lax.rem(s + k, crosses)
        look(j, (crosses + j, j))
        remote(picked.at[crosses + j], back.at[crosses + s], bs.at[crosses + j], br.at[crosses + s], (below, j)).start()
        remote(picked.at[j], back.at[s], bs.at[j], br.at[s], (c, j)).start()
        return carry

    lax.fori_loop(1, crosses, look_far, 0)
    look(s, (crosses + s, s))
    remote(picked.at[crosses + s], back.at[crosses + s], bs.at[crosses + s], br.at[crosses + s], (below, s)).start()
    back[pl.ds(s, 1)] = picked[pl.ds(s, 1)]

    def take_same(k, carry):
        j = lax.rem(s + k, crosses)
        remote(picked.at[j], back.at[j], bs.at[j], br.at[j], (c, j)).wait()
        return carry

    def take_far(j, carry):
        n = crosses + j
        remote(picked.at[n], back.at[n], bs.at[n], br.at[n], (below, j)).wait()
        return carry

    lax.fori_loop(1, crosses, take_same, 0)
    lax.fori_loop(0, crosses, take_far, 0)
    cells = rows * LANES
    warm = jnp.where(
        loc[...] >= cells,
        jnp.concatenate([back[crosses + j] for j in range(crosses)], axis=0),
        jnp.concatenate([back[j] for j in range(crosses)], axis=0),
    )
    whi = warm.astype(bf16)
    tab[...] = jnp.concatenate([whi, (warm - whi.astype(f32)).astype(bf16)], axis=0)
    table = tab[...]
    for r in range(gcount):
        e = exported[r : r + 1, :]
        v = pick_small(table, 1, hi_rows, (e // LANES).astype(f32), (e % LANES).astype(f32), iota)
        gtemp_send[r : r + 1, :] = v[0]
    copies = [
        remote(gtemp_send, gtemp.at[0], gs.at[0], gr.at[0], (above, s)),
        remote(gtemp_send, gtemp.at[1], gs.at[1], gr.at[1], (below, s)),
    ]
    for copy in copies:
        copy.start()

    def warm_own(r, carry):
        e = other[pl.ds(r, 1), :]
        v = pick_small(table, 1, hi_rows, (e // LANES).astype(f32), (e % LANES).astype(f32), iota)
        pq[0, pl.ds(r, 1), :] = v[0]
        return carry

    lax.fori_loop(0, bond_rows, warm_own, 0, unroll=2)
    for copy in copies:
        copy.wait()
    gt = jnp.concatenate([gtemp[0], gtemp[1]], axis=0)
    gt = jnp.concatenate([high(gt), gt - high(gt), jnp.zeros((16 - 4 * gcount, LANES), f32)], axis=0).astype(bf16)

    def warm_ghost(r, carry):
        e = other[pl.ds(r, 1), :] - hi_rows * LANES
        got = jnp.dot(gt, hot((e & (LANES - 1)).astype(f32), iota), preferred_element_type=f32)
        got = got[0 : 2 * gcount] + got[2 * gcount : 4 * gcount]
        h = e // LANES
        v = pq[0, pl.ds(r, 1), :]
        for n in range(2 * gcount):
            v = v + jnp.where((e >= 0) & (h == n), got[n : n + 1], 0.0)
        for ch in range(3):
            pq[3 + ch, pl.ds(r, 1), :] = pq[3 + ch, pl.ds(r, 1), :] * v
        return carry

    lax.fori_loop(0, bond_rows, warm_ghost, 0, unroll=2)
    extra = scatter(3, 6)
    base = own[...]
    n = 3 * hi_rows
    force = base[:n] + extra + jnp.concatenate([warm] * 3, axis=0) * base[n:]
    for ch in range(3):
        for r in range(hi_rows):
            where = slice(r * LANES, (r + 1) * LANES)
            v = vel[ch : ch + 1, where] + 0.5 * force[ch * hi_rows + r : ch * hi_rows + r + 1]
            vel_out[ch : ch + 1, where] = v
            pos_out[ch : ch + 1, where] = pos[ch : ch + 1, where] + 0.5 * v


def per_device(
    cuts, crosses, temp, kappa, locator, gain, mark, pos, vel, acted, other, gap, snapped, exported
):
    nx, ny, nz = temp.shape
    rows = nx * ny
    temp2, kappa2 = temp.reshape(rows, nz), kappa.reshape(rows, nz)
    flat = lambda a: a.reshape(-1, LANES)
    loc, gain, mark = flat(locator), flat(gain), flat(mark)
    acted, other, gap, snapped, exported = map(flat, (acted, other, gap, snapped, exported))
    hi_rows = loc.shape[0]
    per = hi_rows // crosses
    gcount = exported.shape[0]
    bonds = acted.shape[0]
    shape = jax.ShapeDtypeStruct
    dma = pltpu.SemaphoreType.DMA
    lists, hx, hy, ghosts, d_own = pl.pallas_call(
        functools.partial(exchange_kernel, cuts, crosses),
        out_shape=(
            shape((2 * crosses, 2 * per, LANES), f32),
            shape((2, 2, ny, nz), f32),
            shape((2, 2, nx, nz), f32),
            shape((2, 3 * gcount, LANES), f32),
            shape((3, bonds, LANES), f32),
        ),
        in_specs=[VMEM] * 9,
        out_specs=(VMEM,) * 5,
        scratch_shapes=[
            pltpu.VMEM((crosses, 2 * per, LANES), f32),
            pltpu.VMEM((2, 2, nx, nz), f32),
            pltpu.VMEM((6 * hi_rows, LANES), bf16),
            pltpu.VMEM((3 * hi_rows, LANES), f32),
            pltpu.VMEM((3 * gcount, LANES), f32),
            dma((2 * crosses,)),
            dma((2 * crosses,)),
            dma((10,)),
            dma((10,)),
        ],
        compiler_params=pltpu.CompilerParams(collective_id=0, has_side_effects=True),
        name="exchange",
    )(loc, gain, mark, temp2, kappa2, pos, acted, other, exported)
    lr = 2 * crosses * per
    src, row, zed = pl.pallas_call(
        functools.partial(deposit_kernel, crosses, rows * nz),
        out_shape=(shape((rows, nz), f32), shape((lr, LANES), f32), shape((lr, LANES), f32)),
        in_specs=[VMEM],
        out_specs=(VMEM,) * 3,
        scratch_shapes=[
            pltpu.VMEM((lr, LANES), f32),
            pltpu.VMEM((2 * LANES, lr * LANES), bf16),
            pltpu.VMEM((256, LANES), bf16),
        ],
        name="deposit",
    )(lists)
    temp_new, pos_new, vel_new = pl.pallas_call(
        functools.partial(main_kernel, cuts, crosses),
        out_shape=(shape((rows, nz), f32), shape(pos.shape, f32), shape(vel.shape, f32)),
        in_specs=[VMEM] * 17,
        out_specs=(VMEM,) * 3,
        scratch_shapes=[
            pltpu.VMEM((rows + 2 * ny, nz), f32),
            pltpu.VMEM((rows + 2 * ny, nz), f32),
            pltpu.VMEM((rows + 2 * ny, nz), f32),
            pltpu.VMEM((rows + 2 * ny, nz), f32),
            pltpu.VMEM((2, 2, nx, nz), f32),
            pltpu.VMEM((2, nx, nz), f32),
            pltpu.VMEM((2, nx, nz), f32),
            pltpu.VMEM((2 * nz, rows), bf16),
            pltpu.VMEM((256, LANES), bf16),
            pltpu.VMEM((2 * crosses, per, LANES), f32),
            pltpu.VMEM((2 * crosses, per, LANES), f32),
            pltpu.VMEM((2, 2, nx, nz), f32),
            pltpu.VMEM((gcount, LANES), f32),
            pltpu.VMEM((2, gcount, LANES), f32),
            pltpu.VMEM((6, bonds, LANES), f32),
            pltpu.VMEM((6 * hi_rows, LANES), f32),
            pltpu.VMEM((2 * hi_rows, LANES), bf16),
            dma((4,)),
            dma((4,)),
            dma((4,)),
            dma((4,)),
            dma((2 * crosses,)),
            dma((2 * crosses,)),
            dma((2,)),
            dma((2,)),
        ],
        compiler_params=pltpu.CompilerParams(collective_id=1, has_side_effects=True),
        name="heat_and_bonds",
    )(temp2, kappa2, src, row, zed, hx, hy, ghosts, d_own, acted, other, gap, snapped, exported, loc, pos, vel)
    return temp_new.reshape(nx, ny, nz), pos_new, vel_new


def solution(mesh):
    both = P(("cut", "cross"))
    return jax.shard_map(
        functools.partial(per_device, mesh.shape["cut"], mesh.shape["cross"]),
        mesh=mesh,
        in_specs=(P("cut", "cross", None),) * 2
        + (both,) * 3
        + (P(None, ("cut", "cross")),) * 2
        + (both,) * 5,
        out_specs=(P("cut", "cross", None), P(None, ("cut", "cross")), P(None, ("cut", "cross"))),
        check_vma=False,
    )
```

```python
import functools

import jax
import jax.numpy as jnp
from jax import lax
from jax.experimental import pallas as pl
from jax.experimental.pallas import tpu as pltpu
from jax.sharding import PartitionSpec as P

f32 = jnp.float32
bf16 = jnp.bfloat16
i32 = jnp.int32
MESH = pl.DeviceIdType.MESH
NT = (((1,), (1,)), ((), ()))
LANES = 128
VMEM = pl.BlockSpec(memory_space=pltpu.VMEM)


def stack(tile, count):
    return jnp.concatenate([tile] * count, axis=0)


def rows16(row):
    return jnp.broadcast_to(row, (16, row.shape[1])).astype(bf16)


def hot(row, iota):
    r = stack(rows16(row), iota.shape[0] // 16)
    return jnp.where(iota == r, jnp.ones_like(iota), jnp.zeros_like(iota))


def spread(row, val, iota):
    r = stack(rows16(row), iota.shape[0] // 16)
    v = stack(rows16(val), iota.shape[0] // 16)
    return jnp.where(iota == r, v, jnp.zeros_like(iota))


def iota_rows(count):
    return lax.broadcasted_iota(i32, (count, LANES), 0).astype(f32).astype(bf16)


def high(v):
    return v.astype(bf16).astype(f32)


def conduct(t):
    return 0.5 + 1.0 / (1.0 + t * t)


def peers(cuts, crosses):
    c, s = lax.axis_index("cut"), lax.axis_index("cross")
    below, above = lax.rem(c + cuts - 1, cuts), lax.rem(c + 1, cuts)
    return c, s, below, above


def greet(cuts, crosses):
    c, s, below, above = peers(cuts, crosses)
    barrier = pltpu.get_barrier_semaphore()

    def one(k, carry):
        pl.semaphore_signal(barrier, inc=1, device_id=(below, k), device_id_type=MESH)
        pl.semaphore_signal(barrier, inc=1, device_id=(above, k), device_id_type=MESH)
        return carry

    lax.fori_loop(0, crosses, one, 0)

    def other(k, carry):
        j = lax.rem(s + k, crosses)
        pl.semaphore_signal(barrier, inc=1, device_id=(c, j), device_id_type=MESH)
        return carry

    lax.fori_loop(1, crosses, other, 0)


def await_all(crosses):
    pl.semaphore_wait(pltpu.get_barrier_semaphore(), 3 * crosses - 1)


def remote(src, dst, send, recv, device):
    return pltpu.make_async_remote_copy(
        src_ref=src, dst_ref=dst, send_sem=send, recv_sem=recv, device_id=device, device_id_type=MESH
    )


def lane_pick(row, index):
    return jnp.take_along_axis(row, index, axis=1, mode="promise_in_bounds")


def table_pick(rows, high_index, low_index, start):
    out = start
    for number, row in rows:
        wide = jnp.broadcast_to(row, low_index.shape)
        out = jnp.where(high_index == number, lane_pick(wide, low_index), out)
    return out


def kernel(
    cuts, crosses, loc, gain, mark, temp, kappa, pos, vel, acted, other, gap, snapped, exported,
    temp_out, pos_out, vel_out,
    lists, send_lists, hx, hy, ysend0, ghosts, gsend,
    row, zed, val, sp, ohl, big, d1, src, ta, tb, ca, cb, ysend, flux, tt, picked, back, stage,
    gtemp_send, gtemp, pq, own,
    send_sem, recv_sem, hsend, hrecv, xs, xr, ys, yr, bs, br, gs, gr,
):
    c, s, below, above = peers(cuts, crosses)
    left, right = lax.rem(s + crosses - 1, crosses), lax.rem(s + 1, crosses)
    greet(cuts, crosses)
    rows = temp.shape[0]
    nx = hy.shape[2]
    ny = rows // nx
    cells = rows * LANES
    hi_rows = loc.shape[0]
    per = hi_rows // crosses
    gcount = exported.shape[0]
    bond_rows = acted.shape[0]

    w = loc[...].astype(f32)
    power = mark[...].astype(f32) * gain[...] * 0.5
    for j in range(crosses):
        send_lists[j, 0:per, :] = w[j * per : (j + 1) * per]
        send_lists[j, per : 2 * per, :] = power[j * per : (j + 1) * per]
    for a, ref in enumerate((temp, kappa)):
        ysend0[a, 0] = ref[pl.ds(0, nx, stride=ny), :]
        ysend0[a, 1] = ref[pl.ds(ny - 1, nx, stride=ny), :]
    e8 = jnp.concatenate([exported[...]] * (8 // gcount), axis=0)
    eh, el = e8 // LANES, e8 % LANES
    zero8 = jnp.zeros((8, LANES), f32)

    def row_of(ref, ch, r):
        return ref[ch : ch + 1, pl.ds(pl.multiple_of(r * LANES, LANES), LANES)]

    def export_rows(r, acc):
        return tuple(table_pick([(r, row_of(pos, ch, r))], eh, el, acc[ch]) for ch in range(3))

    acc = lax.fori_loop(0, hi_rows, export_rows, (zero8,) * 3, unroll=8)
    for ch in range(3):
        gsend[ch * gcount : (ch + 1) * gcount, :] = acc[ch][:gcount]

    group = 16

    def differences(k, carry):
        where = pl.ds(pl.multiple_of(k * group, group), group)
        qa, qb = acted[where, :], other[where, :]
        index = [(q[h : h + 8] // LANES, q[h : h + 8] % LANES) for q in (qa, qb) for h in range(0, group, 8)]

        def one(r, acc):
            out = []
            for ch in range(3):
                wide = jnp.broadcast_to(row_of(pos, ch, r), (8, LANES))
                for n, (h, l) in enumerate(index):
                    out.append(jnp.where(h == r, lane_pick(wide, l), acc[ch * len(index) + n]))
            return tuple(out)

        acc = lax.fori_loop(0, hi_rows, one, (zero8,) * (3 * len(index)), unroll=4)
        half = len(index) // 2
        for ch in range(3):
            for n in range(half):
                first, second = acc[ch * len(index) + n], acc[ch * len(index) + half + n]
                pq[ch, pl.ds(pl.multiple_of(k * group + 8 * n, 8), 8), :] = second - first
        return carry

    lax.fori_loop(0, bond_rows // group, differences, 0)
    await_all(crosses)

    def send_one(k, carry):
        j = lax.rem(s + k, crosses)
        n = crosses + j
        remote(send_lists.at[j], lists.at[crosses + s], send_sem.at[n], recv_sem.at[crosses + s], (above, j)).start()
        return carry

    def send_same(k, carry):
        j = lax.rem(s + k, crosses)
        remote(send_lists.at[j], lists.at[s], send_sem.at[j], recv_sem.at[s], (c, j)).start()
        return carry

    lax.fori_loop(1, crosses, send_same, 0)
    lax.fori_loop(0, crosses, send_one, 0)
    lists[pl.ds(s, 1)] = send_lists[pl.ds(s, 1)]
    early = []
    for a, ref in enumerate((temp, kappa)):
        early.append(remote(ysend0.at[a, 1], hy.at[a, 0], hsend.at[4 * a + 2], hrecv.at[4 * a + 2], (c, right)))
        early.append(remote(ysend0.at[a, 0], hy.at[a, 1], hsend.at[4 * a + 3], hrecv.at[4 * a + 3], (c, left)))
        early.append(remote(ref.at[pl.ds(rows - ny, ny)], hx.at[a, 0], hsend.at[4 * a], hrecv.at[4 * a], (above, s)))
        early.append(remote(ref.at[pl.ds(0, ny)], hx.at[a, 1], hsend.at[4 * a + 1], hrecv.at[4 * a + 1], (below, s)))
    early.append(remote(gsend, ghosts.at[0], hsend.at[8], hrecv.at[8], (above, s)))
    early.append(remote(gsend, ghosts.at[1], hsend.at[9], hrecv.at[9], (below, s)))
    for copy in early:
        copy.start()

    block = 16 * ny

    def begin(b, carry):
        where = pl.ds(pl.multiple_of(b * block, block), block)
        there = pl.ds(pl.multiple_of(b * block + ny, ny), block)
        t = temp[where, :]
        ta[there, :] = t
        ca[there, :] = kappa[where, :] * conduct(t)
        return carry

    lax.fori_loop(0, rows // block, begin, 0)
    big[...] = iota_rows(256)
    iota = big[...]
    small = iota[:LANES]

    def lows(k, carry):
        for u in range(4):
            r = k * 4 + u
            a = (acted[pl.ds(r, 1), :] % LANES).astype(f32)
            ohl[:, pl.ds(pl.multiple_of(r * LANES, LANES), LANES)] = hot(a, small)
        return carry

    lax.fori_loop(0, bond_rows // 4, lows, 0)

    def take_same(k, carry):
        j = lax.rem(s + k, crosses)
        remote(send_lists.at[j], lists.at[j], send_sem.at[j], recv_sem.at[j], (c, j)).wait()
        return carry

    def take_one(j, carry):
        n = crosses + j
        remote(send_lists.at[j], lists.at[n], send_sem.at[n], recv_sem.at[n], (above, j)).wait()
        return carry

    lax.fori_loop(1, crosses, take_same, 0)
    lax.fori_loop(0, crosses, take_one, 0)

    for b in range(2 * crosses):
        q = lists[b, 0:per, :].astype(i32)
        here = (q >= cells) == (b >= crosses)
        q = q & (cells - 1)
        row[b * per : (b + 1) * per, :] = jnp.where(here, q // LANES, -1).astype(f32)
        zed[b * per : (b + 1) * per, :] = (q % LANES).astype(f32)
        val[b * per : (b + 1) * per, :] = jnp.where(here, lists[b, per : 2 * per, :], 0.0)
    count = row.shape[0]

    def build(k, carry):
        for u in range(4):
            r = k * 4 + u
            z = zed[pl.ds(r, 1), :]
            v = val[pl.ds(r, 1), :]
            hi = high(v)
            where = pl.ds(pl.multiple_of(r * LANES, LANES), LANES)
            sp[0:LANES, where] = spread(z, hi, small)
            sp[LANES : 2 * LANES, where] = spread(z, v - hi, small)
        return carry

    lax.fori_loop(0, count // 4, build, 0)
    r_all = row[...].astype(i32)
    y = r_all & (ny - 1)
    y = jnp.where(y == 0, 0, jnp.where(y == ny - 1, 1, y + 1))
    val[...] = jnp.where(r_all < 0, -1, y * nx + r_all // ny).astype(f32)
    tall, depth = 512, 16

    def deposit(m):
        first = m * float(tall)

        def inner(k, acc):
            pieces = []
            for h in range(depth):
                r = val[pl.ds(k * depth + h, 1), :] - first
                parts = []
                for g in range(tall // 256):
                    q = r - 256.0 * g
                    parts.append(hot(jnp.where((q >= 0) & (q < 256), q, -1.0), iota))
                pieces.append(jnp.concatenate(parts, axis=0))
            where = pl.ds(pl.multiple_of(k * (depth * LANES), depth * LANES), depth * LANES)
            return acc + lax.dot_general(
                jnp.concatenate(pieces, axis=1), sp[:, where], NT, preferred_element_type=f32
            )

        acc = lax.fori_loop(0, count // depth, inner, jnp.zeros((tall, 2 * LANES), f32))
        return acc[:, :LANES] + acc[:, LANES:]

    planes = tall // nx
    got = deposit(0.0)
    for n, y in enumerate((0, ny - 1) + tuple(range(1, planes - 1))):
        src[pl.ds(y, nx, stride=ny), :] = got[n * nx : (n + 1) * nx]

    for copy in early:
        copy.wait()

    final = crosses - 1
    low_edge, high_edge = s == 0, s == final
    sub = lax.broadcasted_iota(i32, (ny, LANES), 0)
    lane = lax.broadcasted_iota(i32, (ny, LANES), 1)

    def edge(cref, tref):
        cref[0:ny, :] = hx[1, 0] * conduct(tref[0:ny, :])
        cref[rows + ny : rows + 2 * ny, :] = hx[1, 1] * conduct(tref[rows + ny : rows + 2 * ny, :])

    def rim(tlo, thi, tref, cref):
        for n, (off, plane, k, at) in enumerate(((low_edge, tlo, hy[1, 0], ny), (high_edge, thi, hy[1, 1], 2 * ny - 1))):
            t = jnp.where(off, 0.0, plane)
            cc = jnp.where(off, 0.0, k) * conduct(t)
            t0 = tref[pl.ds(at, nx, stride=ny), :]
            c0 = cref[pl.ds(at, nx, stride=ny), :]
            flux[n] = (cc + c0) * ((t0 - t) if n == 0 else (t - t0))

    def step(tin, cin, emit):
        many = 16

        def body(b, before):
            for u in range(many):
                x = b * many + u
                here = pl.ds(pl.multiple_of(x * ny + ny, ny), ny)
                ahead = pl.ds(pl.multiple_of(x * ny + 2 * ny, ny), ny)
                t0, c0 = tin[here, :], cin[here, :]
                t1, c1 = tin[ahead, :], cin[ahead, :]
                fx = (c0 + c1) * (t1 - t0)
                at = pl.ds(x, 1)
                ahead_t, ahead_c = pltpu.roll(t0, ny - 1, 0), pltpu.roll(c0, ny - 1, 0)
                fy = jnp.where(sub == ny - 1, flux[1, at, :], (c0 + ahead_c) * (ahead_t - t0))
                fy0 = jnp.where(sub == 0, flux[0, at, :], pltpu.roll(fy, 1, 0))
                ct = c0 * t0
                tz, cz = pltpu.roll(t0, LANES - 1, 1), pltpu.roll(c0, LANES - 1, 1)
                fz = jnp.where(lane == LANES - 1, -ct, (c0 + cz) * (tz - t0))
                fz0 = jnp.where(lane == 0, ct, pltpu.roll(fz, 1, 1))
                emit(x, t0 + 0.5 * (((fx - before) + (fy - fy0)) + (fz - fz0)))
                before = fx
            return before

        t0, c0 = tin[ny : 2 * ny, :], cin[ny : 2 * ny, :]
        tm, cm = tin[0:ny, :], cin[0:ny, :]
        lax.fori_loop(0, nx // many, body, (cm + c0) * (t0 - tm))

    def send_x(k, tref):
        copies = [
            remote(tref.at[pl.ds(rows, ny)], tref.at[pl.ds(0, ny)], xs.at[2 * k], xr.at[2 * k], (above, s)),
            remote(
                tref.at[pl.ds(ny, ny)], tref.at[pl.ds(rows + ny, ny)], xs.at[2 * k + 1], xr.at[2 * k + 1], (below, s)
            ),
        ]
        for copy in copies:
            copy.start()
        return copies

    def send_y(k):
        copies = [
            remote(ysend.at[k, 1], stage.at[k, 0], ys.at[2 * k], yr.at[2 * k], (c, right)),
            remote(ysend.at[k, 0], stage.at[k, 1], ys.at[2 * k + 1], yr.at[2 * k + 1], (c, left)),
        ]
        for copy in copies:
            copy.start()
        return copies

    ta[0:ny, :] = hx[0, 0]
    ta[rows + ny : rows + 2 * ny, :] = hx[0, 1]
    edge(ca, ta)
    rim(hy[0, 0], hy[0, 1], ta, ca)

    def emit_first(x, t):
        d1[pl.ds(pl.multiple_of(x * ny, ny), ny), :] = t

    step(ta, ca, emit_first)
    for n, y in enumerate((0, ny - 1)):
        ysend[0, n] = d1[pl.ds(y, nx, stride=ny), :] + src[pl.ds(y, nx, stride=ny), :]
    first = send_y(0)

    def others(m, carry):
        got = deposit(m.astype(f32))
        for n in range(planes):
            src[pl.ds(m * planes + (n - 1), nx, stride=ny), :] = got[n * nx : (n + 1) * nx]
        return carry

    lax.fori_loop(1, rows // tall, others, 0)

    def finish(b, carry):
        where = pl.ds(pl.multiple_of(b * block, block), block)
        there = pl.ds(pl.multiple_of(b * block + ny, ny), block)
        t = d1[where, :] + src[where, :]
        tb[there, :] = t
        cb[there, :] = kappa[where, :] * conduct(t)
        return carry

    lax.fori_loop(0, rows // block, finish, 0)
    first += send_x(0, tb)

    extra_rows = [(hi_rows + side * gcount + g, side, g) for side in range(2) for g in range(gcount)]
    for k in range(0, bond_rows, 8):
        q = other[k : k + 8, :]
        h, l = q // LANES, q % LANES
        for ch in range(3):
            d = pq[ch, k : k + 8, :]
            g = table_pick([(n, ghosts[side, ch * gcount + i : ch * gcount + i + 1, :]) for n, side, i in extra_rows], h, l, zero8)
            pq[ch, k : k + 8, :] = d + g
    d = [pq[ch] for ch in range(3)]
    dist = jnp.sqrt(d[0] * d[0] + d[1] * d[1] + d[2] * d[2])
    g = gap[...]
    base = (1.0 - snapped[...].astype(f32)) / jnp.maximum(dist, 0.3)
    p = base * (dist - g)
    q = base * (-0.1 * g)
    for ch in range(3):
        pq[ch] = p * d[ch]
        pq[3 + ch] = q * d[ch]
    iota32 = iota[:hi_rows]

    def scatter(values):
        def body(k, acc):
            lhs = []
            for u in range(depth):
                r = k * depth + u
                h = (acted[pl.ds(r, 1), :] // LANES).astype(f32)
                tops, bottoms = [], []
                for v in values(r):
                    top = high(v)
                    tops.append(spread(h, top, iota32))
                    bottoms.append(spread(h, v - top, iota32))
                lhs.append(jnp.concatenate(tops + bottoms, axis=0))
            where = pl.ds(pl.multiple_of(k * (depth * LANES), depth * LANES), depth * LANES)
            return acc + lax.dot_general(
                jnp.concatenate(lhs, axis=1), ohl[:, where], NT, preferred_element_type=f32
            )

        n = 3 * hi_rows
        acc = lax.fori_loop(0, bond_rows // depth, body, jnp.zeros((2 * n, LANES), f32))
        return acc[:n] + acc[n:]

    def rows_of(lo):
        return lambda r: [pq[lo + ch, pl.ds(r, 1), :] for ch in range(3)]

    own[0] = scatter(rows_of(0))

    for copy in first:
        copy.wait()
    edge(cb, tb)
    rim(stage[0, 0], stage[0, 1], tb, cb)

    def emit_second(x, t):
        where = pl.ds(pl.multiple_of(x * ny, ny), ny)
        here = pl.ds(pl.multiple_of(x * ny + ny, ny), ny)
        t = t + src[where, :]
        ta[here, :] = t
        ca[here, :] = kappa[where, :] * conduct(t)

    step(tb, cb, emit_second)
    for n, y in enumerate((ny, 2 * ny - 1)):
        ysend[1, n] = ta[pl.ds(y, nx, stride=ny), :]
    second = send_y(1) + send_x(1, ta)
    own[1] = scatter(rows_of(3))
    for copy in second:
        copy.wait()
    edge(ca, ta)
    rim(stage[1, 0], stage[1, 1], ta, ca)

    def emit_third(x, t):
        where = pl.ds(pl.multiple_of(x * ny, ny), ny)
        temp_out[where, :] = t + src[where, :]

    step(ta, ca, emit_third)

    for k in range(rows // LANES):
        b = temp_out[k * LANES : (k + 1) * LANES, :].T
        hi = b.astype(bf16)
        tt[0:LANES, k * LANES : (k + 1) * LANES] = hi
        tt[LANES : 2 * LANES, k * LANES : (k + 1) * LANES] = (b - hi.astype(f32)).astype(bf16)
    zs = lax.broadcasted_iota(i32, (LANES, LANES), 0).astype(f32)

    def look(slots):
        cols = []
        for n in slots:
            for h in range(per):
                r = row[pl.ds(n * per + h, 1), :]
                parts = []
                for k in range(rows // 256):
                    q = r - 256.0 * k
                    parts.append(hot(jnp.where((q >= 0) & (q < 256), q, -1.0), iota))
                cols.append(jnp.concatenate(parts, axis=0))
        got = jnp.dot(tt[...], jnp.concatenate(cols, axis=1), preferred_element_type=f32)
        got = got[:LANES] + got[LANES:]
        for i, n in enumerate(slots):
            for h in range(per):
                u = i * per + h
                z = zed[pl.ds(n * per + h, 1), :]
                v = jnp.where(zs == z, got[:, u * LANES : (u + 1) * LANES], 0.0)
                picked[n, h : h + 1, :] = jnp.sum(v, axis=0, keepdims=True)

    def look_far(k, carry):
        j = lax.rem(s + k, crosses)
        look((crosses + j, j))
        remote(picked.at[crosses + j], back.at[crosses + s], bs.at[crosses + j], br.at[crosses + s], (below, j)).start()
        remote(picked.at[j], back.at[s], bs.at[j], br.at[s], (c, j)).start()
        return carry

    lax.fori_loop(1, crosses, look_far, 0)
    look((crosses + s, s))
    remote(picked.at[crosses + s], back.at[crosses + s], bs.at[crosses + s], br.at[crosses + s], (below, s)).start()
    back[pl.ds(s, 1)] = picked[pl.ds(s, 1)]

    def back_same(k, carry):
        j = lax.rem(s + k, crosses)
        remote(picked.at[j], back.at[j], bs.at[j], br.at[j], (c, j)).wait()
        return carry

    def back_far(j, carry):
        n = crosses + j
        remote(picked.at[n], back.at[n], bs.at[n], br.at[n], (below, j)).wait()
        return carry

    lax.fori_loop(1, crosses, back_same, 0)
    lax.fori_loop(0, crosses, back_far, 0)
    warm = jnp.where(
        loc[...] >= cells,
        jnp.concatenate([back[crosses + j] for j in range(crosses)], axis=0),
        jnp.concatenate([back[j] for j in range(crosses)], axis=0),
    )
    table = [(r, warm[r : r + 1]) for r in range(hi_rows)]
    gtemp_send[...] = table_pick(table, eh, el, zero8)[:gcount]
    copies = [
        remote(gtemp_send, gtemp.at[0], gs.at[0], gr.at[0], (above, s)),
        remote(gtemp_send, gtemp.at[1], gs.at[1], gr.at[1], (below, s)),
    ]
    for copy in copies:
        copy.start()
    partner = []
    for k in range(0, bond_rows, 8):
        q = other[k : k + 8, :]
        partner.append(table_pick(table, q // LANES, q % LANES, zero8))
    for copy in copies:
        copy.wait()
    for n, k in enumerate(range(0, bond_rows, 8)):
        q = other[k : k + 8, :]
        t = table_pick(
            [(m, gtemp[side, i : i + 1, :]) for m, side, i in extra_rows], q // LANES, q % LANES, partner[n]
        )
        for ch in range(3):
            pq[3 + ch, k : k + 8, :] = pq[3 + ch, k : k + 8, :] * t
    force = own[0] + scatter(rows_of(3)) + jnp.concatenate([warm] * 3, axis=0) * own[1]
    for ch in range(3):
        for r in range(hi_rows):
            where = slice(r * LANES, (r + 1) * LANES)
            v = vel[ch : ch + 1, where] + 0.5 * force[ch * hi_rows + r : ch * hi_rows + r + 1]
            vel_out[ch : ch + 1, where] = v
            pos_out[ch : ch + 1, where] = pos[ch : ch + 1, where] + 0.5 * v


def per_device(
    cuts, crosses, temp, kappa, locator, gain, mark, pos, vel, acted, other, gap, snapped, exported
):
    nx, ny, nz = temp.shape
    rows = nx * ny
    flat = lambda a: a.reshape(-1, LANES)
    loc, gain, mark = flat(locator), flat(gain), flat(mark)
    acted, other, gap, snapped, exported = map(flat, (acted, other, gap, snapped, exported))
    hi_rows = loc.shape[0]
    per = hi_rows // crosses
    gcount = exported.shape[0]
    bonds = acted.shape[0]
    lr = 2 * crosses * per
    shape = jax.ShapeDtypeStruct
    dma = pltpu.SemaphoreType.DMA
    vm = pltpu.VMEM
    plane = (2, 2, nx, nz)
    padded = (rows + 2 * ny, nz)
    temp_new, pos_new, vel_new = pl.pallas_call(
        functools.partial(kernel, cuts, crosses),
        out_shape=(shape((rows, nz), f32), shape(pos.shape, f32), shape(vel.shape, f32)),
        in_specs=[VMEM] * 12,
        out_specs=(VMEM,) * 3,
        scratch_shapes=[
            vm((2 * crosses, 2 * per, LANES), f32),
            vm((crosses, 2 * per, LANES), f32),
            vm((2, 2, ny, nz), f32),
            vm(plane, f32),
            vm(plane, f32),
            vm((2, 3 * gcount, LANES), f32),
            vm((3 * gcount, LANES), f32),
            vm((lr, LANES), f32),
            vm((lr, LANES), f32),
            vm((lr, LANES), f32),
            vm((2 * LANES, lr * LANES), bf16),
            vm((LANES, bonds * LANES), bf16),
            vm((256, LANES), bf16),
            vm((rows, nz), f32),
            vm((rows, nz), f32),
            vm(padded, f32),
            vm(padded, f32),
            vm(padded, f32),
            vm(padded, f32),
            vm(plane, f32),
            vm((2, nx, nz), f32),
            vm((2 * nz, rows), bf16),
            vm((2 * crosses, per, LANES), f32),
            vm((2 * crosses, per, LANES), f32),
            vm(plane, f32),
            vm((gcount, LANES), f32),
            vm((2, gcount, LANES), f32),
            vm((6, bonds, LANES), f32),
            vm((2, 3 * hi_rows, LANES), f32),
            dma((2 * crosses,)),
            dma((2 * crosses,)),
            dma((10,)),
            dma((10,)),
            dma((4,)),
            dma((4,)),
            dma((4,)),
            dma((4,)),
            dma((2 * crosses,)),
            dma((2 * crosses,)),
            dma((2,)),
            dma((2,)),
        ],
        compiler_params=pltpu.CompilerParams(collective_id=0, has_side_effects=True),
        name="substeps",
    )(loc, gain, mark, temp.reshape(rows, nz), kappa.reshape(rows, nz), pos, vel, acted, other, gap, snapped, exported)
    return temp_new.reshape(nx, ny, nz), pos_new, vel_new


def solution(mesh):
    both = P(("cut", "cross"))
    return jax.shard_map(
        functools.partial(per_device, mesh.shape["cut"], mesh.shape["cross"]),
        mesh=mesh,
        in_specs=(P("cut", "cross", None),) * 2
        + (both,) * 3
        + (P(None, ("cut", "cross")),) * 2
        + (both,) * 5,
        out_specs=(P("cut", "cross", None), P(None, ("cut", "cross")), P(None, ("cut", "cross"))),
        check_vma=False,
    )
```

```python
import functools

import jax
import jax.numpy as jnp
from jax import lax
from jax.experimental import pallas as pl
from jax.experimental.pallas import tpu as pltpu
from jax.sharding import PartitionSpec as P

f32 = jnp.float32
bf16 = jnp.bfloat16
i32 = jnp.int32
MESH = pl.DeviceIdType.MESH
NT = (((1,), (1,)), ((), ()))
LANES = 128
VMEM = pl.BlockSpec(memory_space=pltpu.VMEM)
ANY = pl.BlockSpec(memory_space=pl.ANY)


def stack(tile, count):
    return jnp.concatenate([tile] * count, axis=0)


def rows16(row):
    return jnp.broadcast_to(row, (16, row.shape[1])).astype(bf16)


def hot(row, iota):
    r = stack(rows16(row), iota.shape[0] // 16)
    return jnp.where(iota == r, jnp.ones_like(iota), jnp.zeros_like(iota))


def spread(row, val, iota):
    r = stack(rows16(row), iota.shape[0] // 16)
    v = stack(rows16(val), iota.shape[0] // 16)
    return jnp.where(iota == r, v, jnp.zeros_like(iota))


def iota_rows(count):
    return lax.broadcasted_iota(i32, (count, LANES), 0).astype(f32).astype(bf16)


def high(v):
    return v.astype(bf16).astype(f32)


def conduct(t):
    return 0.5 + 1.0 / (1.0 + t * t)


def peers(cuts, crosses):
    c, s = lax.axis_index("cut"), lax.axis_index("cross")
    below, above = lax.rem(c + cuts - 1, cuts), lax.rem(c + 1, cuts)
    return c, s, below, above


def greet(cuts, crosses):
    c, s, below, above = peers(cuts, crosses)
    barrier = pltpu.get_barrier_semaphore()

    for device in ((below, s), (above, s)):
        pl.semaphore_signal(barrier, inc=1, device_id=device, device_id_type=MESH)

    def other(k, carry):
        j = lax.rem(s + k, crosses)
        pl.semaphore_signal(barrier, inc=1, device_id=(c, j), device_id_type=MESH)
        return carry

    lax.fori_loop(1, crosses, other, 0)


def await_all(crosses):
    pl.semaphore_wait(pltpu.get_barrier_semaphore(), crosses + 1)


def remote(src, dst, send, recv, device):
    return pltpu.make_async_remote_copy(
        src_ref=src, dst_ref=dst, send_sem=send, recv_sem=recv, device_id=device, device_id_type=MESH
    )


def lane_pick(row, index):
    return jnp.take_along_axis(row, index, axis=1, mode="promise_in_bounds")


def table_pick(rows, high_index, low_index, start):
    out = start
    for number, row in rows:
        wide = jnp.broadcast_to(row, low_index.shape)
        out = jnp.where(high_index == number, lane_pick(wide, low_index), out)
    return out


def kernel(
    cuts, crosses, loc, gain, mark, temp_hbm, kappa_hbm, pos, acted, other, gap, snapped, exported,
    temp_hbm_out, force_out,
    temp, kappa, temp_out, lists, send_lists, hx, hy, ysend0, ghosts, gsend,
    row, zed, val, sp, ohl, big, d1, src, ta, tb, ca, cb, ysend, flux, tt, picked, far, ret, back, stage,
    gtemp_send, gtemp, pq, own,
    send_sem, recv_sem, hsend, hrecv, xs, xr, ys, yr, bs, br, gs, gr, local,
):
    c, s, below, above = peers(cuts, crosses)
    left, right = lax.rem(s + crosses - 1, crosses), lax.rem(s + 1, crosses)
    loads = [
        pltpu.make_async_copy(temp_hbm, temp, local.at[0]),
        pltpu.make_async_copy(kappa_hbm, kappa, local.at[1]),
    ]
    for load in loads:
        load.start()
    greet(cuts, crosses)
    rows = temp.shape[0]
    nx = hy.shape[2]
    ny = rows // nx
    cells = rows * LANES
    hi_rows = loc.shape[0]
    per = hi_rows // crosses
    gcount = exported.shape[0]
    bond_rows = acted.shape[0]

    w = loc[...].astype(f32)
    power = mark[...].astype(f32) * gain[...] * 0.5
    for j in range(crosses):
        send_lists[j, 0:per, :] = w[j * per : (j + 1) * per]
        send_lists[j, per : 2 * per, :] = power[j * per : (j + 1) * per]
    e8 = jnp.concatenate([exported[...]] * (8 // gcount), axis=0)
    eh, el = e8 // LANES, e8 % LANES
    zero8 = jnp.zeros((8, LANES), f32)

    def row_of(ref, ch, r):
        return ref[ch : ch + 1, pl.ds(pl.multiple_of(r * LANES, LANES), LANES)]

    def export_rows(r, acc):
        return tuple(table_pick([(r, row_of(pos, ch, r))], eh, el, acc[ch]) for ch in range(3))

    acc = lax.fori_loop(0, hi_rows, export_rows, (zero8,) * 3, unroll=8)
    for ch in range(3):
        gsend[ch * gcount : (ch + 1) * gcount, :] = acc[ch][:gcount]

    for load in loads:
        load.wait()
    for a, ref in enumerate((temp, kappa)):
        ysend0[a, 0] = ref[pl.ds(0, nx, stride=ny), :]
        ysend0[a, 1] = ref[pl.ds(ny - 1, nx, stride=ny), :]

    group = 16

    def differences(k, carry):
        where = pl.ds(pl.multiple_of(k * group, group), group)
        qa, qb = acted[where, :], other[where, :]
        index = [(q[h : h + 8] // LANES, q[h : h + 8] % LANES) for q in (qa, qb) for h in range(0, group, 8)]

        def one(r, acc):
            out = []
            for ch in range(3):
                wide = jnp.broadcast_to(row_of(pos, ch, r), (8, LANES))
                for n, (h, l) in enumerate(index):
                    out.append(jnp.where(h == r, lane_pick(wide, l), acc[ch * len(index) + n]))
            return tuple(out)

        acc = lax.fori_loop(0, hi_rows, one, (zero8,) * (3 * len(index)), unroll=4)
        half = len(index) // 2
        for ch in range(3):
            for n in range(half):
                first, second = acc[ch * len(index) + n], acc[ch * len(index) + half + n]
                pq[ch, pl.ds(pl.multiple_of(k * group + 8 * n, 8), 8), :] = second - first
        return carry

    await_all(crosses)

    def send_same(k, carry):
        j = lax.rem(s + k, crosses)
        remote(send_lists.at[j], lists.at[s], send_sem.at[j], recv_sem.at[s], (c, j)).start()
        return carry

    lax.fori_loop(1, crosses, send_same, 0)
    lists[pl.ds(s, 1)] = send_lists[pl.ds(s, 1)]
    early = []
    for a, ref in enumerate((temp, kappa)):
        early.append(remote(ysend0.at[a, 1], hy.at[a, 0], hsend.at[4 * a + 2], hrecv.at[4 * a + 2], (c, right)))
        early.append(remote(ysend0.at[a, 0], hy.at[a, 1], hsend.at[4 * a + 3], hrecv.at[4 * a + 3], (c, left)))
        early.append(remote(ref.at[pl.ds(rows - ny, ny)], hx.at[a, 0], hsend.at[4 * a], hrecv.at[4 * a], (above, s)))
        early.append(remote(ref.at[pl.ds(0, ny)], hx.at[a, 1], hsend.at[4 * a + 1], hrecv.at[4 * a + 1], (below, s)))
    early.append(remote(gsend, ghosts.at[0], hsend.at[8], hrecv.at[8], (above, s)))
    early.append(remote(gsend, ghosts.at[1], hsend.at[9], hrecv.at[9], (below, s)))
    for copy in early:
        copy.start()

    block = 16 * ny

    def begin(b, carry):
        where = pl.ds(pl.multiple_of(b * block, block), block)
        there = pl.ds(pl.multiple_of(b * block + ny, ny), block)
        t = temp[where, :]
        ta[there, :] = t
        ca[there, :] = kappa[where, :] * conduct(t)
        return carry

    lax.fori_loop(0, rows // block, begin, 0)
    big[...] = iota_rows(256)
    iota = big[...]
    small = iota[:LANES]

    def lows(k, carry):
        for u in range(4):
            r = k * 4 + u
            a = (acted[pl.ds(r, 1), :] % LANES).astype(f32)
            ohl[:, pl.ds(pl.multiple_of(r * LANES, LANES), LANES)] = hot(a, small)
        return carry

    lax.fori_loop(0, bond_rows // 4, lows, 0)

    def take_same(k, carry):
        j = lax.rem(s + k, crosses)
        remote(send_lists.at[j], lists.at[j], send_sem.at[j], recv_sem.at[j], (c, j)).wait()
        return carry

    lax.fori_loop(1, crosses, take_same, 0)
    relay = remote(
        lists.at[pl.ds(0, crosses)], lists.at[pl.ds(crosses, crosses)], hsend.at[10], hrecv.at[10], (above, s)
    )
    relay.start()

    count = row.shape[0]

    def build(k, carry):
        for u in range(4):
            r = k * 4 + u
            z = zed[pl.ds(r, 1), :]
            v = val[pl.ds(r, 1), :]
            hi = high(v)
            where = pl.ds(pl.multiple_of(r * LANES, LANES), LANES)
            sp[0:LANES, where] = spread(z, hi, small)
            sp[LANES : 2 * LANES, where] = spread(z, v - hi, small)
        return carry

    def decode(half):
        for b in range(half * crosses, (half + 1) * crosses):
            q = lists[b, 0:per, :].astype(i32)
            here = (q >= cells) == (half == 1)
            q = q & (cells - 1)
            row[b * per : (b + 1) * per, :] = jnp.where(here, q // LANES, -1).astype(f32)
            zed[b * per : (b + 1) * per, :] = (q % LANES).astype(f32)
            val[b * per : (b + 1) * per, :] = jnp.where(here, lists[b, per : 2 * per, :], 0.0)
        lax.fori_loop(half * count // 8, (half + 1) * count // 8, build, 0)
        where = slice(half * count // 2, (half + 1) * count // 2)
        r_all = row[where, :].astype(i32)
        y = r_all & (ny - 1)
        y = jnp.where(y == 0, 0, jnp.where(y == ny - 1, 1, y + 1))
        val[where, :] = jnp.where(r_all < 0, -1, y * nx + r_all // ny).astype(f32)

    tall, depth = 512, 16

    def deposit(m, begin, end, acc):
        first = m * float(tall)

        def inner(k, acc):
            pieces = []
            for h in range(depth):
                r = val[pl.ds(k * depth + h, 1), :] - first
                parts = []
                for g in range(tall // 256):
                    q = r - 256.0 * g
                    parts.append(hot(jnp.where((q >= 0) & (q < 256), q, -1.0), iota))
                pieces.append(jnp.concatenate(parts, axis=0))
            where = pl.ds(pl.multiple_of(k * (depth * LANES), depth * LANES), depth * LANES)
            return acc + lax.dot_general(
                jnp.concatenate(pieces, axis=1), sp[:, where], NT, preferred_element_type=f32
            )

        return lax.fori_loop(begin, end, inner, acc)

    planes = tall // nx
    nothing = jnp.zeros((tall, 2 * LANES), f32)
    steps = count // depth
    decode(0)
    got = deposit(0.0, 0, steps // 2, nothing)
    relay.wait()
    decode(1)
    got = deposit(0.0, steps // 2, steps, got)
    got = got[:, :LANES] + got[:, LANES:]
    for n, y in enumerate((0, ny - 1) + tuple(range(1, planes - 1))):
        src[pl.ds(y, nx, stride=ny), :] = got[n * nx : (n + 1) * nx]

    for copy in early:
        copy.wait()

    final = crosses - 1
    low_edge, high_edge = s == 0, s == final
    sub = lax.broadcasted_iota(i32, (ny, LANES), 0)
    lane = lax.broadcasted_iota(i32, (ny, LANES), 1)

    def edge(cref, tref):
        cref[0:ny, :] = hx[1, 0] * conduct(tref[0:ny, :])
        cref[rows + ny : rows + 2 * ny, :] = hx[1, 1] * conduct(tref[rows + ny : rows + 2 * ny, :])

    def rim(tlo, thi, tref, cref):
        for n, (off, plane, k, at) in enumerate(((low_edge, tlo, hy[1, 0], ny), (high_edge, thi, hy[1, 1], 2 * ny - 1))):
            t = jnp.where(off, 0.0, plane)
            cc = jnp.where(off, 0.0, k) * conduct(t)
            t0 = tref[pl.ds(at, nx, stride=ny), :]
            c0 = cref[pl.ds(at, nx, stride=ny), :]
            flux[n] = (cc + c0) * ((t0 - t) if n == 0 else (t - t0))

    def step(tin, cin, emit):
        many = 16

        def body(b, before):
            for u in range(many):
                x = b * many + u
                here = pl.ds(pl.multiple_of(x * ny + ny, ny), ny)
                ahead = pl.ds(pl.multiple_of(x * ny + 2 * ny, ny), ny)
                t0, c0 = tin[here, :], cin[here, :]
                t1, c1 = tin[ahead, :], cin[ahead, :]
                fx = (c0 + c1) * (t1 - t0)
                at = pl.ds(x, 1)
                ahead_t, ahead_c = pltpu.roll(t0, ny - 1, 0), pltpu.roll(c0, ny - 1, 0)
                fy = jnp.where(sub == ny - 1, flux[1, at, :], (c0 + ahead_c) * (ahead_t - t0))
                fy0 = jnp.where(sub == 0, flux[0, at, :], pltpu.roll(fy, 1, 0))
                ct = c0 * t0
                tz, cz = pltpu.roll(t0, LANES - 1, 1), pltpu.roll(c0, LANES - 1, 1)
                fz = jnp.where(lane == LANES - 1, -ct, (c0 + cz) * (tz - t0))
                fz0 = jnp.where(lane == 0, ct, pltpu.roll(fz, 1, 1))
                emit(x, t0 + 0.5 * (((fx - before) + (fy - fy0)) + (fz - fz0)))
                before = fx
            return before

        t0, c0 = tin[ny : 2 * ny, :], cin[ny : 2 * ny, :]
        tm, cm = tin[0:ny, :], cin[0:ny, :]
        lax.fori_loop(0, nx // many, body, (cm + c0) * (t0 - tm))

    def send_x(k, tref):
        copies = [
            remote(tref.at[pl.ds(rows, ny)], tref.at[pl.ds(0, ny)], xs.at[2 * k], xr.at[2 * k], (above, s)),
            remote(
                tref.at[pl.ds(ny, ny)], tref.at[pl.ds(rows + ny, ny)], xs.at[2 * k + 1], xr.at[2 * k + 1], (below, s)
            ),
        ]
        for copy in copies:
            copy.start()
        return copies

    def send_y(k):
        copies = [
            remote(ysend.at[k, 1], stage.at[k, 0], ys.at[2 * k], yr.at[2 * k], (c, right)),
            remote(ysend.at[k, 0], stage.at[k, 1], ys.at[2 * k + 1], yr.at[2 * k + 1], (c, left)),
        ]
        for copy in copies:
            copy.start()
        return copies

    ta[0:ny, :] = hx[0, 0]
    ta[rows + ny : rows + 2 * ny, :] = hx[0, 1]
    edge(ca, ta)
    rim(hy[0, 0], hy[0, 1], ta, ca)

    def emit_first(x, t):
        d1[pl.ds(pl.multiple_of(x * ny, ny), ny), :] = t

    step(ta, ca, emit_first)
    for n, y in enumerate((0, ny - 1)):
        ysend[0, n] = d1[pl.ds(y, nx, stride=ny), :] + src[pl.ds(y, nx, stride=ny), :]
    first = send_y(0)

    def others(m, carry):
        got = deposit(m.astype(f32), 0, steps, nothing)
        got = got[:, :LANES] + got[:, LANES:]
        for n in range(planes):
            src[pl.ds(m * planes + (n - 1), nx, stride=ny), :] = got[n * nx : (n + 1) * nx]
        return carry

    lax.fori_loop(1, rows // tall, others, 0)

    def finish(b, carry):
        where = pl.ds(pl.multiple_of(b * block, block), block)
        there = pl.ds(pl.multiple_of(b * block + ny, ny), block)
        t = d1[where, :] + src[where, :]
        tb[there, :] = t
        cb[there, :] = kappa[where, :] * conduct(t)
        return carry

    lax.fori_loop(0, rows // block, finish, 0)
    first += send_x(0, tb)

    lax.fori_loop(0, bond_rows // group // 2, differences, 0)
    iota32 = iota[:hi_rows]

    def scatter(values):
        def body(k, acc):
            lhs = []
            for u in range(depth):
                r = k * depth + u
                h = (acted[pl.ds(r, 1), :] // LANES).astype(f32)
                tops, bottoms = [], []
                for v in values(r):
                    top = high(v)
                    tops.append(spread(h, top, iota32))
                    bottoms.append(spread(h, v - top, iota32))
                lhs.append(jnp.concatenate(tops + bottoms, axis=0))
            where = pl.ds(pl.multiple_of(k * (depth * LANES), depth * LANES), depth * LANES)
            return acc + lax.dot_general(
                jnp.concatenate(lhs, axis=1), ohl[:, where], NT, preferred_element_type=f32
            )

        n = 3 * hi_rows
        acc = lax.fori_loop(0, bond_rows // depth, body, jnp.zeros((2 * n, LANES), f32))
        return acc[:n] + acc[n:]

    def rows_of(lo):
        return lambda r: [pq[lo + ch, pl.ds(r, 1), :] for ch in range(3)]

    for copy in first:
        copy.wait()
    edge(cb, tb)
    rim(stage[0, 0], stage[0, 1], tb, cb)

    def emit_second(x, t):
        where = pl.ds(pl.multiple_of(x * ny, ny), ny)
        here = pl.ds(pl.multiple_of(x * ny + ny, ny), ny)
        t = t + src[where, :]
        ta[here, :] = t
        ca[here, :] = kappa[where, :] * conduct(t)

    step(tb, cb, emit_second)
    for n, y in enumerate((ny, 2 * ny - 1)):
        ysend[1, n] = ta[pl.ds(y, nx, stride=ny), :]
    second = send_y(1) + send_x(1, ta)
    lax.fori_loop(bond_rows // group // 2, bond_rows // group, differences, 0)
    extra_rows = [(hi_rows + side * gcount + g, side, g) for side in range(2) for g in range(gcount)]
    for k in range(0, bond_rows, 8):
        q = other[k : k + 8, :]
        h, l = q // LANES, q % LANES
        for ch in range(3):
            d = pq[ch, k : k + 8, :]
            g = table_pick([(n, ghosts[side, ch * gcount + i : ch * gcount + i + 1, :]) for n, side, i in extra_rows], h, l, zero8)
            pq[ch, k : k + 8, :] = d + g
    d = [pq[ch] for ch in range(3)]
    dist = jnp.sqrt(d[0] * d[0] + d[1] * d[1] + d[2] * d[2])
    g = gap[...]
    base = (1.0 - snapped[...].astype(f32)) / jnp.maximum(dist, 0.3)
    p = base * (dist - g)
    q = base * (-0.1 * g)
    for ch in range(3):
        pq[ch] = p * d[ch]
        pq[3 + ch] = q * d[ch]
    for copy in second:
        copy.wait()
    edge(ca, ta)
    rim(stage[1, 0], stage[1, 1], ta, ca)

    def emit_third(x, t):
        where = pl.ds(pl.multiple_of(x * ny, ny), ny)
        temp_out[where, :] = t + src[where, :]

    step(ta, ca, emit_third)
    store = pltpu.make_async_copy(temp_out, temp_hbm_out, local.at[2])
    store.start()

    for k in range(rows // LANES):
        b = temp_out[k * LANES : (k + 1) * LANES, :].T
        hi = b.astype(bf16)
        tt[0:LANES, k * LANES : (k + 1) * LANES] = hi
        tt[LANES : 2 * LANES, k * LANES : (k + 1) * LANES] = (b - hi.astype(f32)).astype(bf16)
    zs = lax.broadcasted_iota(i32, (LANES, LANES), 0).astype(f32)

    def look(slots):
        cols = []
        for n in slots:
            for h in range(per):
                r = row[pl.ds(n * per + h, 1), :]
                parts = []
                for k in range(rows // 256):
                    q = r - 256.0 * k
                    parts.append(hot(jnp.where((q >= 0) & (q < 256), q, -1.0), iota))
                cols.append(jnp.concatenate(parts, axis=0))
        got = jnp.dot(tt[...], jnp.concatenate(cols, axis=1), preferred_element_type=f32)
        got = got[:LANES] + got[LANES:]
        for i, n in enumerate(slots):
            for h in range(per):
                u = i * per + h
                z = zed[pl.ds(n * per + h, 1), :]
                v = jnp.where(zs == z, got[:, u * LANES : (u + 1) * LANES], 0.0)
                picked[n, h : h + 1, :] = jnp.sum(v, axis=0, keepdims=True)

    def look_below(k, carry):
        look((crosses + 2 * k, crosses + 2 * k + 1))
        return carry

    lax.fori_loop(0, crosses // 2, look_below, 0)
    hand = remote(picked.at[pl.ds(crosses, crosses)], far, hsend.at[11], hrecv.at[11], (below, s))
    hand.start()

    def pair(k):
        return lax.rem(s + 2 * k + 1, crosses), lax.rem(s + 2 * k + 2, crosses)

    def merge(j):
        m = row[pl.ds(j * per, per), :] < 0
        return jnp.where(m, far[pl.ds(j, 1)].reshape(per, LANES), picked[pl.ds(j, 1)].reshape(per, LANES))

    def back_to(j):
        ret[pl.ds(j, 1)] = merge(j).reshape(1, per, LANES)
        remote(ret.at[j], back.at[s], bs.at[j], br.at[s], (c, j)).start()

    held = 3

    def look_first(k, carry):
        look(pair(k))
        return carry

    lax.fori_loop(0, held, look_first, 0)
    hand.wait()

    def send_held(i, carry):
        back_to(lax.rem(s + i, crosses))
        return carry

    lax.fori_loop(1, 2 * held + 1, send_held, 0)

    def look_then(k, carry):
        a, b = pair(k)
        look((a, b))
        back_to(a)
        back_to(b)
        return carry

    lax.fori_loop(held, crosses // 2 - 1, look_then, 0)
    a, b = pair(crosses // 2 - 1)
    look((a, b))
    back_to(a)
    back[pl.ds(s, 1)] = merge(s).reshape(1, per, LANES)
    own[0] = scatter(rows_of(0))
    own[1] = scatter(rows_of(3))

    def back_same(k, carry):
        j = lax.rem(s + k, crosses)
        remote(ret.at[j], back.at[j], bs.at[j], br.at[j], (c, j)).wait()
        return carry

    lax.fori_loop(1, crosses, back_same, 0)
    warm = jnp.concatenate([back[j] for j in range(crosses)], axis=0)
    table = [(r, warm[r : r + 1]) for r in range(hi_rows)]
    gtemp_send[...] = table_pick(table, eh, el, zero8)[:gcount]
    copies = [
        remote(gtemp_send, gtemp.at[0], gs.at[0], gr.at[0], (above, s)),
        remote(gtemp_send, gtemp.at[1], gs.at[1], gr.at[1], (below, s)),
    ]
    for copy in copies:
        copy.start()
    partner = []
    for k in range(0, bond_rows, 8):
        q = other[k : k + 8, :]
        partner.append(table_pick(table, q // LANES, q % LANES, zero8))
    for copy in copies:
        copy.wait()
    for n, k in enumerate(range(0, bond_rows, 8)):
        q = other[k : k + 8, :]
        t = table_pick(
            [(m, gtemp[side, i : i + 1, :]) for m, side, i in extra_rows], q // LANES, q % LANES, partner[n]
        )
        for ch in range(3):
            pq[3 + ch, k : k + 8, :] = pq[3 + ch, k : k + 8, :] * t
    force_out[...] = own[0] + scatter(rows_of(3)) + jnp.concatenate([warm] * 3, axis=0) * own[1]
    store.wait()


def update_kernel(temp, force, pos, vel, temp_out, pos_out, vel_out, held, sems):
    parts = held.shape[0]
    rows = held.shape[1]
    where = [pl.ds(n * rows, rows) for n in range(parts)]
    loads = [pltpu.make_async_copy(temp.at[w], held.at[n], sems.at[0, n]) for n, w in enumerate(where)]
    stores = [pltpu.make_async_copy(held.at[n], temp_out.at[w], sems.at[1, n]) for n, w in enumerate(where)]
    for load in loads:
        load.start()
    for load, store in zip(loads, stores):
        load.wait()
        store.start()
    for ch in range(3):
        hi_rows = pos.shape[1] // LANES
        for r in range(hi_rows):
            at = slice(r * LANES, (r + 1) * LANES)
            v = vel[ch : ch + 1, at] + 0.5 * force[ch * hi_rows + r : ch * hi_rows + r + 1]
            vel_out[ch : ch + 1, at] = v
            pos_out[ch : ch + 1, at] = pos[ch : ch + 1, at] + 0.5 * v
    for store in stores:
        store.wait()


def per_device(
    cuts, crosses, temp, kappa, locator, gain, mark, pos, vel, acted, other, gap, snapped, exported
):
    nx, ny, nz = temp.shape
    rows = nx * ny
    flat = lambda a: a.reshape(-1, LANES)
    loc, gain, mark = flat(locator), flat(gain), flat(mark)
    acted, other, gap, snapped, exported = map(flat, (acted, other, gap, snapped, exported))
    hi_rows = loc.shape[0]
    per = hi_rows // crosses
    gcount = exported.shape[0]
    bonds = acted.shape[0]
    lr = 2 * crosses * per
    shape = jax.ShapeDtypeStruct
    dma = pltpu.SemaphoreType.DMA
    vm = pltpu.VMEM
    plane = (2, 2, nx, nz)
    padded = (rows + 2 * ny, nz)
    temp_new, force = pl.pallas_call(
        functools.partial(kernel, cuts, crosses),
        out_shape=(shape((rows, nz), f32), shape((3 * hi_rows, LANES), f32)),
        in_specs=[VMEM] * 3 + [ANY] * 2 + [VMEM] * 6,
        out_specs=(ANY, VMEM),
        scratch_shapes=[
            vm((rows, nz), f32),
            vm((rows, nz), f32),
            vm((rows, nz), f32),
            vm((2 * crosses, 2 * per, LANES), f32),
            vm((crosses, 2 * per, LANES), f32),
            vm((2, 2, ny, nz), f32),
            vm(plane, f32),
            vm(plane, f32),
            vm((2, 3 * gcount, LANES), f32),
            vm((3 * gcount, LANES), f32),
            vm((lr, LANES), f32),
            vm((lr, LANES), f32),
            vm((lr, LANES), f32),
            vm((2 * LANES, lr * LANES), bf16),
            vm((LANES, bonds * LANES), bf16),
            vm((256, LANES), bf16),
            vm((rows, nz), f32),
            vm((rows, nz), f32),
            vm(padded, f32),
            vm(padded, f32),
            vm(padded, f32),
            vm(padded, f32),
            vm(plane, f32),
            vm((2, nx, nz), f32),
            vm((2 * nz, rows), bf16),
            vm((2 * crosses, per, LANES), f32),
            vm((crosses, per, LANES), f32),
            vm((crosses, per, LANES), f32),
            vm((crosses, per, LANES), f32),
            vm(plane, f32),
            vm((gcount, LANES), f32),
            vm((2, gcount, LANES), f32),
            vm((6, bonds, LANES), f32),
            vm((2, 3 * hi_rows, LANES), f32),
            dma((crosses,)),
            dma((crosses,)),
            dma((12,)),
            dma((12,)),
            dma((4,)),
            dma((4,)),
            dma((4,)),
            dma((4,)),
            dma((crosses,)),
            dma((crosses,)),
            dma((2,)),
            dma((2,)),
            dma((3,)),
        ],
        compiler_params=pltpu.CompilerParams(collective_id=0, has_side_effects=True),
        name="substeps",
    )(loc, gain, mark, temp.reshape(rows, nz), kappa.reshape(rows, nz), pos, acted, other, gap, snapped, exported)
    temp_new, pos_new, vel_new = pl.pallas_call(
        update_kernel,
        out_shape=(shape((rows, nz), f32), shape(pos.shape, f32), shape(vel.shape, f32)),
        in_specs=[ANY] + [VMEM] * 3,
        out_specs=(ANY, VMEM, VMEM),
        scratch_shapes=[vm((4, rows // 4, nz), f32), dma((2, 4))],
        name="update",
    )(temp_new, force, pos, vel)
    return temp_new.reshape(nx, ny, nz), pos_new, vel_new


def solution(mesh):
    both = P(("cut", "cross"))
    return jax.shard_map(
        functools.partial(per_device, mesh.shape["cut"], mesh.shape["cross"]),
        mesh=mesh,
        in_specs=(P("cut", "cross", None),) * 2
        + (both,) * 3
        + (P(None, ("cut", "cross")),) * 2
        + (both,) * 5,
        out_specs=(P("cut", "cross", None), P(None, ("cut", "cross")), P(None, ("cut", "cross"))),
        check_vma=False,
    )
```

```python
import functools

import jax
import jax.numpy as jnp
from jax import lax
from jax.experimental import pallas as pl
from jax.experimental.pallas import tpu as pltpu
from jax.sharding import PartitionSpec as P

f32 = jnp.float32
bf16 = jnp.bfloat16
i32 = jnp.int32
MESH = pl.DeviceIdType.MESH
NT = (((1,), (1,)), ((), ()))
LANES = 128
VMEM = pl.BlockSpec(memory_space=pltpu.VMEM)
ANY = pl.BlockSpec(memory_space=pl.ANY)


def stack(tile, count):
    return jnp.concatenate([tile] * count, axis=0)


def rows16(row):
    return jnp.broadcast_to(row, (16, row.shape[1])).astype(bf16)


def hot(row, iota):
    r = stack(rows16(row), iota.shape[0] // 16)
    return jnp.where(iota == r, jnp.ones_like(iota), jnp.zeros_like(iota))


def spread(row, val, iota):
    r = stack(rows16(row), iota.shape[0] // 16)
    v = stack(rows16(val), iota.shape[0] // 16)
    return jnp.where(iota == r, v, jnp.zeros_like(iota))


def iota_rows(count):
    return lax.broadcasted_iota(i32, (count, LANES), 0).astype(f32).astype(bf16)


def high(v):
    return v.astype(bf16).astype(f32)


def conduct(t):
    return 0.5 + 1.0 / (1.0 + t * t)


def peers(cuts, crosses):
    c, s = lax.axis_index("cut"), lax.axis_index("cross")
    below, above = lax.rem(c + cuts - 1, cuts), lax.rem(c + 1, cuts)
    return c, s, below, above


def greet(cuts, crosses):
    c, s, below, above = peers(cuts, crosses)
    barrier = pltpu.get_barrier_semaphore()

    for device in ((below, s), (above, s)):
        pl.semaphore_signal(barrier, inc=1, device_id=device, device_id_type=MESH)

    def other(k, carry):
        j = lax.rem(s + k, crosses)
        pl.semaphore_signal(barrier, inc=1, device_id=(c, j), device_id_type=MESH)
        return carry

    lax.fori_loop(1, crosses, other, 0)


def await_all(crosses):
    pl.semaphore_wait(pltpu.get_barrier_semaphore(), crosses + 1)


def remote(src, dst, send, recv, device):
    return pltpu.make_async_remote_copy(
        src_ref=src, dst_ref=dst, send_sem=send, recv_sem=recv, device_id=device, device_id_type=MESH
    )


def lane_pick(row, index):
    return jnp.take_along_axis(row, index, axis=1, mode="promise_in_bounds")


def table_pick(rows, high_index, low_index, start):
    out = start
    for number, row in rows:
        wide = jnp.broadcast_to(row, low_index.shape)
        out = jnp.where(high_index == number, lane_pick(wide, low_index), out)
    return out


def kernel(
    cuts, crosses, *refs
):
    inputs, (temp_hbm_out, force_out) = refs[:11], refs[11:13]
    loc, gain, mark, exported, pos, temp, kappa, acted, other, gap, snapped = refs[13:24]
    (
    temp_out, lists, send_lists, hx, hy, ysend0, ghosts, gsend,
    row, zed, val, sp, ohl, big, d1, src, ta, tb, ca, cb, ysend, flux, tt, picked, far, ret, back, stage,
    gtemp_send, gtemp, pq, own,
    send_sem, recv_sem, hsend, hrecv, xs, xr, ys, yr, zs_sem, zr_sem, bs, br, gs, gr, local,
    ) = refs[24:]
    c, s, below, above = peers(cuts, crosses)
    left, right = lax.rem(s + crosses - 1, crosses), lax.rem(s + 1, crosses)
    loads = [pltpu.make_async_copy(a, b, local.at[n]) for n, (a, b) in enumerate(zip(inputs, refs[13:24]))]
    for load in loads:
        load.start()
    greet(cuts, crosses)
    rows = temp.shape[0]
    nx = hy.shape[2]
    ny = rows // nx
    cells = rows * LANES
    hi_rows = loc.shape[0]
    per = hi_rows // crosses
    gcount = exported.shape[0]
    bond_rows = acted.shape[0]

    for load in loads[:5]:
        load.wait()
    w = loc[...].astype(f32)
    power = mark[...].astype(f32) * gain[...] * 0.5
    for j in range(crosses):
        send_lists[j, 0:per, :] = w[j * per : (j + 1) * per]
        send_lists[j, per : 2 * per, :] = power[j * per : (j + 1) * per]
    e8 = jnp.concatenate([exported[...]] * (8 // gcount), axis=0)
    eh, el = e8 // LANES, e8 % LANES
    zero8 = jnp.zeros((8, LANES), f32)

    def row_of(ref, ch, r):
        return ref[ch : ch + 1, pl.ds(pl.multiple_of(r * LANES, LANES), LANES)]

    def export_rows(r, acc):
        return tuple(table_pick([(r, row_of(pos, ch, r))], eh, el, acc[ch]) for ch in range(3))

    acc = lax.fori_loop(0, hi_rows, export_rows, (zero8,) * 3, unroll=8)
    for ch in range(3):
        gsend[ch * gcount : (ch + 1) * gcount, :] = acc[ch][:gcount]

    for load in loads[5:]:
        load.wait()
    for a, ref in enumerate((temp, kappa)):
        ysend0[a, 0] = ref[pl.ds(0, nx, stride=ny), :]
        ysend0[a, 1] = ref[pl.ds(ny - 1, nx, stride=ny), :]

    group = 16

    def differences(k, carry):
        where = pl.ds(pl.multiple_of(k * group, group), group)
        qa, qb = acted[where, :], other[where, :]
        index = [(q[h : h + 8] // LANES, q[h : h + 8] % LANES) for q in (qa, qb) for h in range(0, group, 8)]

        def one(r, acc):
            out = []
            for ch in range(3):
                wide = jnp.broadcast_to(row_of(pos, ch, r), (8, LANES))
                for n, (h, l) in enumerate(index):
                    out.append(jnp.where(h == r, lane_pick(wide, l), acc[ch * len(index) + n]))
            return tuple(out)

        acc = lax.fori_loop(0, hi_rows, one, (zero8,) * (3 * len(index)), unroll=4)
        half = len(index) // 2
        for ch in range(3):
            for n in range(half):
                first, second = acc[ch * len(index) + n], acc[ch * len(index) + half + n]
                pq[ch, pl.ds(pl.multiple_of(k * group + 8 * n, 8), 8), :] = second - first
        return carry

    await_all(crosses)

    def send_same(k, carry):
        j = lax.rem(s + k, crosses)
        remote(send_lists.at[j], lists.at[s], send_sem.at[j], recv_sem.at[s], (c, j)).start()
        return carry

    lax.fori_loop(1, crosses, send_same, 0)
    lists[pl.ds(s, 1)] = send_lists[pl.ds(s, 1)]
    early = []
    for a, ref in enumerate((temp, kappa)):
        early.append(remote(ysend0.at[a, 1], hy.at[a, 0], hsend.at[4 * a + 2], hrecv.at[4 * a + 2], (c, right)))
        early.append(remote(ysend0.at[a, 0], hy.at[a, 1], hsend.at[4 * a + 3], hrecv.at[4 * a + 3], (c, left)))
        early.append(remote(ref.at[pl.ds(rows - ny, ny)], hx.at[a, 0], hsend.at[4 * a], hrecv.at[4 * a], (above, s)))
        early.append(remote(ref.at[pl.ds(0, ny)], hx.at[a, 1], hsend.at[4 * a + 1], hrecv.at[4 * a + 1], (below, s)))
    early.append(remote(gsend, ghosts.at[0], hsend.at[8], hrecv.at[8], (above, s)))
    early.append(remote(gsend, ghosts.at[1], hsend.at[9], hrecv.at[9], (below, s)))
    for copy in early:
        copy.start()

    block = 16 * ny

    def begin(b, carry):
        where = pl.ds(pl.multiple_of(b * block, block), block)
        there = pl.ds(pl.multiple_of(b * block + ny, ny), block)
        t = temp[where, :]
        ta[there, :] = t
        ca[there, :] = kappa[where, :] * conduct(t)
        return carry

    lax.fori_loop(0, rows // block, begin, 0)
    big[...] = iota_rows(256)
    iota = big[...]
    small = iota[:LANES]

    def lows(k, carry):
        for u in range(4):
            r = k * 4 + u
            a = (acted[pl.ds(r, 1), :] % LANES).astype(f32)
            ohl[:, pl.ds(pl.multiple_of(r * LANES, LANES), LANES)] = hot(a, small)
        return carry

    lax.fori_loop(0, bond_rows // 4, lows, 0)

    def take_same(k, carry):
        j = lax.rem(s + k, crosses)
        remote(send_lists.at[j], lists.at[j], send_sem.at[j], recv_sem.at[j], (c, j)).wait()
        return carry

    lax.fori_loop(1, crosses, take_same, 0)
    relay = remote(
        lists.at[pl.ds(0, crosses)], lists.at[pl.ds(crosses, crosses)], hsend.at[10], hrecv.at[10], (above, s)
    )
    relay.start()

    count = row.shape[0]

    def build(k, carry):
        for u in range(8):
            r = k * 8 + u
            z = zed[pl.ds(r, 1), :]
            v = val[pl.ds(r, 1), :]
            hi = high(v)
            where = pl.ds(pl.multiple_of(r * LANES, LANES), LANES)
            sp[0:LANES, where] = spread(z, hi, small)
            sp[LANES : 2 * LANES, where] = spread(z, v - hi, small)
        return carry

    def decode(half):
        for b in range(half * crosses, (half + 1) * crosses):
            q = lists[b, 0:per, :].astype(i32)
            here = (q >= cells) == (half == 1)
            q = q & (cells - 1)
            row[b * per : (b + 1) * per, :] = jnp.where(here, q // LANES, -1).astype(f32)
            zed[b * per : (b + 1) * per, :] = (q % LANES).astype(f32)
            val[b * per : (b + 1) * per, :] = jnp.where(here, lists[b, per : 2 * per, :], 0.0)
        lax.fori_loop(half * count // 16, (half + 1) * count // 16, build, 0)
        where = slice(half * count // 2, (half + 1) * count // 2)
        r_all = row[where, :].astype(i32)
        y = r_all & (ny - 1)
        y = jnp.where(y == 0, 0, jnp.where(y == ny - 1, 1, y + 1))
        val[where, :] = jnp.where(r_all < 0, -1, y * nx + r_all // ny).astype(f32)

    tall, depth = 512, 16

    def deposit(m, begin, end, acc):
        first = m * float(tall)

        def inner(k, acc):
            pieces = []
            for h in range(depth):
                r = val[pl.ds(k * depth + h, 1), :] - first
                parts = []
                for g in range(tall // 256):
                    q = r - 256.0 * g
                    parts.append(hot(jnp.where((q >= 0) & (q < 256), q, -1.0), iota))
                pieces.append(jnp.concatenate(parts, axis=0))
            where = pl.ds(pl.multiple_of(k * (depth * LANES), depth * LANES), depth * LANES)
            return acc + lax.dot_general(
                jnp.concatenate(pieces, axis=1), sp[:, where], NT, preferred_element_type=f32
            )

        return lax.fori_loop(begin, end, inner, acc)

    planes = tall // nx
    nothing = jnp.zeros((tall, 2 * LANES), f32)
    steps = count // depth
    decode(0)
    got = deposit(0.0, 0, steps // 2, nothing)
    relay.wait()
    decode(1)
    got = deposit(0.0, steps // 2, steps, got)
    got = got[:, :LANES] + got[:, LANES:]
    for n, y in enumerate((0, ny - 1) + tuple(range(1, planes - 1))):
        src[pl.ds(y, nx, stride=ny), :] = got[n * nx : (n + 1) * nx]

    for copy in early:
        copy.wait()

    final = crosses - 1
    low_edge, high_edge = s == 0, s == final
    sub = lax.broadcasted_iota(i32, (ny, LANES), 0)
    lane = lax.broadcasted_iota(i32, (ny, LANES), 1)

    def edge(cref, tref):
        cref[0:ny, :] = hx[1, 0] * conduct(tref[0:ny, :])
        cref[rows + ny : rows + 2 * ny, :] = hx[1, 1] * conduct(tref[rows + ny : rows + 2 * ny, :])

    def rim(tlo, thi, tref, cref):
        for n, (off, plane, k, at) in enumerate(((low_edge, tlo, hy[1, 0], ny), (high_edge, thi, hy[1, 1], 2 * ny - 1))):
            t = jnp.where(off, 0.0, plane)
            cc = jnp.where(off, 0.0, k) * conduct(t)
            t0 = tref[pl.ds(at, nx, stride=ny), :]
            c0 = cref[pl.ds(at, nx, stride=ny), :]
            flux[n] = (cc + c0) * ((t0 - t) if n == 0 else (t - t0))

    many = 16

    def step(tin, cin, emit, parts=1, done=None):

        def body(b, before):
            for u in range(many):
                x = b * many + u
                here = pl.ds(pl.multiple_of(x * ny + ny, ny), ny)
                ahead = pl.ds(pl.multiple_of(x * ny + 2 * ny, ny), ny)
                t0, c0 = tin[here, :], cin[here, :]
                t1, c1 = tin[ahead, :], cin[ahead, :]
                fx = (c0 + c1) * (t1 - t0)
                at = pl.ds(x, 1)
                ahead_t, ahead_c = pltpu.roll(t0, ny - 1, 0), pltpu.roll(c0, ny - 1, 0)
                fy = jnp.where(sub == ny - 1, flux[1, at, :], (c0 + ahead_c) * (ahead_t - t0))
                fy0 = jnp.where(sub == 0, flux[0, at, :], pltpu.roll(fy, 1, 0))
                ct = c0 * t0
                tz, cz = pltpu.roll(t0, LANES - 1, 1), pltpu.roll(c0, LANES - 1, 1)
                fz = jnp.where(lane == LANES - 1, -ct, (c0 + cz) * (tz - t0))
                fz0 = jnp.where(lane == 0, ct, pltpu.roll(fz, 1, 1))
                emit(x, t0 + 0.5 * (((fx - before) + (fy - fy0)) + (fz - fz0)))
                before = fx
            return before

        t0, c0 = tin[ny : 2 * ny, :], cin[ny : 2 * ny, :]
        tm, cm = tin[0:ny, :], cin[0:ny, :]
        turns = nx // many // parts

        def piece(k, before):
            before = lax.fori_loop(k * turns, (k + 1) * turns, body, before)
            done(k)
            return before

        if done is None:
            lax.fori_loop(0, turns, body, (cm + c0) * (t0 - tm))
        else:
            lax.fori_loop(0, parts, piece, (cm + c0) * (t0 - tm))

    def send_x(k, tref):
        copies = [
            remote(tref.at[pl.ds(rows, ny)], tref.at[pl.ds(0, ny)], xs.at[2 * k], xr.at[2 * k], (above, s)),
            remote(
                tref.at[pl.ds(ny, ny)], tref.at[pl.ds(rows + ny, ny)], xs.at[2 * k + 1], xr.at[2 * k + 1], (below, s)
            ),
        ]
        for copy in copies:
            copy.start()
        return copies

    def send_y():
        copies = [
            remote(ysend.at[0, 1], stage.at[0, 0], ys.at[0], yr.at[0], (c, right)),
            remote(ysend.at[0, 0], stage.at[0, 1], ys.at[1], yr.at[1], (c, left)),
        ]
        for copy in copies:
            copy.start()
        return copies

    ta[0:ny, :] = hx[0, 0]
    ta[rows + ny : rows + 2 * ny, :] = hx[0, 1]
    edge(ca, ta)
    rim(hy[0, 0], hy[0, 1], ta, ca)

    def emit_first(x, t):
        d1[pl.ds(pl.multiple_of(x * ny, ny), ny), :] = t

    step(ta, ca, emit_first)
    for n, y in enumerate((0, ny - 1)):
        ysend[0, n] = d1[pl.ds(y, nx, stride=ny), :] + src[pl.ds(y, nx, stride=ny), :]
    first = send_y()

    def others(m, carry):
        got = deposit(m.astype(f32), 0, steps, nothing)
        got = got[:, :LANES] + got[:, LANES:]
        for n in range(planes):
            src[pl.ds(m * planes + (n - 1), nx, stride=ny), :] = got[n * nx : (n + 1) * nx]
        return carry

    lax.fori_loop(1, rows // tall, others, 0)

    def finish(b, carry):
        where = pl.ds(pl.multiple_of(b * block, block), block)
        there = pl.ds(pl.multiple_of(b * block + ny, ny), block)
        t = d1[where, :] + src[where, :]
        tb[there, :] = t
        cb[there, :] = kappa[where, :] * conduct(t)
        return carry

    lax.fori_loop(0, rows // block, finish, 0)
    first += send_x(0, tb)

    lax.fori_loop(0, bond_rows // group // 2, differences, 0)
    iota32 = iota[:hi_rows]

    def scatter(values):
        def body(k, acc):
            lhs = []
            for u in range(depth):
                r = k * depth + u
                h = (acted[pl.ds(r, 1), :] // LANES).astype(f32)
                tops, bottoms = [], []
                for v in values(r):
                    top = high(v)
                    tops.append(spread(h, top, iota32))
                    bottoms.append(spread(h, v - top, iota32))
                lhs.append(jnp.concatenate(tops + bottoms, axis=0))
            where = pl.ds(pl.multiple_of(k * (depth * LANES), depth * LANES), depth * LANES)
            return acc + lax.dot_general(
                jnp.concatenate(lhs, axis=1), ohl[:, where], NT, preferred_element_type=f32
            )

        n = 3 * hi_rows
        acc = lax.fori_loop(0, bond_rows // depth, body, jnp.zeros((2 * n, LANES), f32))
        return acc[:n] + acc[n:]

    def rows_of(lo):
        return lambda r: [pq[lo + ch, pl.ds(r, 1), :] for ch in range(3)]

    for copy in first:
        copy.wait()
    edge(cb, tb)
    rim(stage[0, 0], stage[0, 1], tb, cb)

    def emit_second(x, t):
        where = pl.ds(pl.multiple_of(x * ny, ny), ny)
        here = pl.ds(pl.multiple_of(x * ny + ny, ny), ny)
        t = t + src[where, :]
        ta[here, :] = t
        ca[here, :] = kappa[where, :] * conduct(t)

    pieces = 4
    width = nx // pieces

    def strip(k):
        at = pl.ds(pl.multiple_of(k * width, width), width)
        return [
            remote(ysend.at[1, 1, at], stage.at[1, 0, at], zs_sem.at[k], zr_sem.at[k], (c, right)),
            remote(ysend.at[1, 0, at], stage.at[1, 1, at], zs_sem.at[pieces + k], zr_sem.at[pieces + k], (c, left)),
        ]

    def strip_done(k):
        at = pl.ds(pl.multiple_of(k * width, width), width)
        for n, y in enumerate((ny, 2 * ny - 1)):
            ysend[1, n, at, :] = ta[pl.ds(k * (width * ny) + y, width, stride=ny), :]
        for copy in strip(k):
            copy.start()

    step(tb, cb, emit_second, pieces, strip_done)
    second = send_x(1, ta)
    lax.fori_loop(bond_rows // group // 2, bond_rows // group, differences, 0)
    extra_rows = [(hi_rows + side * gcount + g, side, g) for side in range(2) for g in range(gcount)]
    for k in range(0, bond_rows, 8):
        q = other[k : k + 8, :]
        h, l = q // LANES, q % LANES
        for ch in range(3):
            d = pq[ch, k : k + 8, :]
            g = table_pick([(n, ghosts[side, ch * gcount + i : ch * gcount + i + 1, :]) for n, side, i in extra_rows], h, l, zero8)
            pq[ch, k : k + 8, :] = d + g
    d = [pq[ch] for ch in range(3)]
    dist = jnp.sqrt(d[0] * d[0] + d[1] * d[1] + d[2] * d[2])
    g = gap[...]
    base = (1.0 - snapped[...].astype(f32)) / jnp.maximum(dist, 0.3)
    p = base * (dist - g)
    q = base * (-0.1 * g)
    for ch in range(3):
        pq[ch] = p * d[ch]
        pq[3 + ch] = q * d[ch]
    for copy in second:
        copy.wait()

    def strip_taken(k, carry):
        for copy in strip(k):
            copy.wait()
        return carry

    lax.fori_loop(0, pieces, strip_taken, 0)
    edge(ca, ta)
    rim(stage[1, 0], stage[1, 1], ta, ca)

    def emit_third(x, t):
        where = pl.ds(pl.multiple_of(x * ny, ny), ny)
        temp_out[where, :] = t + src[where, :]

    step(ta, ca, emit_third)
    store = pltpu.make_async_copy(temp_out, temp_hbm_out, local.at[11])
    store.start()

    for k in range(rows // LANES):
        b = temp_out[k * LANES : (k + 1) * LANES, :].T
        hi = b.astype(bf16)
        tt[0:LANES, k * LANES : (k + 1) * LANES] = hi
        tt[LANES : 2 * LANES, k * LANES : (k + 1) * LANES] = (b - hi.astype(f32)).astype(bf16)
    zs = lax.broadcasted_iota(i32, (LANES, LANES), 0).astype(f32)

    def look(slots):
        cols = []
        for n in slots:
            for h in range(per):
                r = row[pl.ds(n * per + h, 1), :]
                parts = []
                for k in range(rows // 256):
                    q = r - 256.0 * k
                    parts.append(hot(jnp.where((q >= 0) & (q < 256), q, -1.0), iota))
                cols.append(jnp.concatenate(parts, axis=0))
        got = jnp.dot(tt[...], jnp.concatenate(cols, axis=1), preferred_element_type=f32)
        got = got[:LANES] + got[LANES:]
        for i, n in enumerate(slots):
            for h in range(per):
                u = i * per + h
                z = zed[pl.ds(n * per + h, 1), :]
                v = jnp.where(zs == z, got[:, u * LANES : (u + 1) * LANES], 0.0)
                picked[n, h : h + 1, :] = jnp.sum(v, axis=0, keepdims=True)

    def look_below(k, carry):
        look((crosses + 2 * k, crosses + 2 * k + 1))
        return carry

    lax.fori_loop(0, crosses // 2, look_below, 0)
    hand = remote(picked.at[pl.ds(crosses, crosses)], far, hsend.at[11], hrecv.at[11], (below, s))
    hand.start()

    def pair(k):
        return lax.rem(s + 2 * k + 1, crosses), lax.rem(s + 2 * k + 2, crosses)

    def merge(j):
        m = row[pl.ds(j * per, per), :] < 0
        return jnp.where(m, far[pl.ds(j, 1)].reshape(per, LANES), picked[pl.ds(j, 1)].reshape(per, LANES))

    def back_to(j):
        ret[pl.ds(j, 1)] = merge(j).reshape(1, per, LANES)
        remote(ret.at[j], back.at[s], bs.at[j], br.at[s], (c, j)).start()

    held = 3

    def look_first(k, carry):
        look(pair(k))
        return carry

    lax.fori_loop(0, held, look_first, 0)
    hand.wait()

    def send_held(i, carry):
        back_to(lax.rem(s + i, crosses))
        return carry

    lax.fori_loop(1, 2 * held + 1, send_held, 0)

    def look_then(k, carry):
        a, b = pair(k)
        look((a, b))
        back_to(a)
        back_to(b)
        return carry

    lax.fori_loop(held, crosses // 2 - 1, look_then, 0)
    a, b = pair(crosses // 2 - 1)
    look((a, b))
    back_to(a)
    back[pl.ds(s, 1)] = merge(s).reshape(1, per, LANES)
    own[0] = scatter(rows_of(0))

    def back_same(k, carry):
        j = lax.rem(s + k, crosses)
        remote(ret.at[j], back.at[j], bs.at[j], br.at[j], (c, j)).wait()
        return carry

    lax.fori_loop(1, crosses, back_same, 0)
    warm = jnp.concatenate([back[j] for j in range(crosses)], axis=0)
    table = [(r, warm[r : r + 1]) for r in range(hi_rows)]
    gtemp_send[...] = table_pick(table, eh, el, zero8)[:gcount]
    copies = [
        remote(gtemp_send, gtemp.at[0], gs.at[0], gr.at[0], (above, s)),
        remote(gtemp_send, gtemp.at[1], gs.at[1], gr.at[1], (below, s)),
    ]
    for copy in copies:
        copy.start()
    partner = []
    for k in range(0, bond_rows, 8):
        q = other[k : k + 8, :]
        partner.append(table_pick(table, q // LANES, q % LANES, zero8))
    own[1] = scatter(rows_of(3))
    for copy in copies:
        copy.wait()
    for n, k in enumerate(range(0, bond_rows, 8)):
        q = other[k : k + 8, :]
        t = table_pick(
            [(m, gtemp[side, i : i + 1, :]) for m, side, i in extra_rows], q // LANES, q % LANES, partner[n]
        )
        for ch in range(3):
            pq[3 + ch, k : k + 8, :] = pq[3 + ch, k : k + 8, :] * t
    force_out[...] = own[0] + scatter(rows_of(3)) + jnp.concatenate([warm] * 3, axis=0) * own[1]
    store.wait()


def update_kernel(
    temp, force_hbm, pos_hbm, vel_hbm, temp_out, pos_out, vel_out, held, force, pos, vel, sems, small
):
    parts = held.shape[0]
    rows = held.shape[1]
    first = [
        pltpu.make_async_copy(a, b, small.at[n])
        for n, (a, b) in enumerate(((force_hbm, force), (pos_hbm, pos), (vel_hbm, vel)))
    ]
    where = [pl.ds(n * rows, rows) for n in range(parts)]
    loads = [pltpu.make_async_copy(temp.at[w], held.at[n], sems.at[0, n]) for n, w in enumerate(where)]
    stores = [pltpu.make_async_copy(held.at[n], temp_out.at[w], sems.at[1, n]) for n, w in enumerate(where)]
    for load in first + loads:
        load.start()
    for load in first:
        load.wait()
    hi_rows = pos.shape[1] // LANES
    for r in range(hi_rows):
        at = slice(r * LANES, (r + 1) * LANES)
        v = vel[:, at] + 0.5 * force[pl.ds(r, 3, stride=hi_rows), :]
        vel[:, at] = v
        pos[:, at] = pos[:, at] + 0.5 * v
    last = [pltpu.make_async_copy(vel, vel_out, small.at[3]), pltpu.make_async_copy(pos, pos_out, small.at[4])]
    for store in last:
        store.start()
    for load, store in zip(loads, stores):
        load.wait()
        store.start()
    for store in stores + last:
        store.wait()


def per_device(
    cuts, crosses, temp, kappa, locator, gain, mark, pos, vel, acted, other, gap, snapped, exported
):
    nx, ny, nz = temp.shape
    rows = nx * ny
    flat = lambda a: a.reshape(-1, LANES)
    loc, gain, mark = flat(locator), flat(gain), flat(mark)
    acted, other, gap, snapped, exported = map(flat, (acted, other, gap, snapped, exported))
    hi_rows = loc.shape[0]
    per = hi_rows // crosses
    gcount = exported.shape[0]
    bonds = acted.shape[0]
    lr = 2 * crosses * per
    shape = jax.ShapeDtypeStruct
    dma = pltpu.SemaphoreType.DMA
    vm = pltpu.VMEM
    plane = (2, 2, nx, nz)
    padded = (rows + 2 * ny, nz)
    arrays = (
        loc, gain, mark, exported, pos, temp.reshape(rows, nz), kappa.reshape(rows, nz), acted, other, gap, snapped
    )
    temp_new, force = pl.pallas_call(
        functools.partial(kernel, cuts, crosses),
        out_shape=(shape((rows, nz), f32), shape((3 * hi_rows, LANES), f32)),
        in_specs=[ANY] * 11,
        out_specs=(ANY, VMEM),
        scratch_shapes=[vm(a.shape, a.dtype) for a in arrays]
        + [
            vm((rows, nz), f32),
            vm((2 * crosses, 2 * per, LANES), f32),
            vm((crosses, 2 * per, LANES), f32),
            vm((2, 2, ny, nz), f32),
            vm(plane, f32),
            vm(plane, f32),
            vm((2, 3 * gcount, LANES), f32),
            vm((3 * gcount, LANES), f32),
            vm((lr, LANES), f32),
            vm((lr, LANES), f32),
            vm((lr, LANES), f32),
            vm((2 * LANES, lr * LANES), bf16),
            vm((LANES, bonds * LANES), bf16),
            vm((256, LANES), bf16),
            vm((rows, nz), f32),
            vm((rows, nz), f32),
            vm(padded, f32),
            vm(padded, f32),
            vm(padded, f32),
            vm(padded, f32),
            vm(plane, f32),
            vm((2, nx, nz), f32),
            vm((2 * nz, rows), bf16),
            vm((2 * crosses, per, LANES), f32),
            vm((crosses, per, LANES), f32),
            vm((crosses, per, LANES), f32),
            vm((crosses, per, LANES), f32),
            vm(plane, f32),
            vm((gcount, LANES), f32),
            vm((2, gcount, LANES), f32),
            vm((6, bonds, LANES), f32),
            vm((2, 3 * hi_rows, LANES), f32),
            dma((crosses,)),
            dma((crosses,)),
            dma((12,)),
            dma((12,)),
            dma((4,)),
            dma((4,)),
            dma((2,)),
            dma((2,)),
            dma((8,)),
            dma((8,)),
            dma((crosses,)),
            dma((crosses,)),
            dma((2,)),
            dma((2,)),
            dma((12,)),
        ],
        compiler_params=pltpu.CompilerParams(collective_id=0, has_side_effects=True),
        name="substeps",
    )(*arrays)
    temp_new, pos_new, vel_new = pl.pallas_call(
        update_kernel,
        out_shape=(shape((rows, nz), f32), shape(pos.shape, f32), shape(vel.shape, f32)),
        in_specs=[ANY] * 4,
        out_specs=(ANY,) * 3,
        scratch_shapes=[
            vm((4, rows // 4, nz), f32),
            vm(force.shape, f32),
            vm(pos.shape, f32),
            vm(vel.shape, f32),
            dma((2, 4)),
            dma((5,)),
        ],
        name="update",
    )(temp_new, force, pos, vel)
    return temp_new.reshape(nx, ny, nz), pos_new, vel_new


def solution(mesh):
    both = P(("cut", "cross"))
    return jax.shard_map(
        functools.partial(per_device, mesh.shape["cut"], mesh.shape["cross"]),
        mesh=mesh,
        in_specs=(P("cut", "cross", None),) * 2
        + (both,) * 3
        + (P(None, ("cut", "cross")),) * 2
        + (both,) * 5,
        out_specs=(P("cut", "cross", None), P(None, ("cut", "cross")), P(None, ("cut", "cross"))),
        check_vma=False,
    )
```

```python
import functools

import jax
import jax.numpy as jnp
from jax import lax
from jax.experimental import pallas as pl
from jax.experimental.pallas import tpu as pltpu
from jax.sharding import PartitionSpec as P

f32 = jnp.float32
bf16 = jnp.bfloat16
i32 = jnp.int32
MESH = pl.DeviceIdType.MESH
NT = (((1,), (1,)), ((), ()))
LANES = 128
VMEM = pl.BlockSpec(memory_space=pltpu.VMEM)
ANY = pl.BlockSpec(memory_space=pl.ANY)


def stack(tile, count):
    return jnp.concatenate([tile] * count, axis=0)


def rows16(row):
    return jnp.broadcast_to(row, (16, row.shape[1])).astype(bf16)


def hot(row, iota):
    r = stack(rows16(row), iota.shape[0] // 16)
    return jnp.where(iota == r, jnp.ones_like(iota), jnp.zeros_like(iota))


def spread(row, val, iota):
    r = stack(rows16(row), iota.shape[0] // 16)
    v = stack(rows16(val), iota.shape[0] // 16)
    return jnp.where(iota == r, v, jnp.zeros_like(iota))


def iota_rows(count):
    return lax.broadcasted_iota(i32, (count, LANES), 0).astype(f32).astype(bf16)


def high(v):
    return v.astype(bf16).astype(f32)


def conduct(t):
    return 0.5 + 1.0 / (1.0 + t * t)


def peers(cuts, crosses):
    c, s = lax.axis_index("cut"), lax.axis_index("cross")
    below, above = lax.rem(c + cuts - 1, cuts), lax.rem(c + 1, cuts)
    return c, s, below, above


def greet(cuts, crosses):
    c, s, below, above = peers(cuts, crosses)
    barrier = pltpu.get_barrier_semaphore()

    for device in ((below, s), (above, s)):
        pl.semaphore_signal(barrier, inc=1, device_id=device, device_id_type=MESH)

    def other(k, carry):
        j = lax.rem(s + k, crosses)
        pl.semaphore_signal(barrier, inc=1, device_id=(c, j), device_id_type=MESH)
        return carry

    lax.fori_loop(1, crosses, other, 0)


def await_all(crosses):
    pl.semaphore_wait(pltpu.get_barrier_semaphore(), crosses + 1)


def remote(src, dst, send, recv, device):
    return pltpu.make_async_remote_copy(
        src_ref=src, dst_ref=dst, send_sem=send, recv_sem=recv, device_id=device, device_id_type=MESH
    )


def lane_pick(row, index):
    return jnp.take_along_axis(row, index, axis=1, mode="promise_in_bounds")


def table_pick(rows, high_index, low_index, start):
    out = start
    for number, row in rows:
        wide = jnp.broadcast_to(row, low_index.shape)
        out = jnp.where(high_index == number, lane_pick(wide, low_index), out)
    return out


def kernel(
    cuts, crosses, *refs
):
    inputs, (temp_hbm_out, force_out) = refs[:11], refs[11:13]
    loc, gain, mark, exported, pos, temp, kappa, acted, other, gap, snapped = refs[13:24]
    (
    temp_out, lists, send_lists, hx, hy, ysend0, ghosts, gsend,
    row, zed, val, sp, ohl, big, d1, src, ta, tb, ca, cb, ysend, flux, tt, picked, far, ret, back, stage,
    gtemp_send, gtemp, pq, own,
    send_sem, recv_sem, hsend, hrecv, xs, xr, ys, yr, zs_sem, zr_sem, bs, br, gs, gr, local,
    ) = refs[24:]
    c, s, below, above = peers(cuts, crosses)
    left, right = lax.rem(s + crosses - 1, crosses), lax.rem(s + 1, crosses)
    loads = [pltpu.make_async_copy(a, b, local.at[n]) for n, (a, b) in enumerate(zip(inputs, refs[13:24]))]
    for load in loads:
        load.start()
    greet(cuts, crosses)
    rows = temp.shape[0]
    nx = hy.shape[2]
    ny = rows // nx
    cells = rows * LANES
    hi_rows = loc.shape[0]
    per = hi_rows // crosses
    gcount = exported.shape[0]
    bond_rows = acted.shape[0]

    for load in loads[:3]:
        load.wait()
    w = loc[...].astype(f32)
    power = mark[...].astype(f32) * gain[...] * 0.5
    for j in range(crosses):
        send_lists[j, 0:per, :] = w[j * per : (j + 1) * per]
        send_lists[j, per : 2 * per, :] = power[j * per : (j + 1) * per]
    await_all(crosses)

    def send_same(k, carry):
        j = lax.rem(s + k, crosses)
        remote(send_lists.at[j], lists.at[s], send_sem.at[j], recv_sem.at[s], (c, j)).start()
        return carry

    lax.fori_loop(1, crosses, send_same, 0)
    lists[pl.ds(s, 1)] = send_lists[pl.ds(s, 1)]
    for load in loads[3:]:
        load.wait()
    for a, ref in enumerate((temp, kappa)):
        ysend0[a, 0] = ref[pl.ds(0, nx, stride=ny), :]
        ysend0[a, 1] = ref[pl.ds(ny - 1, nx, stride=ny), :]
    early = []
    for a, ref in enumerate((temp, kappa)):
        early.append(remote(ysend0.at[a, 1], hy.at[a, 0], hsend.at[4 * a + 2], hrecv.at[4 * a + 2], (c, right)))
        early.append(remote(ysend0.at[a, 0], hy.at[a, 1], hsend.at[4 * a + 3], hrecv.at[4 * a + 3], (c, left)))
        early.append(remote(ref.at[pl.ds(rows - ny, ny)], hx.at[a, 0], hsend.at[4 * a], hrecv.at[4 * a], (above, s)))
        early.append(remote(ref.at[pl.ds(0, ny)], hx.at[a, 1], hsend.at[4 * a + 1], hrecv.at[4 * a + 1], (below, s)))
    for copy in early:
        copy.start()
    e8 = jnp.concatenate([exported[...]] * (8 // gcount), axis=0)
    eh, el = e8 // LANES, e8 % LANES
    zero8 = jnp.zeros((8, LANES), f32)

    def row_of(ref, ch, r):
        return ref[ch : ch + 1, pl.ds(pl.multiple_of(r * LANES, LANES), LANES)]

    def export_rows(r, acc):
        return tuple(table_pick([(r, row_of(pos, ch, r))], eh, el, acc[ch]) for ch in range(3))

    acc = lax.fori_loop(0, hi_rows, export_rows, (zero8,) * 3, unroll=8)
    for ch in range(3):
        gsend[ch * gcount : (ch + 1) * gcount, :] = acc[ch][:gcount]

    late = [
        remote(gsend, ghosts.at[0], hsend.at[8], hrecv.at[8], (above, s)),
        remote(gsend, ghosts.at[1], hsend.at[9], hrecv.at[9], (below, s)),
    ]
    for copy in late:
        copy.start()
    early += late

    group = 16

    def differences(k, carry):
        where = pl.ds(pl.multiple_of(k * group, group), group)
        qa, qb = acted[where, :], other[where, :]
        index = [(q[h : h + 8] // LANES, q[h : h + 8] % LANES) for q in (qa, qb) for h in range(0, group, 8)]

        def one(r, acc):
            out = []
            for ch in range(3):
                wide = jnp.broadcast_to(row_of(pos, ch, r), (8, LANES))
                for n, (h, l) in enumerate(index):
                    out.append(jnp.where(h == r, lane_pick(wide, l), acc[ch * len(index) + n]))
            return tuple(out)

        acc = lax.fori_loop(0, hi_rows, one, (zero8,) * (3 * len(index)), unroll=4)
        half = len(index) // 2
        for ch in range(3):
            for n in range(half):
                first, second = acc[ch * len(index) + n], acc[ch * len(index) + half + n]
                pq[ch, pl.ds(pl.multiple_of(k * group + 8 * n, 8), 8), :] = second - first
        return carry

    block = 16 * ny

    def begin(b, carry):
        where = pl.ds(pl.multiple_of(b * block, block), block)
        there = pl.ds(pl.multiple_of(b * block + ny, ny), block)
        t = temp[where, :]
        ta[there, :] = t
        ca[there, :] = kappa[where, :] * conduct(t)
        return carry

    lax.fori_loop(0, rows // block, begin, 0)
    big[...] = iota_rows(256)
    iota = big[...]
    small = iota[:LANES]

    def lows(k, carry):
        for u in range(4):
            r = k * 4 + u
            a = (acted[pl.ds(r, 1), :] % LANES).astype(f32)
            ohl[:, pl.ds(pl.multiple_of(r * LANES, LANES), LANES)] = hot(a, small)
        return carry

    lax.fori_loop(0, bond_rows // 4, lows, 0)
    lax.fori_loop(0, bond_rows // group // 2, differences, 0)

    def take_same(k, carry):
        j = lax.rem(s + k, crosses)
        remote(send_lists.at[j], lists.at[j], send_sem.at[j], recv_sem.at[j], (c, j)).wait()
        return carry

    lax.fori_loop(1, crosses, take_same, 0)
    relay = remote(
        lists.at[pl.ds(0, crosses)], lists.at[pl.ds(crosses, crosses)], hsend.at[10], hrecv.at[10], (above, s)
    )
    relay.start()

    count = row.shape[0]

    def build(k, carry):
        for u in range(8):
            r = k * 8 + u
            z = zed[pl.ds(r, 1), :]
            v = val[pl.ds(r, 1), :]
            hi = high(v)
            where = pl.ds(pl.multiple_of(r * LANES, LANES), LANES)
            sp[0:LANES, where] = spread(z, hi, small)
            sp[LANES : 2 * LANES, where] = spread(z, v - hi, small)
        return carry

    def decode(half):
        for b in range(half * crosses, (half + 1) * crosses):
            q = lists[b, 0:per, :].astype(i32)
            here = (q >= cells) == (half == 1)
            q = q & (cells - 1)
            row[b * per : (b + 1) * per, :] = jnp.where(here, q // LANES, -1).astype(f32)
            zed[b * per : (b + 1) * per, :] = (q % LANES).astype(f32)
            val[b * per : (b + 1) * per, :] = jnp.where(here, lists[b, per : 2 * per, :], 0.0)
        lax.fori_loop(half * count // 16, (half + 1) * count // 16, build, 0)
        where = slice(half * count // 2, (half + 1) * count // 2)
        r_all = row[where, :].astype(i32)
        y = r_all & (ny - 1)
        y = jnp.where(y == 0, 0, jnp.where(y == ny - 1, 1, y + 1))
        val[where, :] = jnp.where(r_all < 0, -1, y * nx + r_all // ny).astype(f32)

    tall, depth = 512, 16

    def deposit(m, begin, end, acc):
        first = m * float(tall)

        def inner(k, acc):
            pieces = []
            for h in range(depth):
                r = val[pl.ds(k * depth + h, 1), :] - first
                parts = []
                for g in range(tall // 256):
                    q = r - 256.0 * g
                    parts.append(hot(jnp.where((q >= 0) & (q < 256), q, -1.0), iota))
                pieces.append(jnp.concatenate(parts, axis=0))
            where = pl.ds(pl.multiple_of(k * (depth * LANES), depth * LANES), depth * LANES)
            return acc + lax.dot_general(
                jnp.concatenate(pieces, axis=1), sp[:, where], NT, preferred_element_type=f32
            )

        return lax.fori_loop(begin, end, inner, acc)

    planes = tall // nx
    nothing = jnp.zeros((tall, 2 * LANES), f32)
    steps = count // depth
    decode(0)
    got = deposit(0.0, 0, steps // 2, nothing)
    relay.wait()
    decode(1)
    got = deposit(0.0, steps // 2, steps, got)
    got = got[:, :LANES] + got[:, LANES:]
    for n, y in enumerate((0, ny - 1) + tuple(range(1, planes - 1))):
        src[pl.ds(y, nx, stride=ny), :] = got[n * nx : (n + 1) * nx]

    for copy in early:
        copy.wait()

    final = crosses - 1
    low_edge, high_edge = s == 0, s == final
    sub = lax.broadcasted_iota(i32, (ny, LANES), 0)
    lane = lax.broadcasted_iota(i32, (ny, LANES), 1)

    def edge(cref, tref):
        cref[0:ny, :] = hx[1, 0] * conduct(tref[0:ny, :])
        cref[rows + ny : rows + 2 * ny, :] = hx[1, 1] * conduct(tref[rows + ny : rows + 2 * ny, :])

    def rim(tlo, thi, tref, cref):
        for n, (off, plane, k, at) in enumerate(((low_edge, tlo, hy[1, 0], ny), (high_edge, thi, hy[1, 1], 2 * ny - 1))):
            t = jnp.where(off, 0.0, plane)
            cc = jnp.where(off, 0.0, k) * conduct(t)
            t0 = tref[pl.ds(at, nx, stride=ny), :]
            c0 = cref[pl.ds(at, nx, stride=ny), :]
            flux[n] = (cc + c0) * ((t0 - t) if n == 0 else (t - t0))

    many = 32

    def step(tin, cin, emit, parts=1, done=None):

        def body(b, before):
            for u in range(many):
                x = b * many + u
                here = pl.ds(pl.multiple_of(x * ny + ny, ny), ny)
                ahead = pl.ds(pl.multiple_of(x * ny + 2 * ny, ny), ny)
                t0, c0 = tin[here, :], cin[here, :]
                t1, c1 = tin[ahead, :], cin[ahead, :]
                fx = (c0 + c1) * (t1 - t0)
                at = pl.ds(x, 1)
                north, south = pl.ds(x * ny + ny + 1, ny), pl.ds(x * ny + ny - 1, ny)
                fy = jnp.where(sub == ny - 1, flux[1, at, :], (c0 + cin[north, :]) * (tin[north, :] - t0))
                fy0 = jnp.where(sub == 0, flux[0, at, :], (c0 + cin[south, :]) * (t0 - tin[south, :]))
                ct = c0 * t0
                tz, cz = pltpu.roll(t0, LANES - 1, 1), pltpu.roll(c0, LANES - 1, 1)
                tw, cw = pltpu.roll(t0, 1, 1), pltpu.roll(c0, 1, 1)
                fz = jnp.where(lane == LANES - 1, -ct, (c0 + cz) * (tz - t0))
                fz0 = jnp.where(lane == 0, ct, (c0 + cw) * (t0 - tw))
                emit(x, t0 + 0.5 * (((fx - before) + (fy - fy0)) + (fz - fz0)))
                before = fx
            return before

        t0, c0 = tin[ny : 2 * ny, :], cin[ny : 2 * ny, :]
        tm, cm = tin[0:ny, :], cin[0:ny, :]
        turns = nx // many // parts

        def piece(k, before):
            before = lax.fori_loop(k * turns, (k + 1) * turns, body, before)
            done(k)
            return before

        if done is None:
            lax.fori_loop(0, turns, body, (cm + c0) * (t0 - tm))
        else:
            lax.fori_loop(0, parts, piece, (cm + c0) * (t0 - tm))

    def send_x(k, tref):
        copies = [
            remote(tref.at[pl.ds(rows, ny)], tref.at[pl.ds(0, ny)], xs.at[2 * k], xr.at[2 * k], (above, s)),
            remote(
                tref.at[pl.ds(ny, ny)], tref.at[pl.ds(rows + ny, ny)], xs.at[2 * k + 1], xr.at[2 * k + 1], (below, s)
            ),
        ]
        for copy in copies:
            copy.start()
        return copies

    def send_y():
        copies = [
            remote(ysend.at[0, 1], stage.at[0, 0], ys.at[0], yr.at[0], (c, right)),
            remote(ysend.at[0, 0], stage.at[0, 1], ys.at[1], yr.at[1], (c, left)),
        ]
        for copy in copies:
            copy.start()
        return copies

    ta[0:ny, :] = hx[0, 0]
    ta[rows + ny : rows + 2 * ny, :] = hx[0, 1]
    edge(ca, ta)
    rim(hy[0, 0], hy[0, 1], ta, ca)

    def emit_first(x, t):
        d1[pl.ds(pl.multiple_of(x * ny, ny), ny), :] = t

    step(ta, ca, emit_first)
    for n, y in enumerate((0, ny - 1)):
        ysend[0, n] = d1[pl.ds(y, nx, stride=ny), :] + src[pl.ds(y, nx, stride=ny), :]
    first = send_y()

    def others(m, carry):
        got = deposit(m.astype(f32), 0, steps, nothing)
        got = got[:, :LANES] + got[:, LANES:]
        for n in range(planes):
            src[pl.ds(m * planes + (n - 1), nx, stride=ny), :] = got[n * nx : (n + 1) * nx]
        return carry

    lax.fori_loop(1, rows // tall, others, 0)

    def finish(b, carry):
        where = pl.ds(pl.multiple_of(b * block, block), block)
        there = pl.ds(pl.multiple_of(b * block + ny, ny), block)
        t = d1[where, :] + src[where, :]
        tb[there, :] = t
        cb[there, :] = kappa[where, :] * conduct(t)
        return carry

    lax.fori_loop(0, rows // block, finish, 0)
    first += send_x(0, tb)

    lax.fori_loop(bond_rows // group // 2, bond_rows // group, differences, 0)
    iota32 = iota[:hi_rows]

    turn = 32

    def scatter(values):
        def body(k, acc):
            lhs = []
            for u in range(turn):
                r = k * turn + u
                h = (acted[pl.ds(r, 1), :] // LANES).astype(f32)
                tops, bottoms = [], []
                for v in values(r):
                    top = high(v)
                    tops.append(spread(h, top, iota32))
                    bottoms.append(spread(h, v - top, iota32))
                lhs.append(jnp.concatenate(tops + bottoms, axis=0))
            where = pl.ds(pl.multiple_of(k * (turn * LANES), turn * LANES), turn * LANES)
            return acc + lax.dot_general(
                jnp.concatenate(lhs, axis=1), ohl[:, where], NT, preferred_element_type=f32
            )

        n = 3 * hi_rows
        acc = lax.fori_loop(0, bond_rows // turn, body, jnp.zeros((2 * n, LANES), f32))
        return acc[:n] + acc[n:]

    def rows_of(lo):
        return lambda r: [pq[lo + ch, pl.ds(r, 1), :] for ch in range(3)]

    for copy in first:
        copy.wait()
    edge(cb, tb)
    rim(stage[0, 0], stage[0, 1], tb, cb)

    def emit_second(x, t):
        where = pl.ds(pl.multiple_of(x * ny, ny), ny)
        here = pl.ds(pl.multiple_of(x * ny + ny, ny), ny)
        t = t + src[where, :]
        ta[here, :] = t
        ca[here, :] = kappa[where, :] * conduct(t)

    pieces = 4
    width = nx // pieces

    def strip(k):
        at = pl.ds(pl.multiple_of(k * width, width), width)
        return [
            remote(ysend.at[1, 1, at], stage.at[1, 0, at], zs_sem.at[k], zr_sem.at[k], (c, right)),
            remote(ysend.at[1, 0, at], stage.at[1, 1, at], zs_sem.at[pieces + k], zr_sem.at[pieces + k], (c, left)),
        ]

    def strip_done(k):
        at = pl.ds(pl.multiple_of(k * width, width), width)
        for n, y in enumerate((ny, 2 * ny - 1)):
            ysend[1, n, at, :] = ta[pl.ds(k * (width * ny) + y, width, stride=ny), :]
        for copy in strip(k):
            copy.start()

    step(tb, cb, emit_second, pieces, strip_done)
    second = send_x(1, ta)
    extra_rows = [(hi_rows + side * gcount + g, side, g) for side in range(2) for g in range(gcount)]
    for k in range(0, bond_rows, 8):
        q = other[k : k + 8, :]
        h, l = q // LANES, q % LANES
        for ch in range(3):
            d = pq[ch, k : k + 8, :]
            g = table_pick([(n, ghosts[side, ch * gcount + i : ch * gcount + i + 1, :]) for n, side, i in extra_rows], h, l, zero8)
            pq[ch, k : k + 8, :] = d + g
    d = [pq[ch] for ch in range(3)]
    dist = jnp.sqrt(d[0] * d[0] + d[1] * d[1] + d[2] * d[2])
    g = gap[...]
    base = (1.0 - snapped[...].astype(f32)) / jnp.maximum(dist, 0.3)
    p = base * (dist - g)
    q = base * (-0.1 * g)
    for ch in range(3):
        pq[ch] = p * d[ch]
        pq[3 + ch] = q * d[ch]
    own[0] = scatter(rows_of(0))
    for copy in second:
        copy.wait()

    def strip_taken(k, carry):
        for copy in strip(k):
            copy.wait()
        return carry

    lax.fori_loop(0, pieces, strip_taken, 0)
    edge(ca, ta)
    rim(stage[1, 0], stage[1, 1], ta, ca)

    def emit_third(x, t):
        where = pl.ds(pl.multiple_of(x * ny, ny), ny)
        temp_out[where, :] = t + src[where, :]

    step(ta, ca, emit_third)
    store = pltpu.make_async_copy(temp_out, temp_hbm_out, local.at[11])
    store.start()

    for k in range(rows // LANES):
        b = temp_out[k * LANES : (k + 1) * LANES, :].T
        hi = b.astype(bf16)
        tt[0:LANES, k * LANES : (k + 1) * LANES] = hi
        tt[LANES : 2 * LANES, k * LANES : (k + 1) * LANES] = (b - hi.astype(f32)).astype(bf16)
    zs = lax.broadcasted_iota(i32, (LANES, LANES), 0).astype(f32)

    def look(slots):
        cols = []
        for n in slots:
            for h in range(per):
                r = row[pl.ds(n * per + h, 1), :]
                parts = []
                for k in range(rows // 256):
                    q = r - 256.0 * k
                    parts.append(hot(jnp.where((q >= 0) & (q < 256), q, -1.0), iota))
                cols.append(jnp.concatenate(parts, axis=0))
        got = jnp.dot(tt[...], jnp.concatenate(cols, axis=1), preferred_element_type=f32)
        got = got[:LANES] + got[LANES:]
        for i, n in enumerate(slots):
            for h in range(per):
                u = i * per + h
                z = zed[pl.ds(n * per + h, 1), :]
                v = jnp.where(zs == z, got[:, u * LANES : (u + 1) * LANES], 0.0)
                picked[n, h : h + 1, :] = jnp.sum(v, axis=0, keepdims=True)

    def look_below(k, carry):
        look((crosses + 2 * k, crosses + 2 * k + 1))
        return carry

    lax.fori_loop(0, crosses // 2, look_below, 0)
    hand = remote(picked.at[pl.ds(crosses, crosses)], far, hsend.at[11], hrecv.at[11], (below, s))
    hand.start()

    chips_y = crosses // 4

    def pair(k):
        far_x = 1 - k // chips_y
        y = lax.rem(s // 4 + lax.rem(k, chips_y) + 1, chips_y)
        x = lax.rem(lax.rem(s // 2, 2) + far_x, 2)
        chip = 4 * y + 2 * x
        return chip + 1 - lax.rem(s, 2), chip + lax.rem(s, 2)

    def merge(j):
        m = row[pl.ds(j * per, per), :] < 0
        return jnp.where(m, far[pl.ds(j, 1)].reshape(per, LANES), picked[pl.ds(j, 1)].reshape(per, LANES))

    def back_to(j):
        ret[pl.ds(j, 1)] = merge(j).reshape(1, per, LANES)
        remote(ret.at[j], back.at[s], bs.at[j], br.at[s], (c, j)).start()

    held = 3

    def look_first(k, carry):
        look(pair(k))
        return carry

    lax.fori_loop(0, held, look_first, 0)
    hand.wait()

    def send_held(k, carry):
        a, b = pair(k)
        back_to(a)
        back_to(b)
        return carry

    lax.fori_loop(0, held, send_held, 0)

    def look_then(k, carry):
        a, b = pair(k)
        look((a, b))
        back_to(a)
        back_to(b)
        return carry

    lax.fori_loop(held, crosses // 2 - 1, look_then, 0)
    a, b = pair(crosses // 2 - 1)
    look((a, b))
    back_to(a)
    back[pl.ds(s, 1)] = merge(s).reshape(1, per, LANES)

    def back_same(k, carry):
        j = lax.rem(s + k, crosses)
        remote(ret.at[j], back.at[j], bs.at[j], br.at[j], (c, j)).wait()
        return carry

    lax.fori_loop(1, crosses, back_same, 0)
    warm = jnp.concatenate([back[j] for j in range(crosses)], axis=0)
    table = [(r, warm[r : r + 1]) for r in range(hi_rows)]
    gtemp_send[...] = table_pick(table, eh, el, zero8)[:gcount]
    copies = [
        remote(gtemp_send, gtemp.at[0], gs.at[0], gr.at[0], (above, s)),
        remote(gtemp_send, gtemp.at[1], gs.at[1], gr.at[1], (below, s)),
    ]
    for copy in copies:
        copy.start()
    partner = []
    for k in range(0, bond_rows, 8):
        q = other[k : k + 8, :]
        partner.append(table_pick(table, q // LANES, q % LANES, zero8))
    own[1] = scatter(rows_of(3))
    for copy in copies:
        copy.wait()
    for n, k in enumerate(range(0, bond_rows, 8)):
        q = other[k : k + 8, :]
        t = table_pick(
            [(m, gtemp[side, i : i + 1, :]) for m, side, i in extra_rows], q // LANES, q % LANES, partner[n]
        )
        for ch in range(3):
            pq[3 + ch, k : k + 8, :] = pq[3 + ch, k : k + 8, :] * t
    force_out[...] = own[0] + scatter(rows_of(3)) + jnp.concatenate([warm] * 3, axis=0) * own[1]
    store.wait()


def update_kernel(
    temp, force_hbm, pos_hbm, vel_hbm, temp_out, pos_out, vel_out, held, force, pos, vel, sems, small
):
    parts = held.shape[0]
    rows = held.shape[1]
    first = [
        pltpu.make_async_copy(a, b, small.at[n])
        for n, (a, b) in enumerate(((force_hbm, force), (pos_hbm, pos), (vel_hbm, vel)))
    ]
    where = [pl.ds(n * rows, rows) for n in range(parts)]
    loads = [pltpu.make_async_copy(temp.at[w], held.at[n], sems.at[0, n]) for n, w in enumerate(where)]
    stores = [pltpu.make_async_copy(held.at[n], temp_out.at[w], sems.at[1, n]) for n, w in enumerate(where)]
    for load in first + loads:
        load.start()
    for load in first:
        load.wait()
    hi_rows = pos.shape[1] // LANES
    for r in range(hi_rows):
        at = slice(r * LANES, (r + 1) * LANES)
        v = vel[:, at] + 0.5 * force[pl.ds(r, 3, stride=hi_rows), :]
        vel[:, at] = v
        pos[:, at] = pos[:, at] + 0.5 * v
    last = [pltpu.make_async_copy(vel, vel_out, small.at[3]), pltpu.make_async_copy(pos, pos_out, small.at[4])]
    for store in last:
        store.start()
    for load, store in zip(loads, stores):
        load.wait()
        store.start()
    for store in stores + last:
        store.wait()


def per_device(
    cuts, crosses, temp, kappa, locator, gain, mark, pos, vel, acted, other, gap, snapped, exported
):
    nx, ny, nz = temp.shape
    rows = nx * ny
    flat = lambda a: a.reshape(-1, LANES)
    loc, gain, mark = flat(locator), flat(gain), flat(mark)
    acted, other, gap, snapped, exported = map(flat, (acted, other, gap, snapped, exported))
    hi_rows = loc.shape[0]
    per = hi_rows // crosses
    gcount = exported.shape[0]
    bonds = acted.shape[0]
    lr = 2 * crosses * per
    shape = jax.ShapeDtypeStruct
    dma = pltpu.SemaphoreType.DMA
    vm = pltpu.VMEM
    plane = (2, 2, nx, nz)
    padded = (rows + 2 * ny, nz)
    arrays = (
        loc, gain, mark, exported, pos, temp.reshape(rows, nz), kappa.reshape(rows, nz), acted, other, gap, snapped
    )
    temp_new, force = pl.pallas_call(
        functools.partial(kernel, cuts, crosses),
        out_shape=(shape((rows, nz), f32), shape((3 * hi_rows, LANES), f32)),
        in_specs=[ANY] * 11,
        out_specs=(ANY, VMEM),
        scratch_shapes=[vm(a.shape, a.dtype) for a in arrays]
        + [
            vm((rows, nz), f32),
            vm((2 * crosses, 2 * per, LANES), f32),
            vm((crosses, 2 * per, LANES), f32),
            vm((2, 2, ny, nz), f32),
            vm(plane, f32),
            vm(plane, f32),
            vm((2, 3 * gcount, LANES), f32),
            vm((3 * gcount, LANES), f32),
            vm((lr, LANES), f32),
            vm((lr, LANES), f32),
            vm((lr, LANES), f32),
            vm((2 * LANES, lr * LANES), bf16),
            vm((LANES, bonds * LANES), bf16),
            vm((256, LANES), bf16),
            vm((rows, nz), f32),
            vm((rows, nz), f32),
            vm(padded, f32),
            vm(padded, f32),
            vm(padded, f32),
            vm(padded, f32),
            vm(plane, f32),
            vm((2, nx, nz), f32),
            vm((2 * nz, rows), bf16),
            vm((2 * crosses, per, LANES), f32),
            vm((crosses, per, LANES), f32),
            vm((crosses, per, LANES), f32),
            vm((crosses, per, LANES), f32),
            vm(plane, f32),
            vm((gcount, LANES), f32),
            vm((2, gcount, LANES), f32),
            vm((6, bonds, LANES), f32),
            vm((2, 3 * hi_rows, LANES), f32),
            dma((crosses,)),
            dma((crosses,)),
            dma((12,)),
            dma((12,)),
            dma((4,)),
            dma((4,)),
            dma((2,)),
            dma((2,)),
            dma((8,)),
            dma((8,)),
            dma((crosses,)),
            dma((crosses,)),
            dma((2,)),
            dma((2,)),
            dma((12,)),
        ],
        compiler_params=pltpu.CompilerParams(collective_id=0, has_side_effects=True),
        name="substeps",
    )(*arrays)
    temp_new, pos_new, vel_new = pl.pallas_call(
        update_kernel,
        out_shape=(shape((rows, nz), f32), shape(pos.shape, f32), shape(vel.shape, f32)),
        in_specs=[ANY] * 4,
        out_specs=(ANY,) * 3,
        scratch_shapes=[
            vm((4, rows // 4, nz), f32),
            vm(force.shape, f32),
            vm(pos.shape, f32),
            vm(vel.shape, f32),
            dma((2, 4)),
            dma((5,)),
        ],
        name="update",
    )(temp_new, force, pos, vel)
    return temp_new.reshape(nx, ny, nz), pos_new, vel_new


def solution(mesh):
    both = P(("cut", "cross"))
    return jax.shard_map(
        functools.partial(per_device, mesh.shape["cut"], mesh.shape["cross"]),
        mesh=mesh,
        in_specs=(P("cut", "cross", None),) * 2
        + (both,) * 3
        + (P(None, ("cut", "cross")),) * 2
        + (both,) * 5,
        out_specs=(P("cut", "cross", None), P(None, ("cut", "cross")), P(None, ("cut", "cross"))),
        check_vma=False,
    )
```

```python
import functools

import jax
import jax.numpy as jnp
from jax import lax
from jax.experimental import pallas as pl
from jax.experimental.pallas import tpu as pltpu
from jax.sharding import PartitionSpec as P

f32 = jnp.float32
bf16 = jnp.bfloat16
i32 = jnp.int32
MESH = pl.DeviceIdType.MESH
NT = (((1,), (1,)), ((), ()))
LANES = 128
VMEM = pl.BlockSpec(memory_space=pltpu.VMEM)
ANY = pl.BlockSpec(memory_space=pl.ANY)


def stack(tile, count):
    return jnp.concatenate([tile] * count, axis=0)


def rows16(row):
    return jnp.broadcast_to(row, (16, row.shape[1])).astype(bf16)


def hot(row, iota):
    r = stack(rows16(row), iota.shape[0] // 16)
    return jnp.where(iota == r, jnp.ones_like(iota), jnp.zeros_like(iota))


def spread(row, val, iota):
    r = stack(rows16(row), iota.shape[0] // 16)
    v = stack(rows16(val), iota.shape[0] // 16)
    return jnp.where(iota == r, v, jnp.zeros_like(iota))


def iota_rows(count):
    return lax.broadcasted_iota(i32, (count, LANES), 0).astype(f32).astype(bf16)


def high(v):
    return v.astype(bf16).astype(f32)


def conduct(t):
    return 0.5 + 1.0 / (1.0 + t * t)


def peers(cuts, crosses):
    c, s = lax.axis_index("cut"), lax.axis_index("cross")
    below, above = lax.rem(c + cuts - 1, cuts), lax.rem(c + 1, cuts)
    return c, s, below, above


def greet(cuts, crosses):
    c, s, below, above = peers(cuts, crosses)
    barrier = pltpu.get_barrier_semaphore()

    for device in ((below, s), (above, s)):
        pl.semaphore_signal(barrier, inc=1, device_id=device, device_id_type=MESH)

    def other(k, carry):
        j = lax.rem(s + k, crosses)
        pl.semaphore_signal(barrier, inc=1, device_id=(c, j), device_id_type=MESH)
        return carry

    lax.fori_loop(1, crosses, other, 0)


def await_all(crosses):
    pl.semaphore_wait(pltpu.get_barrier_semaphore(), crosses + 1)


def remote(src, dst, send, recv, device):
    return pltpu.make_async_remote_copy(
        src_ref=src, dst_ref=dst, send_sem=send, recv_sem=recv, device_id=device, device_id_type=MESH
    )


def lane_pick(row, index):
    return jnp.take_along_axis(row, index, axis=1, mode="promise_in_bounds")


def table_pick(rows, high_index, low_index, start):
    out = start
    for number, row in rows:
        wide = jnp.broadcast_to(row, low_index.shape)
        out = jnp.where(high_index == number, lane_pick(wide, low_index), out)
    return out


def kernel(
    cuts, crosses, *refs
):
    inputs, (temp_hbm_out, force_out) = refs[:11], refs[11:13]
    loc, gain, mark, exported, pos, temp, kappa, acted, other, gap, snapped = refs[13:24]
    (
    temp_out, lists, send_lists, hx, hy, ysend0, ghosts, gsend,
    row, zed, val, sp, ohl, big, d1, src, ta, tb, ca, cb, ysend, flux, tt, picked, far, ret, back, stage,
    gtemp_send, gtemp, pq, own,
    send_sem, recv_sem, hsend, hrecv, xs, xr, ys, yr, zs_sem, zr_sem, bs, br, gs, gr, local,
    ) = refs[24:]
    c, s, below, above = peers(cuts, crosses)
    left, right = lax.rem(s + crosses - 1, crosses), lax.rem(s + 1, crosses)
    loads = [pltpu.make_async_copy(a, b, local.at[n]) for n, (a, b) in enumerate(zip(inputs, refs[13:24]))]
    for load in loads:
        load.start()
    greet(cuts, crosses)
    rows = temp.shape[0]
    nx = hy.shape[2]
    ny = rows // nx
    cells = rows * LANES
    hi_rows = loc.shape[0]
    per = hi_rows // crosses
    gcount = exported.shape[0]
    bond_rows = acted.shape[0]

    for load in loads[:3]:
        load.wait()
    w = loc[...].astype(f32)
    power = mark[...].astype(f32) * gain[...] * 0.5
    for j in range(crosses):
        send_lists[j, 0:per, :] = w[j * per : (j + 1) * per]
        send_lists[j, per : 2 * per, :] = power[j * per : (j + 1) * per]
    await_all(crosses)

    chips_y = crosses // 4

    def pair(k):
        far_x = 1 - k // chips_y
        y = lax.rem(s // 4 + lax.rem(k, chips_y) + 1, chips_y)
        x = lax.rem(lax.rem(s // 2, 2) + far_x, 2)
        chip = 4 * y + 2 * x
        return chip + 1 - lax.rem(s, 2), chip + lax.rem(s, 2)

    def send_to(j):
        remote(send_lists.at[j], lists.at[s], send_sem.at[j], recv_sem.at[s], (c, j)).start()

    def send_same(k, carry):
        a, b = pair(k)
        send_to(a)
        send_to(b)
        return carry

    lax.fori_loop(0, crosses // 2 - 1, send_same, 0)
    send_to(pair(crosses // 2 - 1)[0])
    lists[pl.ds(s, 1)] = send_lists[pl.ds(s, 1)]
    for load in loads[3:]:
        load.wait()
    for a, ref in enumerate((temp, kappa)):
        ysend0[a, 0] = ref[pl.ds(0, nx, stride=ny), :]
        ysend0[a, 1] = ref[pl.ds(ny - 1, nx, stride=ny), :]
    early = []
    for a, ref in enumerate((temp, kappa)):
        early.append(remote(ysend0.at[a, 1], hy.at[a, 0], hsend.at[4 * a + 2], hrecv.at[4 * a + 2], (c, right)))
        early.append(remote(ysend0.at[a, 0], hy.at[a, 1], hsend.at[4 * a + 3], hrecv.at[4 * a + 3], (c, left)))
        early.append(remote(ref.at[pl.ds(rows - ny, ny)], hx.at[a, 0], hsend.at[4 * a], hrecv.at[4 * a], (above, s)))
        early.append(remote(ref.at[pl.ds(0, ny)], hx.at[a, 1], hsend.at[4 * a + 1], hrecv.at[4 * a + 1], (below, s)))
    for copy in early:
        copy.start()
    e8 = jnp.concatenate([exported[...]] * (8 // gcount), axis=0)
    eh, el = e8 // LANES, e8 % LANES
    zero8 = jnp.zeros((8, LANES), f32)

    def row_of(ref, ch, r):
        return ref[ch : ch + 1, pl.ds(pl.multiple_of(r * LANES, LANES), LANES)]

    def export_rows(r, acc):
        return tuple(table_pick([(r, row_of(pos, ch, r))], eh, el, acc[ch]) for ch in range(3))

    acc = lax.fori_loop(0, hi_rows, export_rows, (zero8,) * 3, unroll=8)
    for ch in range(3):
        gsend[ch * gcount : (ch + 1) * gcount, :] = acc[ch][:gcount]

    late = [
        remote(gsend, ghosts.at[0], hsend.at[8], hrecv.at[8], (above, s)),
        remote(gsend, ghosts.at[1], hsend.at[9], hrecv.at[9], (below, s)),
    ]
    for copy in late:
        copy.start()
    early += late

    group = 16

    def differences(k, carry):
        where = pl.ds(pl.multiple_of(k * group, group), group)
        qa, qb = acted[where, :], other[where, :]
        index = [(q[h : h + 8] // LANES, q[h : h + 8] % LANES) for q in (qa, qb) for h in range(0, group, 8)]

        def one(r, acc):
            out = []
            for ch in range(3):
                wide = jnp.broadcast_to(row_of(pos, ch, r), (8, LANES))
                for n, (h, l) in enumerate(index):
                    out.append(jnp.where(h == r, lane_pick(wide, l), acc[ch * len(index) + n]))
            return tuple(out)

        acc = lax.fori_loop(0, hi_rows, one, (zero8,) * (3 * len(index)), unroll=4)
        half = len(index) // 2
        for ch in range(3):
            for n in range(half):
                first, second = acc[ch * len(index) + n], acc[ch * len(index) + half + n]
                pq[ch, pl.ds(pl.multiple_of(k * group + 8 * n, 8), 8), :] = second - first
        return carry

    block = 16 * ny

    def begin(b, carry):
        where = pl.ds(pl.multiple_of(b * block, block), block)
        there = pl.ds(pl.multiple_of(b * block + ny, ny), block)
        t = temp[where, :]
        ta[there, :] = t
        ca[there, :] = kappa[where, :] * conduct(t)
        return carry

    lax.fori_loop(0, rows // block, begin, 0)
    big[...] = iota_rows(256)
    iota = big[...]
    small = iota[:LANES]

    def lows(k, carry):
        for u in range(4):
            r = k * 4 + u
            a = (acted[pl.ds(r, 1), :] % LANES).astype(f32)
            ohl[:, pl.ds(pl.multiple_of(r * LANES, LANES), LANES)] = hot(a, small)
        return carry

    lax.fori_loop(0, bond_rows // 4, lows, 0)
    lax.fori_loop(0, bond_rows // group // 2, differences, 0)

    def take_same(k, carry):
        j = lax.rem(s + k, crosses)
        remote(send_lists.at[j], lists.at[j], send_sem.at[j], recv_sem.at[j], (c, j)).wait()
        return carry

    lax.fori_loop(1, crosses, take_same, 0)
    relay = remote(
        lists.at[pl.ds(0, crosses)], lists.at[pl.ds(crosses, crosses)], hsend.at[10], hrecv.at[10], (above, s)
    )
    relay.start()

    count = row.shape[0]

    def build(k, carry):
        for u in range(8):
            r = k * 8 + u
            z = zed[pl.ds(r, 1), :]
            v = val[pl.ds(r, 1), :]
            hi = high(v)
            where = pl.ds(pl.multiple_of(r * LANES, LANES), LANES)
            sp[0:LANES, where] = spread(z, hi, small)
            sp[LANES : 2 * LANES, where] = spread(z, v - hi, small)
        return carry

    def decode(half):
        for b in range(half * crosses, (half + 1) * crosses):
            q = lists[b, 0:per, :].astype(i32)
            here = (q >= cells) == (half == 1)
            q = q & (cells - 1)
            row[b * per : (b + 1) * per, :] = jnp.where(here, q // LANES, -1).astype(f32)
            zed[b * per : (b + 1) * per, :] = (q % LANES).astype(f32)
            val[b * per : (b + 1) * per, :] = jnp.where(here, lists[b, per : 2 * per, :], 0.0)
        lax.fori_loop(half * count // 16, (half + 1) * count // 16, build, 0)
        where = slice(half * count // 2, (half + 1) * count // 2)
        r_all = row[where, :].astype(i32)
        y = r_all & (ny - 1)
        y = jnp.where(y == 0, 0, jnp.where(y == ny - 1, 1, y + 1))
        val[where, :] = jnp.where(r_all < 0, -1, y * nx + r_all // ny).astype(f32)

    tall, depth = 512, 16

    def deposit(m, begin, end, acc):
        first = m * float(tall)

        def inner(k, acc):
            pieces = []
            for h in range(depth):
                r = val[pl.ds(k * depth + h, 1), :] - first
                parts = []
                for g in range(tall // 256):
                    q = r - 256.0 * g
                    parts.append(hot(jnp.where((q >= 0) & (q < 256), q, -1.0), iota))
                pieces.append(jnp.concatenate(parts, axis=0))
            where = pl.ds(pl.multiple_of(k * (depth * LANES), depth * LANES), depth * LANES)
            return acc + lax.dot_general(
                jnp.concatenate(pieces, axis=1), sp[:, where], NT, preferred_element_type=f32
            )

        return lax.fori_loop(begin, end, inner, acc)

    planes = tall // nx
    nothing = jnp.zeros((tall, 2 * LANES), f32)
    steps = count // depth
    decode(0)
    got = deposit(0.0, 0, steps // 2, nothing)
    relay.wait()
    decode(1)
    got = deposit(0.0, steps // 2, steps, got)
    got = got[:, :LANES] + got[:, LANES:]
    for n, y in enumerate((0, ny - 1) + tuple(range(1, planes - 1))):
        src[pl.ds(y, nx, stride=ny), :] = got[n * nx : (n + 1) * nx]

    for copy in early:
        copy.wait()

    final = crosses - 1
    low_edge, high_edge = s == 0, s == final
    sub = lax.broadcasted_iota(i32, (ny, LANES), 0)
    lane = lax.broadcasted_iota(i32, (ny, LANES), 1)

    def edge(cref, tref):
        cref[0:ny, :] = hx[1, 0] * conduct(tref[0:ny, :])
        cref[rows + ny : rows + 2 * ny, :] = hx[1, 1] * conduct(tref[rows + ny : rows + 2 * ny, :])

    def rim(planes, tref, cref, start=0, size=nx):
        part = pl.ds(start, size)
        for n, (off, at) in enumerate(((low_edge, ny), (high_edge, 2 * ny - 1))):
            t = jnp.where(off, 0.0, planes[n, part, :])
            cc = jnp.where(off, 0.0, hy[1, n, part, :]) * conduct(t)
            here = pl.ds(start * ny + at, size, stride=ny)
            t0 = tref[here, :]
            c0 = cref[here, :]
            flux[n, part, :] = (cc + c0) * ((t0 - t) if n == 0 else (t - t0))

    many = 32
    pieces = nx // many

    def step(tin, cin, emit, done=None):
        def piece(k, carry):
            first = k * (many * ny)
            at0, at1 = pl.ds(pl.multiple_of(first, ny), ny), pl.ds(pl.multiple_of(first + ny, ny), ny)
            before = (cin[at0, :] + cin[at1, :]) * (tin[at1, :] - tin[at0, :])
            for u in range(many):
                x = k * many + u
                here = pl.ds(pl.multiple_of(x * ny + ny, ny), ny)
                ahead = pl.ds(pl.multiple_of(x * ny + 2 * ny, ny), ny)
                t0, c0 = tin[here, :], cin[here, :]
                t1, c1 = tin[ahead, :], cin[ahead, :]
                fx = (c0 + c1) * (t1 - t0)
                at = pl.ds(x, 1)
                north, south = pl.ds(x * ny + ny + 1, ny), pl.ds(x * ny + ny - 1, ny)
                fy = jnp.where(sub == ny - 1, flux[1, at, :], (c0 + cin[north, :]) * (tin[north, :] - t0))
                fy0 = jnp.where(sub == 0, flux[0, at, :], (c0 + cin[south, :]) * (t0 - tin[south, :]))
                ct = c0 * t0
                tz, cz = pltpu.roll(t0, LANES - 1, 1), pltpu.roll(c0, LANES - 1, 1)
                tw, cw = pltpu.roll(t0, 1, 1), pltpu.roll(c0, 1, 1)
                fz = jnp.where(lane == LANES - 1, -ct, (c0 + cz) * (tz - t0))
                fz0 = jnp.where(lane == 0, ct, (c0 + cw) * (t0 - tw))
                emit(x, t0 + 0.5 * (((fx - before) + (fy - fy0)) + (fz - fz0)))
                before = fx
            if done is not None:
                done(k)
            return carry

        return piece

    def inside(piece):
        lax.fori_loop(1, pieces - 1, piece, 0)

    def outside(piece):
        lax.fori_loop(0, 2, lambda n, carry: piece(n * (pieces - 1), carry), 0)

    def send_x(k, tref):
        copies = [
            remote(tref.at[pl.ds(rows, ny)], tref.at[pl.ds(0, ny)], xs.at[2 * k], xr.at[2 * k], (above, s)),
            remote(
                tref.at[pl.ds(ny, ny)], tref.at[pl.ds(rows + ny, ny)], xs.at[2 * k + 1], xr.at[2 * k + 1], (below, s)
            ),
        ]
        for copy in copies:
            copy.start()
        return copies

    def send_y():
        copies = [
            remote(ysend.at[0, 1], stage.at[0, 0], ys.at[0], yr.at[0], (c, right)),
            remote(ysend.at[0, 0], stage.at[0, 1], ys.at[1], yr.at[1], (c, left)),
        ]
        for copy in copies:
            copy.start()
        return copies

    ta[0:ny, :] = hx[0, 0]
    ta[rows + ny : rows + 2 * ny, :] = hx[0, 1]
    edge(ca, ta)
    rim(hy.at[0], ta, ca)

    def emit_first(x, t):
        d1[pl.ds(pl.multiple_of(x * ny, ny), ny), :] = t

    lax.fori_loop(0, pieces, step(ta, ca, emit_first), 0)
    for n, y in enumerate((0, ny - 1)):
        ysend[0, n] = d1[pl.ds(y, nx, stride=ny), :] + src[pl.ds(y, nx, stride=ny), :]
    first = send_y()

    def others(m, carry):
        got = deposit(m.astype(f32), 0, steps, nothing)
        got = got[:, :LANES] + got[:, LANES:]
        for n in range(planes):
            src[pl.ds(m * planes + (n - 1), nx, stride=ny), :] = got[n * nx : (n + 1) * nx]
        return carry

    lax.fori_loop(1, rows // tall, others, 0)

    def finish(b, carry):
        where = pl.ds(pl.multiple_of(b * block, block), block)
        there = pl.ds(pl.multiple_of(b * block + ny, ny), block)
        t = d1[where, :] + src[where, :]
        tb[there, :] = t
        cb[there, :] = kappa[where, :] * conduct(t)
        return carry

    lax.fori_loop(0, rows // block, finish, 0)
    sides = send_x(0, tb)

    lax.fori_loop(bond_rows // group // 2, bond_rows // group, differences, 0)
    iota32 = iota[:hi_rows]

    turn = 32

    def scatter(values):
        def body(k, acc):
            lhs = []
            for u in range(turn):
                r = k * turn + u
                h = (acted[pl.ds(r, 1), :] // LANES).astype(f32)
                tops, bottoms = [], []
                for v in values(r):
                    top = high(v)
                    tops.append(spread(h, top, iota32))
                    bottoms.append(spread(h, v - top, iota32))
                lhs.append(jnp.concatenate(tops + bottoms, axis=0))
            where = pl.ds(pl.multiple_of(k * (turn * LANES), turn * LANES), turn * LANES)
            return acc + lax.dot_general(
                jnp.concatenate(lhs, axis=1), ohl[:, where], NT, preferred_element_type=f32
            )

        n = 3 * hi_rows
        acc = lax.fori_loop(0, bond_rows // turn, body, jnp.zeros((2 * n, LANES), f32))
        return acc[:n] + acc[n:]

    def rows_of(lo):
        return lambda r: [pq[lo + ch, pl.ds(r, 1), :] for ch in range(3)]

    def emit_second(x, t):
        where = pl.ds(pl.multiple_of(x * ny, ny), ny)
        here = pl.ds(pl.multiple_of(x * ny + ny, ny), ny)
        t = t + src[where, :]
        ta[here, :] = t
        ca[here, :] = kappa[where, :] * conduct(t)

    width = nx // pieces

    def strip(k):
        at = pl.ds(pl.multiple_of(k * width, width), width)
        return [
            remote(ysend.at[1, 1, at], stage.at[1, 0, at], zs_sem.at[k], zr_sem.at[k], (c, right)),
            remote(ysend.at[1, 0, at], stage.at[1, 1, at], zs_sem.at[pieces + k], zr_sem.at[pieces + k], (c, left)),
        ]

    def strip_done(k):
        at = pl.ds(pl.multiple_of(k * width, width), width)
        for n, y in enumerate((ny, 2 * ny - 1)):
            ysend[1, n, at, :] = ta[pl.ds(k * (width * ny) + y, width, stride=ny), :]
        for copy in strip(k):
            copy.start()

    for copy in first:
        copy.wait()
    rim(stage.at[0], tb, cb)
    second_step = step(tb, cb, emit_second, strip_done)
    inside(second_step)
    for copy in sides:
        copy.wait()
    edge(cb, tb)
    outside(second_step)
    second = send_x(1, ta)
    extra_rows = [(hi_rows + side * gcount + g, side, g) for side in range(2) for g in range(gcount)]
    for k in range(0, bond_rows, 8):
        q = other[k : k + 8, :]
        h, l = q // LANES, q % LANES
        for ch in range(3):
            d = pq[ch, k : k + 8, :]
            g = table_pick([(n, ghosts[side, ch * gcount + i : ch * gcount + i + 1, :]) for n, side, i in extra_rows], h, l, zero8)
            pq[ch, k : k + 8, :] = d + g
    d = [pq[ch] for ch in range(3)]
    dist = jnp.sqrt(d[0] * d[0] + d[1] * d[1] + d[2] * d[2])
    g = gap[...]
    base = (1.0 - snapped[...].astype(f32)) / jnp.maximum(dist, 0.3)
    p = base * (dist - g)
    q = base * (-0.1 * g)
    for ch in range(3):
        pq[ch] = p * d[ch]
        pq[3 + ch] = q * d[ch]
    own[0] = scatter(rows_of(0))

    def strip_taken(k, carry):
        for copy in strip(k):
            copy.wait()
        rim(stage.at[1], ta, ca, k * width, width)
        return carry

    def emit_third(x, t):
        where = pl.ds(pl.multiple_of(x * ny, ny), ny)
        temp_out[where, :] = t + src[where, :]

    third_step = step(ta, ca, emit_third)
    lax.fori_loop(1, pieces - 1, strip_taken, 0)
    inside(third_step)
    for copy in second:
        copy.wait()
    edge(ca, ta)
    lax.fori_loop(0, 2, lambda n, carry: strip_taken(n * (pieces - 1), carry), 0)
    outside(third_step)
    store = pltpu.make_async_copy(temp_out, temp_hbm_out, local.at[11])
    store.start()

    for k in range(rows // LANES):
        b = temp_out[k * LANES : (k + 1) * LANES, :].T
        hi = b.astype(bf16)
        tt[0:LANES, k * LANES : (k + 1) * LANES] = hi
        tt[LANES : 2 * LANES, k * LANES : (k + 1) * LANES] = (b - hi.astype(f32)).astype(bf16)
    zs = lax.broadcasted_iota(i32, (LANES, LANES), 0).astype(f32)

    def look(slots):
        cols = []
        for n in slots:
            for h in range(per):
                r = row[pl.ds(n * per + h, 1), :]
                parts = []
                for k in range(rows // 256):
                    q = r - 256.0 * k
                    parts.append(hot(jnp.where((q >= 0) & (q < 256), q, -1.0), iota))
                cols.append(jnp.concatenate(parts, axis=0))
        got = jnp.dot(tt[...], jnp.concatenate(cols, axis=1), preferred_element_type=f32)
        got = got[:LANES] + got[LANES:]
        for i, n in enumerate(slots):
            for h in range(per):
                u = i * per + h
                z = zed[pl.ds(n * per + h, 1), :]
                v = jnp.where(zs == z, got[:, u * LANES : (u + 1) * LANES], 0.0)
                picked[n, h : h + 1, :] = jnp.sum(v, axis=0, keepdims=True)

    def look_below(k, carry):
        look((crosses + 2 * k, crosses + 2 * k + 1))
        return carry

    lax.fori_loop(0, crosses // 2, look_below, 0)
    hand = remote(picked.at[pl.ds(crosses, crosses)], far, hsend.at[11], hrecv.at[11], (below, s))
    hand.start()

    def merge(j):
        m = row[pl.ds(j * per, per), :] < 0
        return jnp.where(m, far[pl.ds(j, 1)].reshape(per, LANES), picked[pl.ds(j, 1)].reshape(per, LANES))

    def back_to(j):
        ret[pl.ds(j, 1)] = merge(j).reshape(1, per, LANES)
        remote(ret.at[j], back.at[s], bs.at[j], br.at[s], (c, j)).start()

    held = 3

    def look_first(k, carry):
        look(pair(k))
        return carry

    lax.fori_loop(0, held, look_first, 0)
    hand.wait()

    def send_held(k, carry):
        a, b = pair(k)
        back_to(a)
        back_to(b)
        return carry

    lax.fori_loop(0, held, send_held, 0)

    def look_then(k, carry):
        a, b = pair(k)
        look((a, b))
        back_to(a)
        back_to(b)
        return carry

    lax.fori_loop(held, crosses // 2 - 1, look_then, 0)
    a, b = pair(crosses // 2 - 1)
    look((a, b))
    back_to(a)
    back[pl.ds(s, 1)] = merge(s).reshape(1, per, LANES)

    def back_same(k, carry):
        j = lax.rem(s + k, crosses)
        remote(ret.at[j], back.at[j], bs.at[j], br.at[j], (c, j)).wait()
        return carry

    lax.fori_loop(1, crosses, back_same, 0)
    warm = jnp.concatenate([back[j] for j in range(crosses)], axis=0)
    table = [(r, warm[r : r + 1]) for r in range(hi_rows)]
    gtemp_send[...] = table_pick(table, eh, el, zero8)[:gcount]
    copies = [
        remote(gtemp_send, gtemp.at[0], gs.at[0], gr.at[0], (above, s)),
        remote(gtemp_send, gtemp.at[1], gs.at[1], gr.at[1], (below, s)),
    ]
    for copy in copies:
        copy.start()
    partner = []
    for k in range(0, bond_rows, 8):
        q = other[k : k + 8, :]
        partner.append(table_pick(table, q // LANES, q % LANES, zero8))
    own[1] = scatter(rows_of(3))
    for copy in copies:
        copy.wait()
    for n, k in enumerate(range(0, bond_rows, 8)):
        q = other[k : k + 8, :]
        t = table_pick(
            [(m, gtemp[side, i : i + 1, :]) for m, side, i in extra_rows], q // LANES, q % LANES, partner[n]
        )
        for ch in range(3):
            pq[3 + ch, k : k + 8, :] = pq[3 + ch, k : k + 8, :] * t
    force_out[...] = own[0] + scatter(rows_of(3)) + jnp.concatenate([warm] * 3, axis=0) * own[1]
    store.wait()


def update_kernel(
    temp, force_hbm, pos_hbm, vel_hbm, temp_out, pos_out, vel_out, held, force, pos, vel, sems, small
):
    parts = held.shape[0]
    rows = held.shape[1]
    first = [
        pltpu.make_async_copy(a, b, small.at[n])
        for n, (a, b) in enumerate(((force_hbm, force), (pos_hbm, pos), (vel_hbm, vel)))
    ]
    where = [pl.ds(n * rows, rows) for n in range(parts)]
    loads = [pltpu.make_async_copy(temp.at[w], held.at[n], sems.at[0, n]) for n, w in enumerate(where)]
    stores = [pltpu.make_async_copy(held.at[n], temp_out.at[w], sems.at[1, n]) for n, w in enumerate(where)]
    for load in first + loads:
        load.start()
    for load in first:
        load.wait()
    hi_rows = pos.shape[1] // LANES
    for r in range(hi_rows):
        at = slice(r * LANES, (r + 1) * LANES)
        v = vel[:, at] + 0.5 * force[pl.ds(r, 3, stride=hi_rows), :]
        vel[:, at] = v
        pos[:, at] = pos[:, at] + 0.5 * v
    last = [pltpu.make_async_copy(vel, vel_out, small.at[3]), pltpu.make_async_copy(pos, pos_out, small.at[4])]
    for store in last:
        store.start()
    for load, store in zip(loads, stores):
        load.wait()
        store.start()
    for store in stores + last:
        store.wait()


def per_device(
    cuts, crosses, temp, kappa, locator, gain, mark, pos, vel, acted, other, gap, snapped, exported
):
    nx, ny, nz = temp.shape
    rows = nx * ny
    flat = lambda a: a.reshape(-1, LANES)
    loc, gain, mark = flat(locator), flat(gain), flat(mark)
    acted, other, gap, snapped, exported = map(flat, (acted, other, gap, snapped, exported))
    hi_rows = loc.shape[0]
    per = hi_rows // crosses
    gcount = exported.shape[0]
    bonds = acted.shape[0]
    lr = 2 * crosses * per
    shape = jax.ShapeDtypeStruct
    dma = pltpu.SemaphoreType.DMA
    vm = pltpu.VMEM
    plane = (2, 2, nx, nz)
    padded = (rows + 2 * ny, nz)
    arrays = (
        loc, gain, mark, exported, pos, temp.reshape(rows, nz), kappa.reshape(rows, nz), acted, other, gap, snapped
    )
    temp_new, force = pl.pallas_call(
        functools.partial(kernel, cuts, crosses),
        out_shape=(shape((rows, nz), f32), shape((3 * hi_rows, LANES), f32)),
        in_specs=[ANY] * 11,
        out_specs=(ANY, VMEM),
        scratch_shapes=[vm(a.shape, a.dtype) for a in arrays]
        + [
            vm((rows, nz), f32),
            vm((2 * crosses, 2 * per, LANES), f32),
            vm((crosses, 2 * per, LANES), f32),
            vm((2, 2, ny, nz), f32),
            vm(plane, f32),
            vm(plane, f32),
            vm((2, 3 * gcount, LANES), f32),
            vm((3 * gcount, LANES), f32),
            vm((lr, LANES), f32),
            vm((lr, LANES), f32),
            vm((lr, LANES), f32),
            vm((2 * LANES, lr * LANES), bf16),
            vm((LANES, bonds * LANES), bf16),
            vm((256, LANES), bf16),
            vm((rows, nz), f32),
            vm((rows, nz), f32),
            vm(padded, f32),
            vm(padded, f32),
            vm(padded, f32),
            vm(padded, f32),
            vm(plane, f32),
            vm((2, nx, nz), f32),
            vm((2 * nz, rows), bf16),
            vm((2 * crosses, per, LANES), f32),
            vm((crosses, per, LANES), f32),
            vm((crosses, per, LANES), f32),
            vm((crosses, per, LANES), f32),
            vm(plane, f32),
            vm((gcount, LANES), f32),
            vm((2, gcount, LANES), f32),
            vm((6, bonds, LANES), f32),
            vm((2, 3 * hi_rows, LANES), f32),
            dma((crosses,)),
            dma((crosses,)),
            dma((12,)),
            dma((12,)),
            dma((4,)),
            dma((4,)),
            dma((2,)),
            dma((2,)),
            dma((8,)),
            dma((8,)),
            dma((crosses,)),
            dma((crosses,)),
            dma((2,)),
            dma((2,)),
            dma((12,)),
        ],
        compiler_params=pltpu.CompilerParams(collective_id=0, has_side_effects=True),
        name="substeps",
    )(*arrays)
    temp_new, pos_new, vel_new = pl.pallas_call(
        update_kernel,
        out_shape=(shape((rows, nz), f32), shape(pos.shape, f32), shape(vel.shape, f32)),
        in_specs=[ANY] * 4,
        out_specs=(ANY,) * 3,
        scratch_shapes=[
            vm((4, rows // 4, nz), f32),
            vm(force.shape, f32),
            vm(pos.shape, f32),
            vm(vel.shape, f32),
            dma((2, 4)),
            dma((5,)),
        ],
        name="update",
    )(temp_new, force, pos, vel)
    return temp_new.reshape(nx, ny, nz), pos_new, vel_new


def solution(mesh):
    both = P(("cut", "cross"))
    return jax.shard_map(
        functools.partial(per_device, mesh.shape["cut"], mesh.shape["cross"]),
        mesh=mesh,
        in_specs=(P("cut", "cross", None),) * 2
        + (both,) * 3
        + (P(None, ("cut", "cross")),) * 2
        + (both,) * 5,
        out_specs=(P("cut", "cross", None), P(None, ("cut", "cross")), P(None, ("cut", "cross"))),
        check_vma=False,
    )
```

```python
import functools

import jax
import jax.numpy as jnp
from jax import lax
from jax.experimental import pallas as pl
from jax.experimental.pallas import tpu as pltpu
from jax.sharding import PartitionSpec as P

f32 = jnp.float32
bf16 = jnp.bfloat16
i32 = jnp.int32
MESH = pl.DeviceIdType.MESH
NT = (((1,), (1,)), ((), ()))
LANES = 128
VMEM = pl.BlockSpec(memory_space=pltpu.VMEM)
ANY = pl.BlockSpec(memory_space=pl.ANY)


def stack(tile, count):
    return jnp.concatenate([tile] * count, axis=0)


def rows16(row):
    return jnp.broadcast_to(row, (16, row.shape[1])).astype(bf16)


def hot(row, iota):
    r = stack(rows16(row), iota.shape[0] // 16)
    return jnp.where(iota == r, jnp.ones_like(iota), jnp.zeros_like(iota))


def spread(row, val, iota):
    r = stack(rows16(row), iota.shape[0] // 16)
    v = stack(rows16(val), iota.shape[0] // 16)
    return jnp.where(iota == r, v, jnp.zeros_like(iota))


def iota_rows(count):
    return lax.broadcasted_iota(i32, (count, LANES), 0).astype(f32).astype(bf16)


def high(v):
    return v.astype(bf16).astype(f32)


def conduct(t):
    return 0.5 + 1.0 / (1.0 + t * t)


def peers(cuts, crosses):
    c, s = lax.axis_index("cut"), lax.axis_index("cross")
    below, above = lax.rem(c + cuts - 1, cuts), lax.rem(c + 1, cuts)
    return c, s, below, above


def greet(cuts, crosses):
    c, s, below, above = peers(cuts, crosses)
    barrier = pltpu.get_barrier_semaphore()

    for device in ((below, s), (above, s)):
        pl.semaphore_signal(barrier, inc=1, device_id=device, device_id_type=MESH)

    def other(k, carry):
        j = lax.rem(s + k, crosses)
        pl.semaphore_signal(barrier, inc=1, device_id=(c, j), device_id_type=MESH)
        return carry

    lax.fori_loop(1, crosses, other, 0)


def await_all(crosses):
    pl.semaphore_wait(pltpu.get_barrier_semaphore(), crosses + 1)


def remote(src, dst, send, recv, device):
    return pltpu.make_async_remote_copy(
        src_ref=src, dst_ref=dst, send_sem=send, recv_sem=recv, device_id=device, device_id_type=MESH
    )


def lane_pick(row, index):
    return jnp.take_along_axis(row, index, axis=1, mode="promise_in_bounds")


def table_pick(rows, high_index, low_index, start):
    out = start
    for number, row in rows:
        wide = jnp.broadcast_to(row, low_index.shape)
        out = jnp.where(high_index == number, lane_pick(wide, low_index), out)
    return out


def kernel(
    cuts, crosses, *refs
):
    inputs, (temp_hbm_out, force_out) = refs[:11], refs[11:13]
    loc, gain, mark, exported, pos, temp, kappa, acted, other, gap, snapped = refs[13:24]
    (
    temp_out, lists, send_lists, hx, hy, ysend0, ghosts, gsend,
    row, zed, val, sp, ohl, big, d1, src, ta, tb, ca, cb, ysend, flux, tt, picked, far, ret, back, stage,
    gtemp_send, gtemp, pq, own,
    send_sem, recv_sem, hsend, hrecv, xs, xr, ys, yr, zs_sem, zr_sem, bs, br, gs, gr, local,
    ) = refs[24:]
    c, s, below, above = peers(cuts, crosses)
    left, right = lax.rem(s + crosses - 1, crosses), lax.rem(s + 1, crosses)
    loads = [pltpu.make_async_copy(a, b, local.at[n]) for n, (a, b) in enumerate(zip(inputs, refs[13:24]))]
    for load in loads[:3]:
        load.start()
    greet(cuts, crosses)
    for load in loads[3:]:
        load.start()
    rows = temp.shape[0]
    nx = hy.shape[2]
    ny = rows // nx
    cells = rows * LANES
    hi_rows = loc.shape[0]
    per = hi_rows // crosses
    gcount = exported.shape[0]
    bond_rows = acted.shape[0]

    for load in loads[:3]:
        load.wait()
    w = loc[...].astype(f32)
    power = mark[...].astype(f32) * gain[...] * 0.5
    for j in range(crosses):
        send_lists[j, 0:per, :] = w[j * per : (j + 1) * per]
        send_lists[j, per : 2 * per, :] = power[j * per : (j + 1) * per]
    await_all(crosses)

    chips_y = crosses // 4

    def pair(k):
        far_x = 1 - k // chips_y
        y = lax.rem(s // 4 + lax.rem(k, chips_y) + 1, chips_y)
        x = lax.rem(lax.rem(s // 2, 2) + far_x, 2)
        chip = 4 * y + 2 * x
        return chip + 1 - lax.rem(s, 2), chip + lax.rem(s, 2)

    def send_to(j):
        remote(send_lists.at[j], lists.at[s], send_sem.at[j], recv_sem.at[s], (c, j)).start()

    def send_same(k, carry):
        a, b = pair(k)
        send_to(a)
        send_to(b)
        return carry

    lax.fori_loop(0, crosses // 2 - 1, send_same, 0)
    send_to(pair(crosses // 2 - 1)[0])
    lists[pl.ds(s, 1)] = send_lists[pl.ds(s, 1)]
    for load in loads[3:]:
        load.wait()
    for a, ref in enumerate((temp, kappa)):
        ysend0[a, 0] = ref[pl.ds(0, nx, stride=ny), :]
        ysend0[a, 1] = ref[pl.ds(ny - 1, nx, stride=ny), :]
    early = []
    for a, ref in enumerate((temp, kappa)):
        early.append(remote(ysend0.at[a, 1], hy.at[a, 0], hsend.at[4 * a + 2], hrecv.at[4 * a + 2], (c, right)))
        early.append(remote(ysend0.at[a, 0], hy.at[a, 1], hsend.at[4 * a + 3], hrecv.at[4 * a + 3], (c, left)))
        early.append(remote(ref.at[pl.ds(rows - ny, ny)], hx.at[a, 0], hsend.at[4 * a], hrecv.at[4 * a], (above, s)))
        early.append(remote(ref.at[pl.ds(0, ny)], hx.at[a, 1], hsend.at[4 * a + 1], hrecv.at[4 * a + 1], (below, s)))
    for copy in early:
        copy.start()
    e8 = jnp.concatenate([exported[...]] * (8 // gcount), axis=0)
    eh, el = e8 // LANES, e8 % LANES
    zero8 = jnp.zeros((8, LANES), f32)

    def row_of(ref, ch, r):
        return ref[ch : ch + 1, pl.ds(pl.multiple_of(r * LANES, LANES), LANES)]

    def export_rows(r, acc):
        return tuple(table_pick([(r, row_of(pos, ch, r))], eh, el, acc[ch]) for ch in range(3))

    acc = lax.fori_loop(0, hi_rows, export_rows, (zero8,) * 3, unroll=8)
    for ch in range(3):
        gsend[ch * gcount : (ch + 1) * gcount, :] = acc[ch][:gcount]

    late = [
        remote(gsend, ghosts.at[0], hsend.at[8], hrecv.at[8], (above, s)),
        remote(gsend, ghosts.at[1], hsend.at[9], hrecv.at[9], (below, s)),
    ]
    for copy in late:
        copy.start()
    early += late

    group = 16

    def differences(k, carry):
        where = pl.ds(pl.multiple_of(k * group, group), group)
        qa, qb = acted[where, :], other[where, :]
        index = [(q[h : h + 8] // LANES, q[h : h + 8] % LANES) for q in (qa, qb) for h in range(0, group, 8)]

        def one(r, acc):
            out = []
            for ch in range(3):
                wide = jnp.broadcast_to(row_of(pos, ch, r), (8, LANES))
                for n, (h, l) in enumerate(index):
                    out.append(jnp.where(h == r, lane_pick(wide, l), acc[ch * len(index) + n]))
            return tuple(out)

        acc = lax.fori_loop(0, hi_rows, one, (zero8,) * (3 * len(index)), unroll=4)
        half = len(index) // 2
        for ch in range(3):
            for n in range(half):
                first, second = acc[ch * len(index) + n], acc[ch * len(index) + half + n]
                pq[ch, pl.ds(pl.multiple_of(k * group + 8 * n, 8), 8), :] = second - first
        return carry

    block = 16 * ny

    def begin(b, carry):
        where = pl.ds(pl.multiple_of(b * block, block), block)
        there = pl.ds(pl.multiple_of(b * block + ny, ny), block)
        t = temp[where, :]
        ta[there, :] = t
        ca[there, :] = kappa[where, :] * conduct(t)
        return carry

    lax.fori_loop(0, rows // block, begin, 0)
    big[...] = iota_rows(256)
    iota = big[...]
    small = iota[:LANES]

    def lows(k, carry):
        for u in range(4):
            r = k * 4 + u
            a = (acted[pl.ds(r, 1), :] % LANES).astype(f32)
            ohl[:, pl.ds(pl.multiple_of(r * LANES, LANES), LANES)] = hot(a, small)
        return carry

    lax.fori_loop(0, bond_rows // 4, lows, 0)
    lax.fori_loop(0, bond_rows // group // 2, differences, 0)

    def take_same(k, carry):
        j = lax.rem(s + k, crosses)
        remote(send_lists.at[j], lists.at[j], send_sem.at[j], recv_sem.at[j], (c, j)).wait()
        return carry

    lax.fori_loop(1, crosses, take_same, 0)
    relay = remote(
        lists.at[pl.ds(0, crosses)], lists.at[pl.ds(crosses, crosses)], hsend.at[10], hrecv.at[10], (above, s)
    )
    relay.start()

    count = row.shape[0]

    def build(k, carry):
        for u in range(8):
            r = k * 8 + u
            z = zed[pl.ds(r, 1), :]
            v = val[pl.ds(r, 1), :]
            hi = high(v)
            where = pl.ds(pl.multiple_of(r * LANES, LANES), LANES)
            sp[0:LANES, where] = spread(z, hi, small)
            sp[LANES : 2 * LANES, where] = spread(z, v - hi, small)
        return carry

    def decode(half):
        for b in range(half * crosses, (half + 1) * crosses):
            q = lists[b, 0:per, :].astype(i32)
            here = (q >= cells) == (half == 1)
            q = q & (cells - 1)
            row[b * per : (b + 1) * per, :] = jnp.where(here, q // LANES, -1).astype(f32)
            zed[b * per : (b + 1) * per, :] = (q % LANES).astype(f32)
            val[b * per : (b + 1) * per, :] = jnp.where(here, lists[b, per : 2 * per, :], 0.0)
        lax.fori_loop(half * count // 16, (half + 1) * count // 16, build, 0)
        where = slice(half * count // 2, (half + 1) * count // 2)
        r_all = row[where, :].astype(i32)
        y = r_all & (ny - 1)
        y = jnp.where(y == 0, 0, jnp.where(y == ny - 1, 1, y + 1))
        val[where, :] = jnp.where(r_all < 0, -1, y * nx + r_all // ny).astype(f32)

    tall, depth = 512, 16

    def deposit(m, begin, end, acc):
        first = m * float(tall)

        def inner(k, acc):
            pieces = []
            for h in range(depth):
                r = val[pl.ds(k * depth + h, 1), :] - first
                parts = []
                for g in range(tall // 256):
                    q = r - 256.0 * g
                    parts.append(hot(jnp.where((q >= 0) & (q < 256), q, -1.0), iota))
                pieces.append(jnp.concatenate(parts, axis=0))
            where = pl.ds(pl.multiple_of(k * (depth * LANES), depth * LANES), depth * LANES)
            return acc + lax.dot_general(
                jnp.concatenate(pieces, axis=1), sp[:, where], NT, preferred_element_type=f32
            )

        return lax.fori_loop(begin, end, inner, acc)

    planes = tall // nx
    nothing = jnp.zeros((tall, 2 * LANES), f32)
    steps = count // depth
    decode(0)
    got = deposit(0.0, 0, steps // 2, nothing)
    relay.wait()
    decode(1)
    got = deposit(0.0, steps // 2, steps, got)
    got = got[:, :LANES] + got[:, LANES:]
    for n, y in enumerate((0, ny - 1) + tuple(range(1, planes - 1))):
        src[pl.ds(y, nx, stride=ny), :] = got[n * nx : (n + 1) * nx]

    for copy in early:
        copy.wait()

    final = crosses - 1
    low_edge, high_edge = s == 0, s == final
    sub = lax.broadcasted_iota(i32, (ny, LANES), 0)
    lane = lax.broadcasted_iota(i32, (ny, LANES), 1)

    def edge(cref, tref):
        cref[0:ny, :] = hx[1, 0] * conduct(tref[0:ny, :])
        cref[rows + ny : rows + 2 * ny, :] = hx[1, 1] * conduct(tref[rows + ny : rows + 2 * ny, :])

    def rim(planes, tref, cref, start=0, size=nx):
        part = pl.ds(start, size)
        for n, (off, at) in enumerate(((low_edge, ny), (high_edge, 2 * ny - 1))):
            t = jnp.where(off, 0.0, planes[n, part, :])
            cc = jnp.where(off, 0.0, hy[1, n, part, :]) * conduct(t)
            here = pl.ds(start * ny + at, size, stride=ny)
            t0 = tref[here, :]
            c0 = cref[here, :]
            flux[n, part, :] = (cc + c0) * ((t0 - t) if n == 0 else (t - t0))

    many = 32
    pieces = nx // many

    def step(tin, cin, emit, done=None):
        def piece(k, carry):
            first = k * (many * ny)
            at0, at1 = pl.ds(pl.multiple_of(first, ny), ny), pl.ds(pl.multiple_of(first + ny, ny), ny)
            before = (cin[at0, :] + cin[at1, :]) * (tin[at1, :] - tin[at0, :])
            for u in range(many):
                x = k * many + u
                here = pl.ds(pl.multiple_of(x * ny + ny, ny), ny)
                ahead = pl.ds(pl.multiple_of(x * ny + 2 * ny, ny), ny)
                t0, c0 = tin[here, :], cin[here, :]
                t1, c1 = tin[ahead, :], cin[ahead, :]
                fx = (c0 + c1) * (t1 - t0)
                at = pl.ds(x, 1)
                north, south = pl.ds(x * ny + ny + 1, ny), pl.ds(x * ny + ny - 1, ny)
                fy = jnp.where(sub == ny - 1, flux[1, at, :], (c0 + cin[north, :]) * (tin[north, :] - t0))
                fy0 = jnp.where(sub == 0, flux[0, at, :], (c0 + cin[south, :]) * (t0 - tin[south, :]))
                ct = c0 * t0
                tz, cz = pltpu.roll(t0, LANES - 1, 1), pltpu.roll(c0, LANES - 1, 1)
                tw, cw = pltpu.roll(t0, 1, 1), pltpu.roll(c0, 1, 1)
                fz = jnp.where(lane == LANES - 1, -ct, (c0 + cz) * (tz - t0))
                fz0 = jnp.where(lane == 0, ct, (c0 + cw) * (t0 - tw))
                emit(x, t0 + 0.5 * (((fx - before) + (fy - fy0)) + (fz - fz0)))
                before = fx
            if done is not None:
                done(k)
            return carry

        return piece

    def inside(piece):
        lax.fori_loop(1, pieces - 1, piece, 0)

    def outside(piece):
        lax.fori_loop(0, 2, lambda n, carry: piece(n * (pieces - 1), carry), 0)

    def send_x(k, tref):
        copies = [
            remote(tref.at[pl.ds(rows, ny)], tref.at[pl.ds(0, ny)], xs.at[2 * k], xr.at[2 * k], (above, s)),
            remote(
                tref.at[pl.ds(ny, ny)], tref.at[pl.ds(rows + ny, ny)], xs.at[2 * k + 1], xr.at[2 * k + 1], (below, s)
            ),
        ]
        for copy in copies:
            copy.start()
        return copies

    def send_y():
        copies = [
            remote(ysend.at[0, 1], stage.at[0, 0], ys.at[0], yr.at[0], (c, right)),
            remote(ysend.at[0, 0], stage.at[0, 1], ys.at[1], yr.at[1], (c, left)),
        ]
        for copy in copies:
            copy.start()
        return copies

    ta[0:ny, :] = hx[0, 0]
    ta[rows + ny : rows + 2 * ny, :] = hx[0, 1]
    edge(ca, ta)
    rim(hy.at[0], ta, ca)

    def emit_first(x, t):
        d1[pl.ds(pl.multiple_of(x * ny, ny), ny), :] = t

    lax.fori_loop(0, pieces, step(ta, ca, emit_first), 0)
    for n, y in enumerate((0, ny - 1)):
        ysend[0, n] = d1[pl.ds(y, nx, stride=ny), :] + src[pl.ds(y, nx, stride=ny), :]
    first = send_y()

    def others(m, carry):
        got = deposit(m.astype(f32), 0, steps, nothing)
        got = got[:, :LANES] + got[:, LANES:]
        for n in range(planes):
            src[pl.ds(m * planes + (n - 1), nx, stride=ny), :] = got[n * nx : (n + 1) * nx]
        return carry

    lax.fori_loop(1, rows // tall, others, 0)

    def finish(b, carry):
        where = pl.ds(pl.multiple_of(b * block, block), block)
        there = pl.ds(pl.multiple_of(b * block + ny, ny), block)
        t = d1[where, :] + src[where, :]
        tb[there, :] = t
        cb[there, :] = kappa[where, :] * conduct(t)
        return carry

    lax.fori_loop(0, rows // block, finish, 0)
    sides = send_x(0, tb)

    lax.fori_loop(bond_rows // group // 2, bond_rows // group - 1, differences, 0)
    iota32 = iota[:hi_rows]

    turn = 32

    def scatter(values):
        def body(k, acc):
            lhs = []
            for u in range(turn):
                r = k * turn + u
                h = (acted[pl.ds(r, 1), :] // LANES).astype(f32)
                tops, bottoms = [], []
                for v in values(r):
                    top = high(v)
                    tops.append(spread(h, top, iota32))
                    bottoms.append(spread(h, v - top, iota32))
                lhs.append(jnp.concatenate(tops + bottoms, axis=0))
            where = pl.ds(pl.multiple_of(k * (turn * LANES), turn * LANES), turn * LANES)
            return acc + lax.dot_general(
                jnp.concatenate(lhs, axis=1), ohl[:, where], NT, preferred_element_type=f32
            )

        n = 3 * hi_rows
        acc = lax.fori_loop(0, bond_rows // turn, body, jnp.zeros((2 * n, LANES), f32))
        return acc[:n] + acc[n:]

    def rows_of(lo):
        return lambda r: [pq[lo + ch, pl.ds(r, 1), :] for ch in range(3)]

    def emit_second(x, t):
        where = pl.ds(pl.multiple_of(x * ny, ny), ny)
        here = pl.ds(pl.multiple_of(x * ny + ny, ny), ny)
        t = t + src[where, :]
        ta[here, :] = t
        ca[here, :] = kappa[where, :] * conduct(t)

    width = nx // pieces

    def strip(k):
        at = pl.ds(pl.multiple_of(k * width, width), width)
        return [
            remote(ysend.at[1, 1, at], stage.at[1, 0, at], zs_sem.at[k], zr_sem.at[k], (c, right)),
            remote(ysend.at[1, 0, at], stage.at[1, 1, at], zs_sem.at[pieces + k], zr_sem.at[pieces + k], (c, left)),
        ]

    def strip_done(k):
        at = pl.ds(pl.multiple_of(k * width, width), width)
        for n, y in enumerate((ny, 2 * ny - 1)):
            ysend[1, n, at, :] = ta[pl.ds(k * (width * ny) + y, width, stride=ny), :]
        for copy in strip(k):
            copy.start()

    for copy in first:
        copy.wait()
    rim(stage.at[0], tb, cb)
    second_step = step(tb, cb, emit_second, strip_done)
    inside(second_step)
    for copy in sides:
        copy.wait()
    edge(cb, tb)
    outside(second_step)
    second = send_x(1, ta)
    lax.fori_loop(bond_rows // group - 1, bond_rows // group, differences, 0)
    extra_rows = [(hi_rows + side * gcount + g, side, g) for side in range(2) for g in range(gcount)]
    for k in range(0, bond_rows, 8):
        q = other[k : k + 8, :]
        h, l = q // LANES, q % LANES
        for ch in range(3):
            d = pq[ch, k : k + 8, :]
            g = table_pick([(n, ghosts[side, ch * gcount + i : ch * gcount + i + 1, :]) for n, side, i in extra_rows], h, l, zero8)
            pq[ch, k : k + 8, :] = d + g
    d = [pq[ch] for ch in range(3)]
    dist = jnp.sqrt(d[0] * d[0] + d[1] * d[1] + d[2] * d[2])
    g = gap[...]
    base = (1.0 - snapped[...].astype(f32)) / jnp.maximum(dist, 0.3)
    p = base * (dist - g)
    q = base * (-0.1 * g)
    for ch in range(3):
        pq[ch] = p * d[ch]
        pq[3 + ch] = q * d[ch]

    def strip_taken(k, carry):
        for copy in strip(k):
            copy.wait()
        rim(stage.at[1], ta, ca, k * width, width)
        return carry

    def emit_third(x, t):
        where = pl.ds(pl.multiple_of(x * ny, ny), ny)
        temp_out[where, :] = t + src[where, :]

    third_step = step(ta, ca, emit_third)
    lax.fori_loop(1, pieces - 1, strip_taken, 0)
    inside(third_step)
    for copy in second:
        copy.wait()
    edge(ca, ta)
    lax.fori_loop(0, 2, lambda n, carry: strip_taken(n * (pieces - 1), carry), 0)
    outside(third_step)
    store = pltpu.make_async_copy(temp_out, temp_hbm_out, local.at[11])
    store.start()

    for k in range(rows // LANES):
        b = temp_out[k * LANES : (k + 1) * LANES, :].T
        hi = b.astype(bf16)
        tt[0:LANES, k * LANES : (k + 1) * LANES] = hi
        tt[LANES : 2 * LANES, k * LANES : (k + 1) * LANES] = (b - hi.astype(f32)).astype(bf16)
    zs = lax.broadcasted_iota(i32, (LANES, LANES), 0).astype(f32)

    def look(slots):
        cols = []
        for n in slots:
            for h in range(per):
                r = row[pl.ds(n * per + h, 1), :]
                parts = []
                for k in range(rows // 256):
                    q = r - 256.0 * k
                    parts.append(hot(jnp.where((q >= 0) & (q < 256), q, -1.0), iota))
                cols.append(jnp.concatenate(parts, axis=0))
        got = jnp.dot(tt[...], jnp.concatenate(cols, axis=1), preferred_element_type=f32)
        got = got[:LANES] + got[LANES:]
        for i, n in enumerate(slots):
            for h in range(per):
                u = i * per + h
                z = zed[pl.ds(n * per + h, 1), :]
                v = jnp.where(zs == z, got[:, u * LANES : (u + 1) * LANES], 0.0)
                picked[n, h : h + 1, :] = jnp.sum(v, axis=0, keepdims=True)

    def look_below(k, carry):
        look((crosses + 2 * k, crosses + 2 * k + 1))
        return carry

    lax.fori_loop(0, crosses // 2, look_below, 0)
    hand = remote(picked.at[pl.ds(crosses, crosses)], far, hsend.at[11], hrecv.at[11], (below, s))
    hand.start()

    def merge(j):
        m = row[pl.ds(j * per, per), :] < 0
        return jnp.where(m, far[pl.ds(j, 1)].reshape(per, LANES), picked[pl.ds(j, 1)].reshape(per, LANES))

    def back_to(j):
        ret[pl.ds(j, 1)] = merge(j).reshape(1, per, LANES)
        remote(ret.at[j], back.at[s], bs.at[j], br.at[s], (c, j)).start()

    held = 3

    def look_first(k, carry):
        look(pair(k))
        return carry

    lax.fori_loop(0, held, look_first, 0)
    hand.wait()

    def send_held(k, carry):
        a, b = pair(k)
        back_to(a)
        back_to(b)
        return carry

    lax.fori_loop(0, held, send_held, 0)

    def look_then(k, carry):
        a, b = pair(k)
        look((a, b))
        back_to(a)
        back_to(b)
        return carry

    lax.fori_loop(held, crosses // 2 - 1, look_then, 0)
    a, b = pair(crosses // 2 - 1)
    look((a, b))
    back_to(a)
    back[pl.ds(s, 1)] = merge(s).reshape(1, per, LANES)
    own[0] = scatter(rows_of(0))

    def back_same(k, carry):
        j = lax.rem(s + k, crosses)
        remote(ret.at[j], back.at[j], bs.at[j], br.at[j], (c, j)).wait()
        return carry

    lax.fori_loop(1, crosses, back_same, 0)
    warm = jnp.concatenate([back[j] for j in range(crosses)], axis=0)
    table = [(r, warm[r : r + 1]) for r in range(hi_rows)]
    gtemp_send[...] = table_pick(table, eh, el, zero8)[:gcount]
    copies = [
        remote(gtemp_send, gtemp.at[0], gs.at[0], gr.at[0], (above, s)),
        remote(gtemp_send, gtemp.at[1], gs.at[1], gr.at[1], (below, s)),
    ]
    for copy in copies:
        copy.start()
    partner = []
    for k in range(0, bond_rows, 8):
        q = other[k : k + 8, :]
        partner.append(table_pick(table, q // LANES, q % LANES, zero8))
    own[1] = scatter(rows_of(3))
    for copy in copies:
        copy.wait()
    for n, k in enumerate(range(0, bond_rows, 8)):
        q = other[k : k + 8, :]
        t = table_pick(
            [(m, gtemp[side, i : i + 1, :]) for m, side, i in extra_rows], q // LANES, q % LANES, partner[n]
        )
        for ch in range(3):
            pq[3 + ch, k : k + 8, :] = pq[3 + ch, k : k + 8, :] * t
    force_out[...] = own[0] + scatter(rows_of(3)) + jnp.concatenate([warm] * 3, axis=0) * own[1]
    store.wait()


def update_kernel(
    temp, force_hbm, pos_hbm, vel_hbm, temp_out, pos_out, vel_out, held, force, pos, vel, sems, small
):
    parts = held.shape[0]
    rows = held.shape[1]
    first = [
        pltpu.make_async_copy(a, b, small.at[n])
        for n, (a, b) in enumerate(((force_hbm, force), (pos_hbm, pos), (vel_hbm, vel)))
    ]
    where = [pl.ds(n * rows, rows) for n in range(parts)]
    loads = [pltpu.make_async_copy(temp.at[w], held.at[n], sems.at[0, n]) for n, w in enumerate(where)]
    stores = [pltpu.make_async_copy(held.at[n], temp_out.at[w], sems.at[1, n]) for n, w in enumerate(where)]
    for load in first + loads:
        load.start()
    for load in first:
        load.wait()
    hi_rows = pos.shape[1] // LANES
    for r in range(hi_rows):
        at = slice(r * LANES, (r + 1) * LANES)
        v = vel[:, at] + 0.5 * force[pl.ds(r, 3, stride=hi_rows), :]
        vel[:, at] = v
        pos[:, at] = pos[:, at] + 0.5 * v
    last = [pltpu.make_async_copy(vel, vel_out, small.at[3]), pltpu.make_async_copy(pos, pos_out, small.at[4])]
    for store in last:
        store.start()
    for load, store in zip(loads, stores):
        load.wait()
        store.start()
    for store in stores + last:
        store.wait()


def per_device(
    cuts, crosses, temp, kappa, locator, gain, mark, pos, vel, acted, other, gap, snapped, exported
):
    nx, ny, nz = temp.shape
    rows = nx * ny
    flat = lambda a: a.reshape(-1, LANES)
    loc, gain, mark = flat(locator), flat(gain), flat(mark)
    acted, other, gap, snapped, exported = map(flat, (acted, other, gap, snapped, exported))
    hi_rows = loc.shape[0]
    per = hi_rows // crosses
    gcount = exported.shape[0]
    bonds = acted.shape[0]
    lr = 2 * crosses * per
    shape = jax.ShapeDtypeStruct
    dma = pltpu.SemaphoreType.DMA
    vm = pltpu.VMEM
    plane = (2, 2, nx, nz)
    padded = (rows + 2 * ny, nz)
    arrays = (
        loc, gain, mark, exported, pos, temp.reshape(rows, nz), kappa.reshape(rows, nz), acted, other, gap, snapped
    )
    temp_new, force = pl.pallas_call(
        functools.partial(kernel, cuts, crosses),
        out_shape=(shape((rows, nz), f32), shape((3 * hi_rows, LANES), f32)),
        in_specs=[ANY] * 11,
        out_specs=(ANY, VMEM),
        scratch_shapes=[vm(a.shape, a.dtype) for a in arrays]
        + [
            vm((rows, nz), f32),
            vm((2 * crosses, 2 * per, LANES), f32),
            vm((crosses, 2 * per, LANES), f32),
            vm((2, 2, ny, nz), f32),
            vm(plane, f32),
            vm(plane, f32),
            vm((2, 3 * gcount, LANES), f32),
            vm((3 * gcount, LANES), f32),
            vm((lr, LANES), f32),
            vm((lr, LANES), f32),
            vm((lr, LANES), f32),
            vm((2 * LANES, lr * LANES), bf16),
            vm((LANES, bonds * LANES), bf16),
            vm((256, LANES), bf16),
            vm((rows, nz), f32),
            vm((rows, nz), f32),
            vm(padded, f32),
            vm(padded, f32),
            vm(padded, f32),
            vm(padded, f32),
            vm(plane, f32),
            vm((2, nx, nz), f32),
            vm((2 * nz, rows), bf16),
            vm((2 * crosses, per, LANES), f32),
            vm((crosses, per, LANES), f32),
            vm((crosses, per, LANES), f32),
            vm((crosses, per, LANES), f32),
            vm(plane, f32),
            vm((gcount, LANES), f32),
            vm((2, gcount, LANES), f32),
            vm((6, bonds, LANES), f32),
            vm((2, 3 * hi_rows, LANES), f32),
            dma((crosses,)),
            dma((crosses,)),
            dma((12,)),
            dma((12,)),
            dma((4,)),
            dma((4,)),
            dma((2,)),
            dma((2,)),
            dma((8,)),
            dma((8,)),
            dma((crosses,)),
            dma((crosses,)),
            dma((2,)),
            dma((2,)),
            dma((12,)),
        ],
        compiler_params=pltpu.CompilerParams(collective_id=0, has_side_effects=True),
        name="substeps",
    )(*arrays)
    temp_new, pos_new, vel_new = pl.pallas_call(
        update_kernel,
        out_shape=(shape((rows, nz), f32), shape(pos.shape, f32), shape(vel.shape, f32)),
        in_specs=[ANY] * 4,
        out_specs=(ANY,) * 3,
        scratch_shapes=[
            vm((4, rows // 4, nz), f32),
            vm(force.shape, f32),
            vm(pos.shape, f32),
            vm(vel.shape, f32),
            dma((2, 4)),
            dma((5,)),
        ],
        name="update",
    )(temp_new, force, pos, vel)
    return temp_new.reshape(nx, ny, nz), pos_new, vel_new


def solution(mesh):
    both = P(("cut", "cross"))
    return jax.shard_map(
        functools.partial(per_device, mesh.shape["cut"], mesh.shape["cross"]),
        mesh=mesh,
        in_specs=(P("cut", "cross", None),) * 2
        + (both,) * 3
        + (P(None, ("cut", "cross")),) * 2
        + (both,) * 5,
        out_specs=(P("cut", "cross", None), P(None, ("cut", "cross")), P(None, ("cut", "cross"))),
        check_vma=False,
    )
```
